32 devices in a mesh: wide: 16 (over z, y, core), narrow: 2 (over x).
Axes of the slice: x: 2, y: 2, z: 4, core: 2. Of those that a mesh axis runs over, the one named last changes fastest.
Arguments:
- tokens: bfloat16 [128, 8, 64, 768], P('wide', None, 'narrow'), may hold values from -6 to 6
- masked: int32 [128, 8, 64], P('wide', None, 'narrow'), may hold values 0 or 1
- resolution: int32 [128], P('wide'), may hold values from 0 to 1, as said below
- mask_embed: bfloat16 [768], replicated, may hold values from -5 to 5
- gains: bfloat16 [768, 2], replicated, may hold values from 0.5 to 1.5
- biases: bfloat16 [768, 6], replicated, may hold values from -1 to 1
- w_qkv: bfloat16 [768, 2304], replicated, may hold values from -0.21875 to 0.21875
- w_proj: bfloat16 [768, 768], replicated, may hold values from -1.75 to 1.75
- w_fc1: bfloat16 [768, 3072], replicated, may hold values from -0.21875 to 0.21875
- fc1_bias: bfloat16 [3072], replicated, may hold values from -1 to 1
- w_fc2: bfloat16 [3072, 768], replicated, may hold values from -0.109375 to 0.109375
- cotangent: bfloat16 [128, 8, 64, 768], P('wide', None, 'narrow'), may hold values from -6 to 6
Outputs:
- output: bfloat16 [128, 8, 64, 768], P('wide', None, 'narrow')
- grad_tokens: bfloat16 [128, 8, 64, 768], P('wide', None, 'narrow')
- grad_mask_embed: float32 [768], P(('wide', 'narrow'))
- grad_gains: float32 [768, 2], P(('wide', 'narrow'))
- grad_biases: float32 [768, 6], P(('wide', 'narrow'))
- grad_qkv: float32 [768, 2304], P(('wide', 'narrow'))
- grad_proj: float32 [768, 768], P(('wide', 'narrow'))
- grad_fc1: float32 [768, 3072], P(('wide', 'narrow'))
- grad_fc1_bias: float32 [3072], P(('wide', 'narrow'))
- grad_fc2: float32 [3072, 768], P(('wide', 'narrow'))
The draws below stay inside these ranges and needn't reach their ends.
Inputs may be any that keep to these rules, and one draw needn't show every extreme that they name: `resolution`: 1 marks a clip of 128 mel bins, 0 a clip of 64 mel bins whose frequency rows 4 and above are empty; clips of 128 mel bins come first and both kinds occur.
All inputs are finite; a program needn't handle non-finite values. No bound on the sum of `masked` on one device may be relied on, other than what follows from the above.
Results may differ from the reference program's by a relative error of at most 0.013.
Values may be sent and summed in bfloat16 or wider, within the bound.
No kernel may reach another device: no remote copies, remote signals or barrier semaphores. Data moves between devices by JAX's collectives and lax.ppermute only.
A program may use at most 448 MiB of HBM per device.

```python
import math
import jax
import jax.numpy as jnp
from jax import lax

D = 768
HEADS = 12
FF = 3072
FREQ = 8
TIME = 64
CLIPS = 128


def draw_resolution(key, part):
    highres = jax.random.randint(key, (), 1, CLIPS)
    return (jnp.arange(CLIPS) < highres).astype(jnp.int32)


def with_ends(entries, own_key, smallest, largest):
    index_at = [jax.random.randint(jax.random.fold_in(own_key, axis), (), 0, length) for axis, length in enumerate(entries.shape)]
    widest = entries.shape.index(max(entries.shape))
    beside = index_at[:widest] + [(index_at[widest] + 1) % entries.shape[widest]] + index_at[widest + 1:]
    return entries.at[tuple(index_at)].set(smallest).at[tuple(beside)].set(largest)


def block_levels(key, dims, cuts, least, largest):
    def one(axis_at, shards_of):
        heights = jax.random.uniform(jax.random.fold_in(jax.random.fold_in(key, 6), axis_at), (shards_of,), jnp.float32, least / len(cuts), largest / len(cuts))
        return jnp.repeat(jnp.exp(heights), dims[axis_at] // shards_of).reshape((-1,) + (1,) * (len(dims) - axis_at - 1))

    gain = one(*cuts[0])
    for cut in cuts[1:]:
        gain = gain * one(*cut)
    return gain


def noise(own_key, shape, scale, most, shards=(), kind=jnp.bfloat16):
    values = jax.random.normal(own_key, shape, jnp.float32) * scale
    if len(shards) > 0:
        values = block_levels(own_key, shape, shards, -0.22, 0.18) * values
    return jnp.clip(values, min=-most, max=most).astype(kind)


def setup_inputs(seed: int = 0) -> dict:
    key_of = jax.random.split(jax.random.key(seed), 13)
    return {
        "tokens": noise(key_of[0], (CLIPS, FREQ, TIME, D), 1.0, 6.0, ((0, 16), (2, 2))),
        "masked": with_ends((jax.random.randint(key_of[1], (CLIPS, FREQ, TIME), 0, 8) < 3).astype(jnp.int32), jax.random.fold_in(key_of[1], 1), 0, 1),
        "resolution": draw_resolution(jax.random.fold_in(key_of[12], 71), 0),
        "mask_embed": noise(key_of[3], (D,), 1.0, 5.0),
        "gains": jnp.clip(1.0 + 0.1 * jax.random.normal(key_of[4], (D, 2), jnp.float32), 0.5, 1.5).astype(jnp.bfloat16),
        "biases": noise(key_of[5], (D, 6), 0.2, 1.0),
        "w_qkv": noise(key_of[6], (D, 3 * D), D ** -0.5, 0.21875),
        "w_proj": noise(key_of[7], (D, D), (D // 64) ** -0.5, 1.75),
        "w_fc1": noise(key_of[8], (D, FF), D ** -0.5, 0.21875),
        "fc1_bias": noise(key_of[9], (FF,), 0.2, 1.0),
        "w_fc2": noise(key_of[10], (FF, D), FF ** -0.5, 0.109375),
        "cotangent": noise(key_of[11], (CLIPS, FREQ, TIME, D), 1.0, 6.0, ((0, 16), (2, 2))),
    }


@jax.custom_vjp
def low(v):
    return lax.optimization_barrier(v.astype(jnp.bfloat16)).astype(jnp.float32)

@jax.custom_vjp
def low_back(v):
    return v

def low_keep(v):
    return (low(v), None)

def low_pass(kept, grad):
    return (grad,)

def back_keep(v):
    return (v, None)

def back_low(kept, grad):
    return (low(grad),)
low.defvjp(low_keep, low_pass)
low_back.defvjp(back_keep, back_low)
highest = lax.Precision.HIGHEST
epsilon = 1e-06

def norm_rows(matrix, gain_vec, shift_vec):
    row_mean = lax.optimization_barrier(jnp.mean(matrix, axis=-1, keepdims=True))
    centred = matrix - row_mean
    spread = lax.optimization_barrier(jnp.mean(centred * centred, axis=-1, keepdims=True))
    return centred * lax.rsqrt(spread + epsilon) * gain_vec + shift_vec

def both_ways(value):
    return low_back(low(value))

def forward(params, tokens, masked, resolution):
    mask_embed, gains, biases, w_qkv, w_proj, w_fc1, fc1_bias, w_fc2 = params
    group = math.gcd(CLIPS, 8)
    head_width = D // HEADS
    score_scale = head_width ** (-0.5)

    def one_group(pieces):
        tok_group, mask_group, res_group = pieces
        count = tok_group.shape[0]
        valid = (res_group[:, None] == 1) | (jnp.arange(FREQ)[None, :] < FREQ // 2)
        key_valid = jnp.broadcast_to(valid[:, :, None], (count, FREQ, TIME)).reshape(count, FREQ * TIME)
        entered = jnp.where(mask_group[..., None] == 1, mask_embed, tok_group)
        normed_one = low(norm_rows(entered, gains[:, 0], biases[:, 4]))
        projected = jnp.einsum('gftd,de->gfte', normed_one, w_qkv, precision=highest)
        queries = both_ways(projected[..., :D] + biases[:, 0])
        key_rows = both_ways(projected[..., D:2 * D])
        value_rows = both_ways(projected[..., 2 * D:] + biases[:, 1])
        head_shape = (count, FREQ * TIME, HEADS, head_width)
        head_q = queries.reshape(head_shape)
        head_k = key_rows.reshape(head_shape)
        head_v = value_rows.reshape(head_shape)
        scores = low_back(jnp.einsum('gqhe,gkhe->ghqk', head_q, head_k, precision=highest) * score_scale)
        scores = jnp.where(key_valid[:, None, None, :], scores, -1e+30)
        top = lax.optimization_barrier(jnp.max(scores, axis=-1, keepdims=True))
        shifted = jnp.exp(scores - top)
        probs = low(shifted / lax.optimization_barrier(jnp.sum(shifted, axis=-1, keepdims=True)))
        attended = both_ways(jnp.einsum('ghqk,gkhe->gqhe', probs, head_v, precision=highest)).reshape(count, FREQ, TIME, D)
        branch = low_back(jnp.einsum('gftd,de->gfte', attended, w_proj, precision=highest) + biases[:, 2])
        middle = entered + branch
        normed_two = low(norm_rows(middle, gains[:, 1], biases[:, 5]))
        hidden_pre = low_back(jnp.einsum('gftd,de->gfte', normed_two, w_fc1, precision=highest) + fc1_bias)
        activated = low(jax.nn.gelu(hidden_pre, approximate=False))
        mlp_out = low_back(jnp.einsum('gfte,ed->gftd', activated, w_fc2, precision=highest) + biases[:, 3])
        return jnp.where(valid[:, :, None, None], middle + mlp_out, 0.0)
    shaped = (tokens.reshape(CLIPS // group, group, FREQ, TIME, D), masked.reshape(CLIPS // group, group, FREQ, TIME), resolution.reshape(CLIPS // group, group))
    result = lax.map(jax.checkpoint(one_group), shaped)
    return result.reshape(CLIPS, FREQ, TIME, D)

def reference(tokens, masked, resolution, mask_embed, gains, biases, w_qkv, w_proj, w_fc1, fc1_bias, w_fc2, cotangent):
    params = (mask_embed.astype(jnp.float32), gains.astype(jnp.float32), biases.astype(jnp.float32), w_qkv.astype(jnp.float32), w_proj.astype(jnp.float32), w_fc1.astype(jnp.float32), fc1_bias.astype(jnp.float32), w_fc2.astype(jnp.float32))

    def apply(param_set, token_values):
        return forward(param_set, token_values, masked, resolution)
    output, pullback = jax.vjp(apply, params, tokens.astype(jnp.float32))
    grad_params, grad_tokens = pullback(cotangent.astype(jnp.float32))
    return (output.astype(jnp.bfloat16), grad_tokens.astype(jnp.bfloat16), grad_params[0], grad_params[1], grad_params[2], grad_params[3], grad_params[4], grad_params[5], grad_params[6], grad_params[7])
```

```python
import functools

import jax
import jax.numpy as jnp
from jax import lax
from jax.experimental import pallas as pl
from jax.experimental.pallas import tpu as pltpu
from jax.sharding import PartitionSpec as P

HEADS = 12
EPS = 1e-06
LOG2E = 1.4426950408889634
F32 = jnp.float32
BF16 = jnp.bfloat16
MIB = 1 << 20


def dot_nn(a, b):
    return jnp.dot(a, b, preferred_element_type=F32)


def dot_nt(a, b):
    return lax.dot_general(a, b, (((1,), (1,)), ((), ())), preferred_element_type=F32)


def dot_tn(a, b):
    return lax.dot_general(a, b, (((0,), (0,)), ((), ())), preferred_element_type=F32)


def norm_stats(x):
    centred = x - jnp.mean(x, axis=-1, keepdims=True)
    rstd = lax.rsqrt(jnp.mean(centred * centred, axis=-1, keepdims=True) + EPS)
    return centred * rstd, rstd


def norm_back(grad, x, gain):
    xhat, rstd = norm_stats(x)
    scaled = grad * gain
    inner = jnp.mean(scaled * xhat, axis=-1, keepdims=True)
    outer = jnp.mean(scaled, axis=-1, keepdims=True)
    dx = rstd * (scaled - outer - xhat * inner)
    return dx, jnp.sum(grad * xhat, axis=0, keepdims=True), jnp.sum(grad, axis=0, keepdims=True)


def row_valid(rows, piece_rows, full):
    at = lax.broadcasted_iota(jnp.int32, (rows, 1), 0) % piece_rows
    return (at < piece_rows // 2) | full


def attn_fwd_kernel(c, pieces, info, *refs):
    xs = refs[:pieces]
    vec, wqkv, wproj = refs[pieces : pieces + 3]
    n1_o, qkv_o, att_o, lse_o, mid_o, n2_o = refs[-7:-1]
    lse_s = refs[-1]
    rp, d = xs[0].shape
    rows = rp * pieces
    hw = d // HEADS
    full = info[1 + c] == 1
    for i in range(pieces):
        xhat, _ = norm_stats(xs[i][...].astype(F32))
        n1_o[i * rp : (i + 1) * rp, :] = (xhat * vec[0:1, :] + vec[6:7, :]).astype(BF16)
    n1 = n1_o[...]
    qkv_o[:, 0:d] = (dot_nn(n1, wqkv[:, 0:d]) + vec[2:3, :]).astype(BF16)
    qkv_o[:, d : 2 * d] = dot_nn(n1, wqkv[:, d : 2 * d]).astype(BF16)
    qkv_o[:, 2 * d : 3 * d] = (dot_nn(n1, wqkv[:, 2 * d : 3 * d]) + vec[3:4, :]).astype(BF16)
    scale2 = hw**-0.5 * LOG2E
    bias = jnp.where(row_valid(rows, rp, full), 0.0, -1e30).astype(BF16)
    lane = lax.broadcasted_iota(jnp.int32, (1, 2 * hw), 1)
    head_lane = lax.broadcasted_iota(jnp.int32, (1, 128), 1)
    lse_s[...] = jnp.zeros_like(lse_s)

    def pair(p, carry):
        at = pl.multiple_of(p * 2 * hw, 2 * hw)
        q = qkv_o[:, pl.ds(at, 2 * hw)]
        k = qkv_o[:, pl.ds(pl.multiple_of(d + at, 2 * hw), 2 * hw)]
        v = qkv_o[:, pl.ds(pl.multiple_of(2 * d + at, 2 * hw), 2 * hw)]
        outs = []
        tops = []
        for e in range(2):
            mine = (lane < hw) if e == 0 else (lane >= hw)
            spare = lane == hw * (1 - e)
            one = jnp.where(spare, 1.0, 0.0).astype(BF16)
            qm = jnp.where(mine, q, one)
            km = jnp.where(spare, bias, k)
            s = dot_nt(qm, km)
            top = jnp.max(s, axis=-1, keepdims=True)
            pr = jnp.exp2((s - top) * scale2).astype(BF16)
            vm = jnp.where(mine, v, jnp.ones_like(v))
            outs.append(dot_nn(pr, vm))
            tops.append(top)
        low = lane < hw
        total = pltpu.roll(jnp.where(low, outs[1], outs[0]), hw, 1)
        att_o[:, pl.ds(at, 2 * hw)] = (jnp.where(low, outs[0], outs[1]) / total).astype(BF16)
        log_total = jnp.log2(total) + scale2 * jnp.where(low, tops[0], tops[1])
        first = jnp.broadcast_to(log_total[:, 0:1], (rows, 128))
        second = jnp.broadcast_to(log_total[:, hw : hw + 1], (rows, 128))
        lse_s[...] = jnp.where(
            head_lane == 2 * p, first, jnp.where(head_lane == 2 * p + 1, second, lse_s[...])
        )
        return carry

    lax.fori_loop(0, HEADS // 2, pair, 0)
    lse_o[...] = jnp.transpose(lse_s[...])[0:16, :]
    branch = dot_nn(att_o[...], wproj[...]) + vec[4:5, :]
    for i in range(pieces):
        part = slice(i * rp, (i + 1) * rp)
        middle = xs[i][...].astype(F32) + branch[part, :]
        mid_o[part, :] = middle
        xhat, _ = norm_stats(middle)
        n2_o[part, :] = (xhat * vec[1:2, :] + vec[7:8, :]).astype(BF16)


def attn_fwd(c, info, own, others, vec, wqkv, wproj, held):
    cpd, rp, d = own.shape
    pieces = 1 + len(others)
    rows = rp * pieces
    whole = lambda a: pl.BlockSpec(a.shape, lambda i, s: (0,) * a.ndim)
    at_clip = lambda shape: pl.BlockSpec((None,) + shape, lambda i, s: (c, 0, 0))
    shapes = [
        ((rows, d), BF16),
        ((rows, 3 * d), BF16),
        ((rows, d), BF16),
        ((16, rows), F32),
        ((rows, d), F32),
        ((rows, d), BF16),
    ]
    in_specs = [at_clip((rp, d))] + [whole(o) for o in others] + [whole(vec), whole(wqkv), whole(wproj)]
    operands = [own, *others, vec, wqkv, wproj]
    aliases = {}
    if held is not None:
        aliases = {1 + len(operands) + i: i for i in range(6)}
        in_specs = in_specs + [pl.BlockSpec(memory_space=pl.ANY)] * 6
        operands = operands + list(held)
    return pl.pallas_call(
        functools.partial(attn_fwd_kernel, c, pieces),
        grid_spec=pltpu.PrefetchScalarGridSpec(
            num_scalar_prefetch=1,
            grid=(1,),
            in_specs=in_specs,
            out_specs=[at_clip(s) for s, _ in shapes],
            scratch_shapes=[pltpu.VMEM((rows, 128), F32)],
        ),
        out_shape=[jax.ShapeDtypeStruct((cpd,) + s, t) for s, t in shapes],
        input_output_aliases=aliases,
        compiler_params=pltpu.CompilerParams(vmem_limit_bytes=48 * MIB),
        cost_estimate=pl.CostEstimate(
            flops=2 * rows * d * 4 * d + 16 * HEADS * rows * rows * (d // HEADS),
            bytes_accessed=rows * d * 16 + 8 * d * d,
            transcendentals=HEADS * rows * rows,
        ),
        name="attn_fwd",
    )(info, *operands)


def mlp_fwd_kernel(pieces, info, mid, n2, vec, w1, b1, w2, *outs):
    h_o = outs[pieces]
    rows, d = n2.shape
    rp = rows // pieces
    full = info[1 + pl.program_id(0)] == 1
    ff = w1.shape[1]
    chunk = d
    x = n2[...]
    acc = mid[...] + vec[5:6, :]
    for j in range(ff // chunk):
        part = slice(j * chunk, (j + 1) * chunk)
        h = dot_nn(x, w1[:, part]) + b1[:, part]
        h_o[:, part] = h.astype(BF16)
        act = (h * (0.5 + 0.5 * lax.erf(h * 0.7071067811865476))).astype(BF16)
        acc = acc + dot_nn(act, w2[part, :])
    out = jnp.where(row_valid(rows, rp, full), acc, 0.0).astype(BF16)
    for i in range(pieces):
        outs[i][...] = out[i * rp : (i + 1) * rp, :]


def mlp_fwd(info, mid, n2, vec, w1, b1, w2, clips, pieces):
    cpd, rows, d = n2.shape
    ff = w1.shape[1]
    rp = rows // pieces
    by_clip = lambda w: pl.BlockSpec((None, rows, w), lambda c, s: (c, 0, 0))
    once = lambda a: pl.BlockSpec(a.shape, lambda c, s: (0, 0), pipeline_mode=pl.Buffered(1))
    return pl.pallas_call(
        functools.partial(mlp_fwd_kernel, pieces),
        grid_spec=pltpu.PrefetchScalarGridSpec(
            num_scalar_prefetch=1,
            grid=(cpd,),
            in_specs=[by_clip(d), by_clip(d), once(vec), once(w1), once(b1), once(w2)],
            out_specs=[pl.BlockSpec((None, rp, d), lambda c, s: (s[0] * cpd + c, 0, 0))]
            + [pl.BlockSpec((None, rp, d), lambda c, s: (c, 0, 0))] * (pieces - 1)
            + [by_clip(ff)],
        ),
        out_shape=[jax.ShapeDtypeStruct((clips, rp, d), BF16)]
        + [jax.ShapeDtypeStruct((cpd, rp, d), BF16)] * (pieces - 1)
        + [jax.ShapeDtypeStruct((cpd, rows, ff), BF16)],
        compiler_params=pltpu.CompilerParams(vmem_limit_bytes=56 * MIB),
        cost_estimate=pl.CostEstimate(
            flops=4 * cpd * rows * d * ff,
            bytes_accessed=cpd * rows * (8 * d + 2 * ff) + 4 * d * ff,
            transcendentals=cpd * rows * ff,
        ),
        name="mlp_fwd",
    )(info, mid, n2, vec, w1, b1, w2)


def upstream_of(cots, full):
    rp = cots[0].shape[0]
    keep = row_valid(rp, rp, full)
    return jnp.concatenate(
        [jnp.where(keep, c[...].astype(F32), 0.0) for c in cots], axis=0
    )


def mlp_back_hidden_kernel(pieces, info, *refs):
    cots = refs[:pieces]
    h, w2, dh_o, gw2_o, sums_o, fc1_sums_o, acc = refs[pieces:]
    r = pl.program_id(0)
    last = pl.num_programs(0) - 1
    up = upstream_of(cots, info[1 + r] == 1)
    up_low = up.astype(BF16)
    ff, d = w2.shape
    chunk = d

    @pl.when(r == 0)
    def _():
        acc[...] = jnp.zeros_like(acc)
        sums_o[...] = jnp.zeros_like(sums_o)
        fc1_sums_o[...] = jnp.zeros_like(fc1_sums_o)

    sums_o[0:1, :] += jnp.sum(up, axis=0, keepdims=True)
    for j in range(ff // chunk):
        part = slice(j * chunk, (j + 1) * chunk)
        pre = h[:, part].astype(F32)
        cdf = 0.5 + 0.5 * lax.erf(pre * 0.7071067811865476)
        density = 0.3989422804014327 * jnp.exp2(pre * pre * (-0.5 * LOG2E))
        act = (pre * cdf).astype(BF16)
        grad = dot_nt(up_low, w2[part, :])
        dh = (grad * (cdf + pre * density)).astype(BF16)
        dh_o[:, part] = dh
        fc1_sums_o[0:1, part] += jnp.sum(dh.astype(F32), axis=0, keepdims=True)
        acc[part, :] += dot_tn(act, up_low)

    @pl.when(r == last)
    def _():
        gw2_o[...] = acc[...].astype(BF16)


def mlp_back_hidden(info, cot, cot_others, h, w2):
    clips, rp, d = cot.shape
    cpd, rows, ff = h.shape
    pieces = 1 + len(cot_others)
    once = lambda a: pl.BlockSpec(a.shape, lambda c, s: (0, 0), pipeline_mode=pl.Buffered(1))
    held = lambda shape: pl.BlockSpec(shape, lambda c, s: (0, 0))
    return pl.pallas_call(
        functools.partial(mlp_back_hidden_kernel, pieces),
        grid_spec=pltpu.PrefetchScalarGridSpec(
            num_scalar_prefetch=1,
            grid=(cpd,),
            in_specs=[pl.BlockSpec((None, rp, d), lambda c, s: (s[0] * cpd + c, 0, 0))]
            + [pl.BlockSpec((None, rp, d), lambda c, s: (c, 0, 0))] * (pieces - 1)
            + [pl.BlockSpec((None, rows, ff), lambda c, s: (c, 0, 0)), once(w2)],
            out_specs=[
                pl.BlockSpec((None, rows, ff), lambda c, s: (c, 0, 0)),
                held((ff, d)),
                held((8, d)),
                held((8, ff)),
            ],
            scratch_shapes=[pltpu.VMEM((ff, d), F32)],
        ),
        out_shape=[
            jax.ShapeDtypeStruct((cpd, rows, ff), BF16),
            jax.ShapeDtypeStruct((ff, d), BF16),
            jax.ShapeDtypeStruct((8, d), F32),
            jax.ShapeDtypeStruct((8, ff), F32),
        ],
        compiler_params=pltpu.CompilerParams(vmem_limit_bytes=60 * MIB),
        cost_estimate=pl.CostEstimate(
            flops=4 * cpd * rows * d * ff,
            bytes_accessed=cpd * rows * (2 * d + 4 * ff) + 4 * d * ff,
            transcendentals=2 * cpd * rows * ff,
        ),
        name="mlp_back_hidden",
    )(info, cot, *cot_others, h, w2)


def mlp_back_input_kernel(pieces, info, *refs):
    cots = refs[:pieces]
    dh, n2, mid, vec, w1, dmid_o, gw1_o, sums_o, acc = refs[pieces:]
    r = pl.program_id(0)
    last = pl.num_programs(0) - 1

    @pl.when(r == 0)
    def _():
        acc[...] = jnp.zeros_like(acc)
        sums_o[...] = jnp.zeros_like(sums_o)

    d, ff = w1.shape
    chunk = d
    x = n2[...]
    dn2 = jnp.zeros(mid.shape, F32)
    for j in range(ff // chunk):
        part = slice(j * chunk, (j + 1) * chunk)
        piece = dh[:, part]
        dn2 = dn2 + dot_nt(piece, w1[:, part])
        acc[:, part] += dot_tn(x, piece)
    dx, gain, shift = norm_back(dn2, mid[...], vec[1:2, :])
    dmid = upstream_of(cots, info[1 + r] == 1) + dx
    dmid_o[...] = dmid
    sums_o[0:1, :] += gain
    sums_o[1:2, :] += shift

    @pl.when(r == last)
    def _():
        gw1_o[...] = acc[...].astype(BF16)


def mlp_back_input(info, cot, cot_others, dh, n2, mid, vec, w1):
    clips, rp, d = cot.shape
    cpd, rows, ff = dh.shape
    pieces = 1 + len(cot_others)
    once = lambda a: pl.BlockSpec(a.shape, lambda c, s: (0, 0), pipeline_mode=pl.Buffered(1))
    held = lambda shape: pl.BlockSpec(shape, lambda c, s: (0, 0))
    by_clip = lambda w: pl.BlockSpec((None, rows, w), lambda c, s: (c, 0, 0))
    return pl.pallas_call(
        functools.partial(mlp_back_input_kernel, pieces),
        grid_spec=pltpu.PrefetchScalarGridSpec(
            num_scalar_prefetch=1,
            grid=(cpd,),
            in_specs=[pl.BlockSpec((None, rp, d), lambda c, s: (s[0] * cpd + c, 0, 0))]
            + [pl.BlockSpec((None, rp, d), lambda c, s: (c, 0, 0))] * (pieces - 1)
            + [by_clip(ff), by_clip(d), by_clip(d), once(vec), once(w1)],
            out_specs=[by_clip(d), held((d, ff)), held((8, d))],
            scratch_shapes=[pltpu.VMEM((d, ff), F32)],
        ),
        out_shape=[
            jax.ShapeDtypeStruct((cpd, rows, d), F32),
            jax.ShapeDtypeStruct((d, ff), BF16),
            jax.ShapeDtypeStruct((8, d), F32),
        ],
        compiler_params=pltpu.CompilerParams(vmem_limit_bytes=60 * MIB),
        cost_estimate=pl.CostEstimate(
            flops=4 * cpd * rows * d * ff,
            bytes_accessed=cpd * rows * (12 * d + 2 * ff) + 4 * d * ff,
            transcendentals=0,
        ),
        name="mlp_back_input",
    )(info, cot, *cot_others, dh, n2, mid, vec, w1)


def attn_back_kernel(c, pieces, info, *refs):
    xs = refs[:pieces]
    keep, dmid, qkv, att, lse, vec, wqkv, wproj = refs[pieces : pieces + 8]
    dqkv_o, sums_o, *gtok = refs[-5 - pieces : -3]
    do_s, delta_s, dqt_s = refs[-3:]
    rp, d = xs[0].shape
    rows = rp * pieces
    hw = d // HEADS
    full = info[1 + c] == 1
    low_mid = dmid[...].astype(BF16)
    do_s[...] = dot_nt(low_mid, wproj[...]).astype(BF16)
    prod = do_s[...].astype(F32) * att[...].astype(F32)
    high = prod.astype(BF16)
    rest = (prod - high.astype(F32)).astype(BF16)
    head_of = lax.broadcasted_iota(jnp.int32, (16, d), 1) // hw
    select = (head_of == lax.broadcasted_iota(jnp.int32, (16, d), 0)).astype(BF16)
    delta_s[...] = dot_nt(select, high) + dot_nt(select, rest)
    scale = hw**-0.5
    scale2 = scale * LOG2E
    bias = jnp.where(row_valid(rows, rp, full), 0.0, -1e30).astype(BF16)
    lane = lax.broadcasted_iota(jnp.int32, (1, 2 * hw), 1)

    def pair(p, carry):
        at = pl.multiple_of(p * 2 * hw, 2 * hw)
        q = qkv[:, pl.ds(at, 2 * hw)]
        k = qkv[:, pl.ds(pl.multiple_of(d + at, 2 * hw), 2 * hw)]
        v = qkv[:, pl.ds(pl.multiple_of(2 * d + at, 2 * hw), 2 * hw)]
        do = do_s[:, pl.ds(at, 2 * hw)]
        kt = jnp.transpose(k)
        zero = jnp.zeros_like(q)
        dk = dv = None
        for e in range(2):
            mine = (lane < hw) if e == 0 else (lane >= hw)
            spare = lane == hw * (1 - e)
            one = jnp.where(spare, 1.0, 0.0).astype(BF16)
            qm = jnp.where(mine, q, one)
            km = jnp.where(spare, bias, k)
            st = dot_nt(km, qm)
            pt = jnp.exp2(st * scale2 - lse[pl.ds(2 * p + e, 1), :])
            vm = jnp.where(mine, v, zero)
            dpt = dot_nt(vm, do)
            dst = (pt * (dpt - delta_s[pl.ds(2 * p + e, 1), :])).astype(BF16)
            dom = jnp.where(mine, do, zero)
            qz = jnp.where(mine, q, zero)
            dv_e = dot_nn(pt.astype(BF16), dom)
            dk_e = dot_nn(dst, qz)
            dv = dv_e if dv is None else dv + dv_e
            dk = dk_e if dk is None else dk + dk_e
            dqt_s[pl.ds(pl.multiple_of(at + e * hw, hw), hw), :] = dot_nn(
                kt[e * hw : (e + 1) * hw, :], dst
            )
        dqkv_o[:, pl.ds(pl.multiple_of(d + at, 2 * hw), 2 * hw)] = (dk * scale).astype(BF16)
        dqkv_o[:, pl.ds(pl.multiple_of(2 * d + at, 2 * hw), 2 * hw)] = dv.astype(BF16)
        return carry

    lax.fori_loop(0, HEADS // 2, pair, 0)
    dqkv_o[:, 0:d] = jnp.transpose((dqt_s[...] * scale).astype(BF16))
    dn1 = dot_nt(dqkv_o[...], wqkv[...])
    sums_o[...] = jnp.zeros_like(sums_o)
    sums_o[0:1, :] = jnp.sum(dqkv_o[:, 0:d].astype(F32), axis=0, keepdims=True)
    sums_o[1:2, :] = jnp.sum(dqkv_o[:, 2 * d : 3 * d].astype(F32), axis=0, keepdims=True)
    sums_o[2:3, :] = jnp.sum(low_mid.astype(F32), axis=0, keepdims=True)
    for i in range(pieces):
        part = slice(i * rp, (i + 1) * rp)
        dx, gain, shift = norm_back(dn1[part, :], xs[i][...].astype(F32), vec[0:1, :])
        entered = dmid[part, :] + dx
        kept = entered * keep[part, :]
        gtok[i][...] = kept.astype(BF16)
        sums_o[3:4, :] += gain
        sums_o[4:5, :] += shift
        sums_o[5:6, :] += jnp.sum(entered - kept, axis=0, keepdims=True)


def attn_back(c, info, own, others, keep, dmid, qkv, att, lse, vec, wqkv, wproj, held, clips):
    cpd, rp, d = own.shape
    pieces = 1 + len(others)
    rows = rp * pieces
    whole = lambda a: pl.BlockSpec(a.shape, lambda i, s: (0,) * a.ndim)
    at_clip = lambda shape: pl.BlockSpec((None,) + shape, lambda i, s: (c, 0, 0))
    in_specs = (
        [at_clip((rp, d))]
        + [whole(o) for o in others]
        + [
            at_clip((rows, 1)),
            at_clip((rows, d)),
            at_clip((rows, 3 * d)),
            at_clip((rows, d)),
            at_clip((16, rows)),
            whole(vec),
            whole(wqkv),
            whole(wproj),
        ]
    )
    operands = [own, *others, keep, dmid, qkv, att, lse, vec, wqkv, wproj]
    aliases = {}
    if held is not None:
        aliases = {1 + len(operands) + i: i for i in range(3)}
        in_specs = in_specs + [pl.BlockSpec(memory_space=pl.ANY)] * 3
        operands = operands + list(held)
    return pl.pallas_call(
        functools.partial(attn_back_kernel, c, pieces),
        grid_spec=pltpu.PrefetchScalarGridSpec(
            num_scalar_prefetch=1,
            grid=(1,),
            in_specs=in_specs,
            out_specs=[
                at_clip((rows, 3 * d)),
                at_clip((8, d)),
                pl.BlockSpec((None, rp, d), lambda i, s: (s[0] * cpd + c, 0, 0)),
            ]
            + [pl.BlockSpec((rp, d), lambda i, s: (0, 0))] * (pieces - 1),
            scratch_shapes=[
                pltpu.VMEM((rows, d), BF16),
                pltpu.VMEM((16, rows), F32),
                pltpu.VMEM((d, rows), F32),
            ],
        ),
        out_shape=[
            jax.ShapeDtypeStruct((cpd, rows, 3 * d), BF16),
            jax.ShapeDtypeStruct((cpd, 8, d), F32),
            jax.ShapeDtypeStruct((clips, rp, d), BF16),
        ]
        + [jax.ShapeDtypeStruct((rp, d), BF16)] * (pieces - 1),
        input_output_aliases=aliases,
        compiler_params=pltpu.CompilerParams(vmem_limit_bytes=56 * MIB),
        cost_estimate=pl.CostEstimate(
            flops=2 * rows * d * 4 * d + 40 * HEADS * rows * rows * (d // HEADS),
            bytes_accessed=rows * d * 28 + 8 * d * d,
            transcendentals=HEADS * rows * rows,
        ),
        name="attn_back",
    )(info, *operands)


def weight_grad_kernel(a, b, o):
    o[...] = dot_tn(a[...].astype(BF16), b[...].astype(BF16)).astype(BF16)


def weight_grad(a, b, chunk):
    rows, m = a.shape
    n = b.shape[1]
    return pl.pallas_call(
        weight_grad_kernel,
        grid=(n // chunk,),
        in_specs=[
            pl.BlockSpec((rows, m), lambda j: (0, 0), pipeline_mode=pl.Buffered(1)),
            pl.BlockSpec((rows, chunk), lambda j: (0, j)),
        ],
        out_specs=pl.BlockSpec((m, chunk), lambda j: (0, j)),
        out_shape=jax.ShapeDtypeStruct((m, n), BF16),
        compiler_params=pltpu.CompilerParams(vmem_limit_bytes=48 * MIB),
        cost_estimate=pl.CostEstimate(
            flops=2 * rows * m * n, bytes_accessed=2 * (rows * m + rows * n + m * n), transcendentals=0
        ),
        name="weight_grad",
    )(a, b)


def power_of_two(n):
    return n & (n - 1) == 0


def scatter_sum(x, wide, narrow):
    rows, cols = x.shape
    if not (power_of_two(wide) and power_of_two(narrow)):
        return lax.psum_scatter(
            x.astype(F32), ("wide", "narrow"), scatter_dimension=0, tiled=True
        )
    bits_w, bits_n = wide.bit_length() - 1, narrow.bit_length() - 1
    order = [("wide", b, bits_w - 1 - b, wide) for b in range(bits_w)]
    order += [("narrow", b, bits_w + bits_n - 1 - b, narrow) for b in range(bits_n)]
    t = x.reshape((2,) * (bits_w + bits_n) + (rows // (wide * narrow), cols))
    for step, (axis, b, dim, size) in enumerate(order):
        mine = (lax.axis_index(axis) >> b) & 1
        keep = lax.dynamic_slice_in_dim(t, mine, 1, dim)
        send = lax.dynamic_slice_in_dim(t, 1 - mine, 1, dim)
        got = lax.ppermute(send, axis, [(i, i ^ (1 << b)) for i in range(size)])
        t = keep.astype(F32) + got.astype(F32)
        if step < len(order) - 1:
            t = t.astype(BF16)
    return t.reshape(rows // (wide * narrow), cols).astype(F32)


def body(
    wide,
    narrow,
    tokens,
    masked,
    resolution,
    mask_embed,
    gains,
    biases,
    w_qkv,
    w_proj,
    w_fc1,
    fc1_bias,
    w_fc2,
    cotangent,
):
    clips, freq_rows, cols, d = tokens.shape
    rp = freq_rows * cols
    cpd = clips // narrow
    rows = rp * narrow
    ff = w_fc1.shape[1]
    me = lax.axis_index("narrow")
    flat_tokens = tokens.reshape(clips, rp, d)
    flat_cot = cotangent.reshape(clips, rp, d)
    is_masked = masked.reshape(clips, rp) == 1

    def block_of(array, rank, at, count):
        return lax.dynamic_slice_in_dim(array, rank * cpd + at, count, 0)

    def entered_of(rank, at, count):
        return jnp.where(
            block_of(is_masked, rank, at, count)[:, :, None],
            mask_embed[None, None, :],
            block_of(flat_tokens, rank, at, count),
        )

    def to_rank(array, k):
        return lax.ppermute(array, "narrow", [(i, (i + k) % narrow) for i in range(narrow)])

    def from_rank(array, k):
        return lax.ppermute(array, "narrow", [(i, (i - k) % narrow) for i in range(narrow)])

    info = jnp.concatenate([me[None].astype(jnp.int32), block_of(resolution, me, 0, cpd)])
    vec = jnp.concatenate([gains.astype(F32).T, biases.astype(F32).T], axis=0)
    bias_row = fc1_bias.astype(F32)[None, :]

    shifts = range(1, narrow)
    others = [
        [to_rank(entered_of((me + k) % narrow, c, 1)[0], k) for k in shifts] for c in range(cpd)
    ]
    keep_cols = [block_of(masked.reshape(clips, rp), me, 0, cpd)]
    keep_cols += [to_rank(block_of(masked.reshape(clips, rp), (me + k) % narrow, 0, cpd), k) for k in shifts]
    keep = (jnp.concatenate(keep_cols, axis=1) != 1).astype(F32)[:, :, None]
    own = entered_of(me, 0, cpd)
    cot_send = [block_of(flat_cot, (me + k) % narrow, 0, cpd) for k in shifts]
    if narrow > 1:
        cot_send, others[-1] = lax.optimization_barrier((cot_send, others[-1]))
    cot_others = [to_rank(cot_send[k - 1], k) for k in shifts]

    held = None
    for c in range(cpd):
        held = attn_fwd(c, info, own, others[c], vec, w_qkv, w_proj, held)
    n1, qkv, att, lse, mid, n2 = held

    out, *rest = mlp_fwd(info, mid, n2, vec, w_fc1, bias_row, w_fc2, clips, narrow)
    out_others, h = rest[:-1], rest[-1]
    out_back = [from_rank(out_others[k - 1], k) for k in shifts]

    dh, g_fc2, up_sums, fc1_sums = mlp_back_hidden(info, flat_cot, cot_others, h, w_fc2)
    grad_fc2 = scatter_sum(g_fc2, wide, narrow)
    dmid, g_fc1, two_sums = mlp_back_input(info, flat_cot, cot_others, dh, n2, mid, vec, w_fc1)
    grad_fc1 = scatter_sum(g_fc1, wide, narrow)
    g_proj = weight_grad(att.reshape(cpd * rows, d), dmid.reshape(cpd * rows, d), d)
    grad_proj = scatter_sum(g_proj, wide, narrow)

    held = None
    tok_back = []
    for c in range(cpd):
        *held, = attn_back(
            c, info, own, others[c], keep, dmid, qkv, att, lse, vec, w_qkv, w_proj, held, clips
        )
        tok_back.append([from_rank(g, k) for k, g in zip(shifts, held[3:])])
        held = held[:3]
    dqkv, one_sums, grad_tokens = held
    one = jnp.sum(one_sums, axis=0)
    g_qkv = weight_grad(n1.reshape(cpd * rows, d), dqkv.reshape(cpd * rows, 3 * d), d)
    rows_of = jnp.concatenate(
        [
            one[5:6],
            one[3:4],
            two_sums[0:1],
            one[0:1],
            one[1:2],
            one[2:3],
            up_sums[0:1],
            one[4:5],
            two_sums[1:2],
        ],
        axis=0,
    )
    small = jnp.concatenate([rows_of.T, fc1_sums[0].reshape(d, ff // d)], axis=1)
    small = jnp.pad(small, ((0, 0), (0, -small.shape[1] % 128))).astype(BF16)
    last = scatter_sum(jnp.concatenate([g_qkv, small], axis=1), wide, narrow)
    grad_qkv = last[:, : 3 * d]
    vectors = last[:, 3 * d :]

    for k in shifts:
        rank = (me + k) % narrow
        out = lax.dynamic_update_slice_in_dim(out, out_back[k - 1], rank * cpd, 0)
    for c in range(cpd):
        for k in shifts:
            rank = (me + k) % narrow
            grad_tokens = lax.dynamic_update_slice_in_dim(
                grad_tokens, tok_back[c][k - 1][None], rank * cpd + c, 0
            )
    return (
        out.reshape(tokens.shape),
        grad_tokens.reshape(tokens.shape),
        vectors[:, 0],
        vectors[:, 1:3],
        vectors[:, 3:9],
        grad_qkv,
        grad_proj,
        grad_fc1,
        vectors[:, 9 : 9 + ff // d].reshape(-1),
        grad_fc2,
    )


def solution(mesh):
    split = P("wide", None, "narrow", None)
    every = P(("wide", "narrow"))
    rows = P(("wide", "narrow"), None)
    return jax.shard_map(
        functools.partial(body, mesh.shape["wide"], mesh.shape["narrow"]),
        mesh=mesh,
        in_specs=(split, P("wide", None, "narrow"), P("wide")) + (P(),) * 8 + (split,),
        out_specs=(split, split, every, rows, rows, rows, rows, rows, every, rows),
        check_vma=False,
    )
```

```python
import functools

import jax
import jax.numpy as jnp
from jax import lax
from jax.experimental import pallas as pl
from jax.experimental.pallas import tpu as pltpu
from jax.sharding import PartitionSpec as P

HEADS = 12
EPS = 1e-06
LOG2E = 1.4426950408889634
F32 = jnp.float32
BF16 = jnp.bfloat16
MIB = 1 << 20


def dot_nn(a, b):
    return jnp.dot(a, b, preferred_element_type=F32)


def dot_nt(a, b):
    return lax.dot_general(a, b, (((1,), (1,)), ((), ())), preferred_element_type=F32)


def dot_tn(a, b):
    return lax.dot_general(a, b, (((0,), (0,)), ((), ())), preferred_element_type=F32)


def norm_stats(x):
    centred = x - jnp.mean(x, axis=-1, keepdims=True)
    rstd = lax.rsqrt(jnp.mean(centred * centred, axis=-1, keepdims=True) + EPS)
    return centred * rstd, rstd


def norm_back(grad, x, gain):
    xhat, rstd = norm_stats(x)
    scaled = grad * gain
    inner = jnp.mean(scaled * xhat, axis=-1, keepdims=True)
    outer = jnp.mean(scaled, axis=-1, keepdims=True)
    dx = rstd * (scaled - outer - xhat * inner)
    return dx, jnp.sum(grad * xhat, axis=0, keepdims=True), jnp.sum(grad, axis=0, keepdims=True)


def row_valid(rows, piece_rows, full):
    at = lax.broadcasted_iota(jnp.int32, (rows, 1), 0) % piece_rows
    return (at < piece_rows // 2) | full


def attn_fwd_kernel(c, pieces, info, *refs):
    xs = refs[:pieces]
    vec, wqkv, wproj = refs[pieces : pieces + 3]
    n1_o, qkv_o, att_o, lse_o, mid_o, n2_o = refs[-7:-1]
    lse_s = refs[-1]
    rp, d = xs[0].shape
    rows = rp * pieces
    hw = d // HEADS
    full = info[1 + c] == 1
    for i in range(pieces):
        xhat, _ = norm_stats(xs[i][...].astype(F32))
        n1_o[i * rp : (i + 1) * rp, :] = (xhat * vec[0:1, :] + vec[6:7, :]).astype(BF16)
    n1 = n1_o[...]
    qkv_o[:, 0:d] = (dot_nn(n1, wqkv[:, 0:d]) + vec[2:3, :]).astype(BF16)
    qkv_o[:, d : 2 * d] = dot_nn(n1, wqkv[:, d : 2 * d]).astype(BF16)
    qkv_o[:, 2 * d : 3 * d] = (dot_nn(n1, wqkv[:, 2 * d : 3 * d]) + vec[3:4, :]).astype(BF16)
    scale2 = hw**-0.5 * LOG2E
    bias = jnp.where(row_valid(rows, rp, full), 0.0, -1e30).astype(BF16)
    lane = lax.broadcasted_iota(jnp.int32, (1, 2 * hw), 1)
    head_lane = lax.broadcasted_iota(jnp.int32, (1, 128), 1)
    lse_s[...] = jnp.zeros_like(lse_s)

    def pair(p, carry):
        at = p * 2 * hw
        q = qkv_o[:, pl.ds(at, 2 * hw)]
        k = qkv_o[:, pl.ds(d + at, 2 * hw)]
        v = qkv_o[:, pl.ds(2 * d + at, 2 * hw)]
        outs = []
        tops = []
        for e in range(2):
            mine = (lane < hw) if e == 0 else (lane >= hw)
            spare = lane == hw * (1 - e)
            one = jnp.where(spare, 1.0, 0.0).astype(BF16)
            qm = jnp.where(mine, q, one)
            km = jnp.where(spare, bias, k)
            s = dot_nt(qm, km)
            top = jnp.max(s, axis=-1, keepdims=True)
            pr = jnp.exp2((s - top) * scale2).astype(BF16)
            vm = jnp.where(mine, v, jnp.ones_like(v))
            outs.append(dot_nn(pr, vm))
            tops.append(top)
        low = lane < hw
        total = pltpu.roll(jnp.where(low, outs[1], outs[0]), hw, 1)
        att_o[:, pl.ds(at, 2 * hw)] = (jnp.where(low, outs[0], outs[1]) / total).astype(BF16)
        log_total = jnp.log2(total) + scale2 * jnp.where(low, tops[0], tops[1])
        first = jnp.broadcast_to(log_total[:, 0:1], (rows, 128))
        second = jnp.broadcast_to(log_total[:, hw : hw + 1], (rows, 128))
        lse_s[...] = jnp.where(
            head_lane == 2 * p, first, jnp.where(head_lane == 2 * p + 1, second, lse_s[...])
        )
        return carry

    for p in range(HEADS // 2):
        pair(p, 0)
    lse_o[...] = jnp.transpose(lse_s[...])[0:16, :]
    branch = dot_nn(att_o[...], wproj[...]) + vec[4:5, :]
    for i in range(pieces):
        part = slice(i * rp, (i + 1) * rp)
        middle = xs[i][...].astype(F32) + branch[part, :]
        mid_o[part, :] = middle
        xhat, _ = norm_stats(middle)
        n2_o[part, :] = (xhat * vec[1:2, :] + vec[7:8, :]).astype(BF16)


def attn_fwd(c, info, own, others, vec, wqkv, wproj, held):
    cpd, rp, d = own.shape
    pieces = 1 + len(others)
    rows = rp * pieces
    whole = lambda a: pl.BlockSpec(a.shape, lambda i, s: (0,) * a.ndim)
    at_clip = lambda shape: pl.BlockSpec((None,) + shape, lambda i, s: (c, 0, 0))
    shapes = [
        ((rows, d), BF16),
        ((rows, 3 * d), BF16),
        ((rows, d), BF16),
        ((16, rows), F32),
        ((rows, d), F32),
        ((rows, d), BF16),
    ]
    in_specs = [at_clip((rp, d))] + [whole(o) for o in others] + [whole(vec), whole(wqkv), whole(wproj)]
    operands = [own, *others, vec, wqkv, wproj]
    aliases = {}
    if held is not None:
        aliases = {1 + len(operands) + i: i for i in range(6)}
        in_specs = in_specs + [pl.BlockSpec(memory_space=pl.ANY)] * 6
        operands = operands + list(held)
    return pl.pallas_call(
        functools.partial(attn_fwd_kernel, c, pieces),
        grid_spec=pltpu.PrefetchScalarGridSpec(
            num_scalar_prefetch=1,
            grid=(1,),
            in_specs=in_specs,
            out_specs=[at_clip(s) for s, _ in shapes],
            scratch_shapes=[pltpu.VMEM((rows, 128), F32)],
        ),
        out_shape=[jax.ShapeDtypeStruct((cpd,) + s, t) for s, t in shapes],
        input_output_aliases=aliases,
        compiler_params=pltpu.CompilerParams(vmem_limit_bytes=48 * MIB),
        cost_estimate=pl.CostEstimate(
            flops=2 * rows * d * 4 * d + 16 * HEADS * rows * rows * (d // HEADS),
            bytes_accessed=rows * d * 16 + 8 * d * d,
            transcendentals=HEADS * rows * rows,
        ),
        name="attn_fwd",
    )(info, *operands)


def mlp_fwd_kernel(pieces, info, mid, n2, vec, w1, b1, w2, *outs):
    h_o = outs[pieces]
    rows, d = n2.shape
    rp = rows // pieces
    full = info[1 + pl.program_id(0)] == 1
    ff = w1.shape[1]
    chunk = d
    x = n2[...]
    acc = mid[...] + vec[5:6, :]
    for j in range(ff // chunk):
        part = slice(j * chunk, (j + 1) * chunk)
        h = dot_nn(x, w1[:, part]) + b1[:, part]
        h_o[:, part] = h.astype(BF16)
        act = (h * (0.5 + 0.5 * lax.erf(h * 0.7071067811865476))).astype(BF16)
        acc = acc + dot_nn(act, w2[part, :])
    out = jnp.where(row_valid(rows, rp, full), acc, 0.0).astype(BF16)
    for i in range(pieces):
        outs[i][...] = out[i * rp : (i + 1) * rp, :]


def mlp_fwd(info, mid, n2, vec, w1, b1, w2, clips, pieces):
    cpd, rows, d = n2.shape
    ff = w1.shape[1]
    rp = rows // pieces
    by_clip = lambda w: pl.BlockSpec((None, rows, w), lambda c, s: (c, 0, 0))
    once = lambda a: pl.BlockSpec(a.shape, lambda c, s: (0, 0), pipeline_mode=pl.Buffered(1))
    return pl.pallas_call(
        functools.partial(mlp_fwd_kernel, pieces),
        grid_spec=pltpu.PrefetchScalarGridSpec(
            num_scalar_prefetch=1,
            grid=(cpd,),
            in_specs=[by_clip(d), by_clip(d), once(vec), once(w1), once(b1), once(w2)],
            out_specs=[pl.BlockSpec((None, rp, d), lambda c, s: (s[0] * cpd + c, 0, 0))]
            + [pl.BlockSpec((None, rp, d), lambda c, s: (c, 0, 0))] * (pieces - 1)
            + [by_clip(ff)],
        ),
        out_shape=[jax.ShapeDtypeStruct((clips, rp, d), BF16)]
        + [jax.ShapeDtypeStruct((cpd, rp, d), BF16)] * (pieces - 1)
        + [jax.ShapeDtypeStruct((cpd, rows, ff), BF16)],
        compiler_params=pltpu.CompilerParams(vmem_limit_bytes=56 * MIB),
        cost_estimate=pl.CostEstimate(
            flops=4 * cpd * rows * d * ff,
            bytes_accessed=cpd * rows * (8 * d + 2 * ff) + 4 * d * ff,
            transcendentals=cpd * rows * ff,
        ),
        name="mlp_fwd",
    )(info, mid, n2, vec, w1, b1, w2)


def upstream_of(cots, full):
    rp = cots[0].shape[0]
    keep = row_valid(rp, rp, full)
    return jnp.concatenate(
        [jnp.where(keep, c[...].astype(F32), 0.0) for c in cots], axis=0
    )


def mlp_back_hidden_kernel(pieces, info, *refs):
    cots = refs[:pieces]
    h, w2, dh_o, gw2_o, sums_o, fc1_sums_o, acc = refs[pieces:]
    r = pl.program_id(0)
    last = pl.num_programs(0) - 1
    up = upstream_of(cots, info[1 + r] == 1)
    up_low = up.astype(BF16)
    ff, d = w2.shape
    chunk = d

    @pl.when(r == 0)
    def _():
        acc[...] = jnp.zeros_like(acc)
        sums_o[...] = jnp.zeros_like(sums_o)
        fc1_sums_o[...] = jnp.zeros_like(fc1_sums_o)

    sums_o[0:1, :] += jnp.sum(up, axis=0, keepdims=True)
    for j in range(ff // chunk):
        part = slice(j * chunk, (j + 1) * chunk)
        pre = h[:, part].astype(F32)
        cdf = 0.5 + 0.5 * lax.erf(pre * 0.7071067811865476)
        density = 0.3989422804014327 * jnp.exp2(pre * pre * (-0.5 * LOG2E))
        act = (pre * cdf).astype(BF16)
        grad = dot_nt(up_low, w2[part, :])
        dh = (grad * (cdf + pre * density)).astype(BF16)
        dh_o[:, part] = dh
        fc1_sums_o[0:1, part] += jnp.sum(dh.astype(F32), axis=0, keepdims=True)
        acc[part, :] += dot_tn(act, up_low)

    @pl.when(r == last)
    def _():
        gw2_o[...] = acc[...].astype(BF16)


def mlp_back_hidden(info, cot, cot_others, h, w2):
    clips, rp, d = cot.shape
    cpd, rows, ff = h.shape
    pieces = 1 + len(cot_others)
    once = lambda a: pl.BlockSpec(a.shape, lambda c, s: (0, 0), pipeline_mode=pl.Buffered(1))
    held = lambda shape: pl.BlockSpec(shape, lambda c, s: (0, 0))
    return pl.pallas_call(
        functools.partial(mlp_back_hidden_kernel, pieces),
        grid_spec=pltpu.PrefetchScalarGridSpec(
            num_scalar_prefetch=1,
            grid=(cpd,),
            in_specs=[pl.BlockSpec((None, rp, d), lambda c, s: (s[0] * cpd + c, 0, 0))]
            + [pl.BlockSpec((None, rp, d), lambda c, s: (c, 0, 0))] * (pieces - 1)
            + [pl.BlockSpec((None, rows, ff), lambda c, s: (c, 0, 0)), once(w2)],
            out_specs=[
                pl.BlockSpec((None, rows, ff), lambda c, s: (c, 0, 0)),
                held((ff, d)),
                held((8, d)),
                held((8, ff)),
            ],
            scratch_shapes=[pltpu.VMEM((ff, d), F32)],
        ),
        out_shape=[
            jax.ShapeDtypeStruct((cpd, rows, ff), BF16),
            jax.ShapeDtypeStruct((ff, d), BF16),
            jax.ShapeDtypeStruct((8, d), F32),
            jax.ShapeDtypeStruct((8, ff), F32),
        ],
        compiler_params=pltpu.CompilerParams(vmem_limit_bytes=60 * MIB),
        cost_estimate=pl.CostEstimate(
            flops=4 * cpd * rows * d * ff,
            bytes_accessed=cpd * rows * (2 * d + 4 * ff) + 4 * d * ff,
            transcendentals=2 * cpd * rows * ff,
        ),
        name="mlp_back_hidden",
    )(info, cot, *cot_others, h, w2)


def mlp_back_input_kernel(pieces, info, *refs):
    cots = refs[:pieces]
    dh, n2, mid, att, vec, w1, dmid_o, gw_o, sums_o, acc = refs[pieces:]
    r = pl.program_id(0)
    last = pl.num_programs(0) - 1

    @pl.when(r == 0)
    def _():
        acc[...] = jnp.zeros_like(acc)
        sums_o[...] = jnp.zeros_like(sums_o)

    d, ff = w1.shape
    chunk = d
    x = n2[...]
    dn2 = jnp.zeros(mid.shape, F32)
    for j in range(ff // chunk):
        part = slice(j * chunk, (j + 1) * chunk)
        piece = dh[:, part]
        dn2 = dn2 + dot_nt(piece, w1[:, part])
        acc[:, part] += dot_tn(x, piece)
    dx, gain, shift = norm_back(dn2, mid[...], vec[1:2, :])
    dmid = upstream_of(cots, info[1 + r] == 1) + dx
    dmid_o[...] = dmid
    acc[:, ff : ff + d] += dot_tn(att[...], dmid.astype(BF16))
    sums_o[0:1, :] += gain
    sums_o[1:2, :] += shift

    @pl.when(r == last)
    def _():
        gw_o[...] = acc[...].astype(BF16)


def mlp_back_input(info, cot, cot_others, dh, n2, mid, att, vec, w1):
    clips, rp, d = cot.shape
    cpd, rows, ff = dh.shape
    pieces = 1 + len(cot_others)
    once = lambda a: pl.BlockSpec(a.shape, lambda c, s: (0, 0), pipeline_mode=pl.Buffered(1))
    held = lambda shape: pl.BlockSpec(shape, lambda c, s: (0, 0))
    by_clip = lambda w: pl.BlockSpec((None, rows, w), lambda c, s: (c, 0, 0))
    return pl.pallas_call(
        functools.partial(mlp_back_input_kernel, pieces),
        grid_spec=pltpu.PrefetchScalarGridSpec(
            num_scalar_prefetch=1,
            grid=(cpd,),
            in_specs=[pl.BlockSpec((None, rp, d), lambda c, s: (s[0] * cpd + c, 0, 0))]
            + [pl.BlockSpec((None, rp, d), lambda c, s: (c, 0, 0))] * (pieces - 1)
            + [by_clip(ff), by_clip(d), by_clip(d), by_clip(d), once(vec), once(w1)],
            out_specs=[by_clip(d), held((d, ff + d)), held((8, d))],
            scratch_shapes=[pltpu.VMEM((d, ff + d), F32)],
        ),
        out_shape=[
            jax.ShapeDtypeStruct((cpd, rows, d), F32),
            jax.ShapeDtypeStruct((d, ff + d), BF16),
            jax.ShapeDtypeStruct((8, d), F32),
        ],
        compiler_params=pltpu.CompilerParams(vmem_limit_bytes=60 * MIB),
        cost_estimate=pl.CostEstimate(
            flops=4 * cpd * rows * d * ff,
            bytes_accessed=cpd * rows * (12 * d + 2 * ff) + 4 * d * ff,
            transcendentals=0,
        ),
        name="mlp_back_input",
    )(info, cot, *cot_others, dh, n2, mid, att, vec, w1)


def attn_back_kernel(c, pieces, info, *refs):
    xs = refs[:pieces]
    keep, dmid, qkv, att, lse, vec, wqkv, wproj = refs[pieces : pieces + 8]
    dqkv_o, sums_o, *gtok = refs[-5 - pieces : -3]
    do_s, delta_s, dqt_s = refs[-3:]
    rp, d = xs[0].shape
    rows = rp * pieces
    hw = d // HEADS
    full = info[1 + c] == 1
    low_mid = dmid[...].astype(BF16)
    do_s[...] = dot_nt(low_mid, wproj[...]).astype(BF16)
    prod = do_s[...].astype(F32) * att[...].astype(F32)
    high = prod.astype(BF16)
    rest = (prod - high.astype(F32)).astype(BF16)
    head_of = lax.broadcasted_iota(jnp.int32, (16, d), 1) // hw
    select = (head_of == lax.broadcasted_iota(jnp.int32, (16, d), 0)).astype(BF16)
    delta_s[...] = dot_nt(select, high) + dot_nt(select, rest)
    scale = hw**-0.5
    scale2 = scale * LOG2E
    bias = jnp.where(row_valid(rows, rp, full), 0.0, -1e30).astype(BF16)
    lane = lax.broadcasted_iota(jnp.int32, (1, 2 * hw), 1)

    def pair(p, carry):
        at = p * 2 * hw
        q = qkv[:, pl.ds(at, 2 * hw)]
        k = qkv[:, pl.ds(d + at, 2 * hw)]
        v = qkv[:, pl.ds(2 * d + at, 2 * hw)]
        do = do_s[:, pl.ds(at, 2 * hw)]
        kt = jnp.transpose(k)
        zero = jnp.zeros_like(q)
        dk = dv = None
        for e in range(2):
            mine = (lane < hw) if e == 0 else (lane >= hw)
            spare = lane == hw * (1 - e)
            one = jnp.where(spare, 1.0, 0.0).astype(BF16)
            qm = jnp.where(mine, q, one)
            km = jnp.where(spare, bias, k)
            st = dot_nt(km, qm)
            pt = jnp.exp2(st * scale2 - lse[pl.ds(2 * p + e, 1), :])
            vm = jnp.where(mine, v, zero)
            dpt = dot_nt(vm, do)
            dst = (pt * (dpt - delta_s[pl.ds(2 * p + e, 1), :])).astype(BF16)
            dom = jnp.where(mine, do, zero)
            qz = jnp.where(mine, q, zero)
            dv_e = dot_nn(pt.astype(BF16), dom)
            dk_e = dot_nn(dst, qz)
            dv = dv_e if dv is None else dv + dv_e
            dk = dk_e if dk is None else dk + dk_e
            dqt_s[pl.ds(at + e * hw, hw), :] = dot_nn(
                kt[e * hw : (e + 1) * hw, :], dst
            )
        dqkv_o[:, pl.ds(d + at, 2 * hw)] = (dk * scale).astype(BF16)
        dqkv_o[:, pl.ds(2 * d + at, 2 * hw)] = dv.astype(BF16)
        return carry

    for p in range(HEADS // 2):
        pair(p, 0)
    dqkv_o[:, 0:d] = jnp.transpose((dqt_s[...] * scale).astype(BF16))
    dn1 = dot_nt(dqkv_o[...], wqkv[...])
    sums_o[...] = jnp.zeros_like(sums_o)
    sums_o[0:1, :] = jnp.sum(dqkv_o[:, 0:d].astype(F32), axis=0, keepdims=True)
    sums_o[1:2, :] = jnp.sum(dqkv_o[:, 2 * d : 3 * d].astype(F32), axis=0, keepdims=True)
    sums_o[2:3, :] = jnp.sum(low_mid.astype(F32), axis=0, keepdims=True)
    for i in range(pieces):
        part = slice(i * rp, (i + 1) * rp)
        dx, gain, shift = norm_back(dn1[part, :], xs[i][...].astype(F32), vec[0:1, :])
        entered = dmid[part, :] + dx
        kept = entered * keep[part, :]
        gtok[i][...] = kept.astype(BF16)
        sums_o[3:4, :] += gain
        sums_o[4:5, :] += shift
        sums_o[5:6, :] += jnp.sum(entered - kept, axis=0, keepdims=True)


def attn_back(c, info, own, others, keep, dmid, qkv, att, lse, vec, wqkv, wproj, held, clips):
    cpd, rp, d = own.shape
    pieces = 1 + len(others)
    rows = rp * pieces
    whole = lambda a: pl.BlockSpec(a.shape, lambda i, s: (0,) * a.ndim)
    at_clip = lambda shape: pl.BlockSpec((None,) + shape, lambda i, s: (c, 0, 0))
    in_specs = (
        [at_clip((rp, d))]
        + [whole(o) for o in others]
        + [
            at_clip((rows, 1)),
            at_clip((rows, d)),
            at_clip((rows, 3 * d)),
            at_clip((rows, d)),
            at_clip((16, rows)),
            whole(vec),
            whole(wqkv),
            whole(wproj),
        ]
    )
    operands = [own, *others, keep, dmid, qkv, att, lse, vec, wqkv, wproj]
    aliases = {}
    if held is not None:
        aliases = {1 + len(operands) + i: i for i in range(3)}
        in_specs = in_specs + [pl.BlockSpec(memory_space=pl.ANY)] * 3
        operands = operands + list(held)
    return pl.pallas_call(
        functools.partial(attn_back_kernel, c, pieces),
        grid_spec=pltpu.PrefetchScalarGridSpec(
            num_scalar_prefetch=1,
            grid=(1,),
            in_specs=in_specs,
            out_specs=[
                at_clip((rows, 3 * d)),
                at_clip((8, d)),
                pl.BlockSpec((None, rp, d), lambda i, s: (s[0] * cpd + c, 0, 0)),
            ]
            + [pl.BlockSpec((rp, d), lambda i, s: (0, 0))] * (pieces - 1),
            scratch_shapes=[
                pltpu.VMEM((rows, d), BF16),
                pltpu.VMEM((16, rows), F32),
                pltpu.VMEM((d, rows), F32),
            ],
        ),
        out_shape=[
            jax.ShapeDtypeStruct((cpd, rows, 3 * d), BF16),
            jax.ShapeDtypeStruct((cpd, 8, d), F32),
            jax.ShapeDtypeStruct((clips, rp, d), BF16),
        ]
        + [jax.ShapeDtypeStruct((rp, d), BF16)] * (pieces - 1),
        input_output_aliases=aliases,
        compiler_params=pltpu.CompilerParams(vmem_limit_bytes=56 * MIB),
        cost_estimate=pl.CostEstimate(
            flops=2 * rows * d * 4 * d + 40 * HEADS * rows * rows * (d // HEADS),
            bytes_accessed=rows * d * 28 + 8 * d * d,
            transcendentals=HEADS * rows * rows,
        ),
        name="attn_back",
    )(info, *operands)


def weight_grad_kernel(a, b, o):
    o[...] = dot_tn(a[...].astype(BF16), b[...].astype(BF16)).astype(BF16)


def weight_grad(a, b, chunk):
    rows, m = a.shape
    n = b.shape[1]
    return pl.pallas_call(
        weight_grad_kernel,
        grid=(n // chunk,),
        in_specs=[
            pl.BlockSpec((rows, m), lambda j: (0, 0), pipeline_mode=pl.Buffered(1)),
            pl.BlockSpec((rows, chunk), lambda j: (0, j)),
        ],
        out_specs=pl.BlockSpec((m, chunk), lambda j: (0, j)),
        out_shape=jax.ShapeDtypeStruct((m, n), BF16),
        compiler_params=pltpu.CompilerParams(vmem_limit_bytes=48 * MIB),
        cost_estimate=pl.CostEstimate(
            flops=2 * rows * m * n, bytes_accessed=2 * (rows * m + rows * n + m * n), transcendentals=0
        ),
        name="weight_grad",
    )(a, b)


def power_of_two(n):
    return n & (n - 1) == 0


class ScatterSum:
    def __init__(self, x, wide, narrow):
        rows, cols = x.shape
        self.block = (rows // (wide * narrow), cols)
        self.sums = None
        if not (power_of_two(wide) and power_of_two(narrow)):
            self.order = []
            self.sums = lax.psum_scatter(
                x.astype(F32), ("wide", "narrow"), scatter_dimension=0, tiled=True
            )
            return
        bits_w, bits_n = wide.bit_length() - 1, narrow.bit_length() - 1
        self.order = [("wide", b, bits_w - 1 - b, wide) for b in range(bits_w)]
        self.order += [("narrow", b, bits_w + bits_n - 1 - b, narrow) for b in range(bits_n)]
        self.send_next(x.reshape((2,) * (bits_w + bits_n) + self.block))

    def send_next(self, t):
        if not self.order:
            self.sums = t
            return
        axis, bit, dim, size = self.order.pop(0)
        mine = (lax.axis_index(axis) >> bit) & 1
        self.keep = lax.dynamic_slice_in_dim(t, mine, 1, dim)
        self.sent = lax.dynamic_slice_in_dim(t, 1 - mine, 1, dim)
        self.got = lax.ppermute(self.sent, axis, [(i, i ^ (1 << bit)) for i in range(size)])

    def step(self):
        if self.sums is not None:
            return self.sums
        t = self.keep.astype(F32) + self.got.astype(F32)
        self.send_next(t.astype(BF16) if self.order else t)
        return self.sent if self.sums is None else self.sums

    def finish(self):
        while self.sums is None:
            self.step()
        return self.sums.reshape(self.block).astype(F32)


def after(value, *others):
    return lax.optimization_barrier((value, others))[0]


def body(
    wide,
    narrow,
    tokens,
    masked,
    resolution,
    mask_embed,
    gains,
    biases,
    w_qkv,
    w_proj,
    w_fc1,
    fc1_bias,
    w_fc2,
    cotangent,
):
    clips, freq_rows, cols, d = tokens.shape
    rp = freq_rows * cols
    cpd = clips // narrow
    rows = rp * narrow
    ff = w_fc1.shape[1]
    me = lax.axis_index("narrow")
    flat_tokens = tokens.reshape(clips, rp, d)
    flat_cot = cotangent.reshape(clips, rp, d)
    is_masked = masked.reshape(clips, rp) == 1

    def block_of(array, rank, at, count):
        return lax.dynamic_slice_in_dim(array, rank * cpd + at, count, 0)

    def entered_of(rank, at, count):
        return jnp.where(
            block_of(is_masked, rank, at, count)[:, :, None],
            mask_embed[None, None, :],
            block_of(flat_tokens, rank, at, count),
        )

    def to_rank(array, k):
        return lax.ppermute(array, "narrow", [(i, (i + k) % narrow) for i in range(narrow)])

    def from_rank(array, k):
        return lax.ppermute(array, "narrow", [(i, (i - k) % narrow) for i in range(narrow)])

    info = jnp.concatenate([me[None].astype(jnp.int32), block_of(resolution, me, 0, cpd)])
    vec = jnp.concatenate([gains.astype(F32).T, biases.astype(F32).T], axis=0)
    bias_row = fc1_bias.astype(F32)[None, :]

    shifts = range(1, narrow)
    others = [
        [to_rank(entered_of((me + k) % narrow, c, 1)[0], k) for k in shifts] for c in range(cpd)
    ]
    keep_cols = [block_of(masked.reshape(clips, rp), me, 0, cpd)]
    keep_cols += [to_rank(block_of(masked.reshape(clips, rp), (me + k) % narrow, 0, cpd), k) for k in shifts]
    keep = (jnp.concatenate(keep_cols, axis=1) != 1).astype(F32)[:, :, None]
    own = entered_of(me, 0, cpd)
    cot_send = [block_of(flat_cot, (me + k) % narrow, 0, cpd) for k in shifts]

    held = None
    for c in range(cpd):
        here = after(info, keep) if c == 1 else info
        held = attn_fwd(c, here, own, others[c], vec, w_qkv, w_proj, held)
        if c == min(1, cpd - 1):
            cot_send = after(cot_send, held[3])
    cot_others = [to_rank(cot_send[k - 1], k) for k in shifts]
    n1, qkv, att, lse, mid, n2 = held

    out, *rest = mlp_fwd(info, mid, n2, vec, w_fc1, bias_row, w_fc2, clips, narrow)
    out_others, h = rest[:-1], rest[-1]
    out_back = [from_rank(out_others[k - 1], k) for k in shifts]

    dh, g_fc2, up_sums, fc1_sums = mlp_back_hidden(info, flat_cot, cot_others, h, w_fc2)
    fc2_chain = ScatterSum(g_fc2, wide, narrow)
    dmid, g_fc1, two_sums = mlp_back_input(info, flat_cot, cot_others, dh, n2, mid, att, vec, w_fc1)
    fc1_chain = ScatterSum(g_fc1, wide, narrow)

    held = None
    tok_back = []
    for c in range(cpd):
        ready = [fc2_chain.step()] + ([fc1_chain.step()] if c > 0 else []) + ([out_back] if c == min(2, cpd - 1) else [])
        if c > 1:
            ready.append(tok_back[c - 2])
        here = after(info, *ready)
        *held, = attn_back(
            c, here, own, others[c], keep, dmid, qkv, att, lse, vec, w_qkv, w_proj, held, clips
        )
        tok_back.append([from_rank(g, k) for k, g in zip(shifts, held[3:])])
        held = held[:3]
    dqkv, one_sums, grad_tokens = held
    one = jnp.sum(one_sums, axis=0)
    n1 = after(n1, fc2_chain.step(), fc1_chain.step())
    g_qkv = weight_grad(n1.reshape(cpd * rows, d), dqkv.reshape(cpd * rows, 3 * d), d)
    rows_of = jnp.concatenate(
        [
            one[5:6],
            one[3:4],
            two_sums[0:1],
            one[0:1],
            one[1:2],
            one[2:3],
            up_sums[0:1],
            one[4:5],
            two_sums[1:2],
        ],
        axis=0,
    )
    small = jnp.concatenate([rows_of.T, fc1_sums[0].reshape(d, ff // d)], axis=1)
    small = jnp.pad(small, ((0, 0), (0, -small.shape[1] % 128))).astype(BF16)
    last = ScatterSum(jnp.concatenate([g_qkv, small], axis=1), wide, narrow).finish()
    grad_fc2 = fc2_chain.finish()
    fc1_proj = fc1_chain.finish()
    grad_fc1, grad_proj = fc1_proj[:, :ff], fc1_proj[:, ff:]
    grad_qkv = last[:, : 3 * d]
    vectors = last[:, 3 * d :]

    for k in shifts:
        rank = (me + k) % narrow
        out = lax.dynamic_update_slice_in_dim(out, out_back[k - 1], rank * cpd, 0)
    for c in range(cpd):
        for k in shifts:
            rank = (me + k) % narrow
            grad_tokens = lax.dynamic_update_slice_in_dim(
                grad_tokens, tok_back[c][k - 1][None], rank * cpd + c, 0
            )
    return (
        out.reshape(tokens.shape),
        grad_tokens.reshape(tokens.shape),
        vectors[:, 0],
        vectors[:, 1:3],
        vectors[:, 3:9],
        grad_qkv,
        grad_proj,
        grad_fc1,
        vectors[:, 9 : 9 + ff // d].reshape(-1),
        grad_fc2,
    )


def solution(mesh):
    split = P("wide", None, "narrow", None)
    every = P(("wide", "narrow"))
    rows = P(("wide", "narrow"), None)
    return jax.shard_map(
        functools.partial(body, mesh.shape["wide"], mesh.shape["narrow"]),
        mesh=mesh,
        in_specs=(split, P("wide", None, "narrow"), P("wide")) + (P(),) * 8 + (split,),
        out_specs=(split, split, every, rows, rows, rows, rows, rows, every, rows),
        check_vma=False,
    )
```

```python
import functools

import jax
import jax.numpy as jnp
from jax import lax
from jax.experimental import pallas as pl
from jax.experimental.pallas import tpu as pltpu
from jax.sharding import PartitionSpec as P

HEADS = 12
EPS = 1e-06
LOG2E = 1.4426950408889634
F32 = jnp.float32
BF16 = jnp.bfloat16
MIB = 1 << 20


def dot_nn(a, b):
    return jnp.dot(a, b, preferred_element_type=F32)


def dot_nt(a, b):
    return lax.dot_general(a, b, (((1,), (1,)), ((), ())), preferred_element_type=F32)


def dot_tn(a, b):
    return lax.dot_general(a, b, (((0,), (0,)), ((), ())), preferred_element_type=F32)


def norm_stats(x):
    centred = x - jnp.mean(x, axis=-1, keepdims=True)
    rstd = lax.rsqrt(jnp.mean(centred * centred, axis=-1, keepdims=True) + EPS)
    return centred * rstd, rstd


def norm_back(grad, x, gain):
    xhat, rstd = norm_stats(x)
    scaled = grad * gain
    inner = jnp.mean(scaled * xhat, axis=-1, keepdims=True)
    outer = jnp.mean(scaled, axis=-1, keepdims=True)
    dx = rstd * (scaled - outer - xhat * inner)
    return dx, jnp.sum(grad * xhat, axis=0, keepdims=True), jnp.sum(grad, axis=0, keepdims=True)


def copies_of(pairs, sems):
    return [pltpu.make_async_copy(a, b, sems.at[i]) for i, (a, b) in enumerate(pairs)]


def row_valid(rows, piece_rows, full):
    at = lax.broadcasted_iota(jnp.int32, (rows, 1), 0) % piece_rows
    return (at < piece_rows // 2) | full


def attn_fwd_kernel(c, pieces, info, *refs):
    xs = refs[:pieces]
    vec, wqkv, wproj = refs[pieces : pieces + 3]
    made = refs[-8:-2]
    n1_o, qkv_o, att_o, lse_o, mid_o, n2_o = made
    lse_s, sems = refs[-2:]
    saves = copies_of([(m, o.at[c]) for m, o in zip(made, refs[-14:-8])], sems)
    rp, d = xs[0].shape
    rows = rp * pieces
    hw = d // HEADS
    full = info[1 + c] == 1
    for i in range(pieces):
        xhat, _ = norm_stats(xs[i][...].astype(F32))
        n1_o[i * rp : (i + 1) * rp, :] = (xhat * vec[0:1, :] + vec[6:7, :]).astype(BF16)
    saves[0].start()
    n1 = n1_o[...]
    qkv_o[:, 0:d] = (dot_nn(n1, wqkv[:, 0:d]) + vec[2:3, :]).astype(BF16)
    qkv_o[:, d : 2 * d] = dot_nn(n1, wqkv[:, d : 2 * d]).astype(BF16)
    qkv_o[:, 2 * d : 3 * d] = (dot_nn(n1, wqkv[:, 2 * d : 3 * d]) + vec[3:4, :]).astype(BF16)
    saves[1].start()
    scale2 = hw**-0.5 * LOG2E
    bias = jnp.where(row_valid(rows, rp, full), 0.0, -1e30).astype(BF16)
    lane = lax.broadcasted_iota(jnp.int32, (1, 2 * hw), 1)
    head_lane = lax.broadcasted_iota(jnp.int32, (1, 128), 1)
    lse_s[...] = jnp.zeros_like(lse_s)

    def pair(p, carry):
        at = p * 2 * hw
        q = qkv_o[:, pl.ds(at, 2 * hw)]
        k = qkv_o[:, pl.ds(d + at, 2 * hw)]
        v = qkv_o[:, pl.ds(2 * d + at, 2 * hw)]
        outs = []
        tops = []
        for e in range(2):
            mine = (lane < hw) if e == 0 else (lane >= hw)
            spare = lane == hw * (1 - e)
            one = jnp.where(spare, 1.0, 0.0).astype(BF16)
            qm = jnp.where(mine, q, one)
            km = jnp.where(spare, bias, k)
            s = dot_nt(qm, km)
            top = jnp.max(s, axis=-1, keepdims=True)
            pr = jnp.exp2((s - top) * scale2).astype(BF16)
            vm = jnp.where(mine, v, jnp.ones_like(v))
            outs.append(dot_nn(pr, vm))
            tops.append(top)
        low = lane < hw
        total = pltpu.roll(jnp.where(low, outs[1], outs[0]), hw, 1)
        att_o[:, pl.ds(at, 2 * hw)] = (jnp.where(low, outs[0], outs[1]) / total).astype(BF16)
        log_total = jnp.log2(total) + scale2 * jnp.where(low, tops[0], tops[1])
        first = jnp.broadcast_to(log_total[:, 0:1], (rows, 128))
        second = jnp.broadcast_to(log_total[:, hw : hw + 1], (rows, 128))
        lse_s[...] = jnp.where(
            head_lane == 2 * p, first, jnp.where(head_lane == 2 * p + 1, second, lse_s[...])
        )
        return carry

    for p in range(HEADS // 2):
        pair(p, 0)
    lse_o[...] = jnp.transpose(lse_s[...])[0:16, :]
    saves[2].start()
    saves[3].start()
    branch = dot_nn(att_o[...], wproj[...]) + vec[4:5, :]
    for i in range(pieces):
        part = slice(i * rp, (i + 1) * rp)
        middle = xs[i][...].astype(F32) + branch[part, :]
        mid_o[part, :] = middle.astype(BF16)
        xhat, _ = norm_stats(middle)
        n2_o[part, :] = (xhat * vec[1:2, :] + vec[7:8, :]).astype(BF16)
    saves[4].start()
    saves[5].start()
    for save in saves:
        save.wait()


def attn_fwd(c, info, own, others, vec, wqkv, wproj, held):
    cpd, rp, d = own.shape
    pieces = 1 + len(others)
    rows = rp * pieces
    whole = lambda a: pl.BlockSpec(a.shape, lambda i, s: (0,) * a.ndim)
    at_clip = lambda shape: pl.BlockSpec((None,) + shape, lambda i, s: (c, 0, 0))
    shapes = [
        ((rows, d), BF16),
        ((rows, 3 * d), BF16),
        ((rows, d), BF16),
        ((16, rows), F32),
        ((rows, d), BF16),
        ((rows, d), BF16),
    ]
    in_specs = [at_clip((rp, d))] + [whole(o) for o in others] + [whole(vec), whole(wqkv), whole(wproj)]
    operands = [own, *others, vec, wqkv, wproj]
    aliases = {}
    if held is not None:
        aliases = {1 + len(operands) + i: i for i in range(6)}
        in_specs = in_specs + [pl.BlockSpec(memory_space=pl.ANY)] * 6
        operands = operands + list(held)
    return pl.pallas_call(
        functools.partial(attn_fwd_kernel, c, pieces),
        grid_spec=pltpu.PrefetchScalarGridSpec(
            num_scalar_prefetch=1,
            grid=(1,),
            in_specs=in_specs,
            out_specs=[pl.BlockSpec(memory_space=pl.ANY)] * len(shapes),
            scratch_shapes=[pltpu.VMEM(s, t) for s, t in shapes]
            + [pltpu.VMEM((rows, 128), F32), pltpu.SemaphoreType.DMA((len(shapes),))],
        ),
        out_shape=[jax.ShapeDtypeStruct((cpd,) + s, t) for s, t in shapes],
        input_output_aliases=aliases,
        compiler_params=pltpu.CompilerParams(vmem_limit_bytes=34 * MIB),
        cost_estimate=pl.CostEstimate(
            flops=2 * rows * d * 4 * d + 16 * HEADS * rows * rows * (d // HEADS),
            bytes_accessed=rows * d * 16 + 8 * d * d,
            transcendentals=HEADS * rows * rows,
        ),
        name="attn_fwd",
    )(info, *operands)


def mlp_fwd_kernel(pieces, info, mid, n2, vec, w1, b1, w2, *outs):
    h_o = outs[pieces]
    rows, d = n2.shape
    rp = rows // pieces
    full = info[1 + pl.program_id(0)] == 1
    ff = w1.shape[1]
    chunk = d
    x = n2[...]
    acc = mid[...].astype(F32) + vec[5:6, :]
    for j in range(ff // chunk):
        part = slice(j * chunk, (j + 1) * chunk)
        h = dot_nn(x, w1[:, part]) + b1[:, part]
        h_o[:, part] = h.astype(BF16)
        act = (h * (0.5 + 0.5 * lax.erf(h * 0.7071067811865476))).astype(BF16)
        acc = acc + dot_nn(act, w2[part, :])
    out = jnp.where(row_valid(rows, rp, full), acc, 0.0).astype(BF16)
    for i in range(pieces):
        outs[i][...] = out[i * rp : (i + 1) * rp, :]


def mlp_fwd(info, mid, n2, vec, w1, b1, w2, clips, pieces):
    cpd, rows, d = n2.shape
    ff = w1.shape[1]
    rp = rows // pieces
    by_clip = lambda w: pl.BlockSpec((None, rows, w), lambda c, s: (c, 0, 0))
    once = lambda a: pl.BlockSpec(a.shape, lambda c, s: (0, 0), pipeline_mode=pl.Buffered(1))
    return pl.pallas_call(
        functools.partial(mlp_fwd_kernel, pieces),
        grid_spec=pltpu.PrefetchScalarGridSpec(
            num_scalar_prefetch=1,
            grid=(cpd,),
            in_specs=[by_clip(d), by_clip(d), once(vec), once(w1), once(b1), once(w2)],
            out_specs=[pl.BlockSpec((None, rp, d), lambda c, s: (s[0] * cpd + c, 0, 0))]
            + [pl.BlockSpec((None, rp, d), lambda c, s: (c, 0, 0))] * (pieces - 1)
            + [by_clip(ff)],
        ),
        out_shape=[jax.ShapeDtypeStruct((clips, rp, d), BF16)]
        + [jax.ShapeDtypeStruct((cpd, rp, d), BF16)] * (pieces - 1)
        + [jax.ShapeDtypeStruct((cpd, rows, ff), BF16)],
        compiler_params=pltpu.CompilerParams(vmem_limit_bytes=36 * MIB),
        cost_estimate=pl.CostEstimate(
            flops=4 * cpd * rows * d * ff,
            bytes_accessed=cpd * rows * (8 * d + 2 * ff) + 4 * d * ff,
            transcendentals=cpd * rows * ff,
        ),
        name="mlp_fwd",
    )(info, mid, n2, vec, w1, b1, w2)


def upstream_of(cots, full):
    rp = cots[0].shape[0]
    keep = row_valid(rp, rp, full)
    return jnp.concatenate(
        [jnp.where(keep, c[...].astype(F32), 0.0) for c in cots], axis=0
    )


def mlp_back_kernel(pieces, cpd, info, *refs):
    cots = refs[:pieces]
    h, n2, mid, att, vec, w1, w2 = refs[pieces : pieces + 7]
    dmid_o, sums_o, fc1_sums_o, keep2, send2, keep1, send1 = refs[pieces + 7 : pieces + 14]
    acc1, acc2, dh_s, stage1, stage2, sems1, sems2 = refs[pieces + 14 :]
    r = pl.program_id(0)
    rows, d = mid.shape
    ff = w1.shape[1]
    chunk = d
    count = ff // chunk
    unit1 = keep1.shape[1]
    unit2 = keep2.shape[1]
    per2 = chunk // (2 * unit2)
    mine = info[1 + cpd]

    def saves1(j):
        cols = pl.ds(j * chunk, chunk)
        slot = j % 2
        return [
            pltpu.make_async_copy(
                stage1.at[slot, :, side], to.at[:, :, cols], sems1.at[slot, i]
            )
            for i, (side, to) in enumerate(((mine, keep1), (1 - mine, send1)))
        ]

    def saves2(j):
        at = pl.ds(j * per2, per2)
        slot = j % 2
        return [
            pltpu.make_async_copy(stage2.at[slot, :, side], to.at[at], sems2.at[slot, i])
            for i, (side, to) in enumerate(((mine, keep2), (1 - mine, send2)))
        ]

    def step(first, last):
        up = upstream_of(cots, info[1 + r] == 1)
        up_low = up.astype(BF16)
        up_sum = jnp.sum(up, axis=0, keepdims=True)
        for j in range(count):
            part = slice(j * chunk, (j + 1) * chunk)
            pre = h[:, part].astype(F32)
            cdf = 0.5 + 0.5 * lax.erf(pre * 0.7071067811865476)
            density = 0.3989422804014327 * jnp.exp2(pre * pre * (-0.5 * LOG2E))
            act = (pre * cdf).astype(BF16)
            grad = dot_nt(up_low, w2[part, :])
            dh = (grad * (cdf + pre * density)).astype(BF16)
            dh_s[:, part] = dh
            sums = jnp.sum(dh.astype(F32), axis=0, keepdims=True)
            total = dot_tn(act, up_low)
            if first:
                fc1_sums_o[0:1, part] = sums
            else:
                fc1_sums_o[0:1, part] += sums
                total = acc2[part, :] + total
            if last:
                if j > 1:
                    for save in saves2(j - 2):
                        save.wait()
                stage2[j % 2] = total.astype(BF16).reshape(per2, 2, unit2, d)
                for save in saves2(j):
                    save.start()
            else:
                acc2[part, :] = total
        dn2 = dot_nt(dh_s[...], w1[...])
        dx, gain, shift = norm_back(dn2, mid[...].astype(F32), vec[1:2, :])
        dmid = (up + dx).astype(BF16)
        dmid_o[...] = dmid
        if first:
            sums_o[0:1, :] = gain
            sums_o[1:2, :] = shift
            sums_o[2:3, :] = up_sum
        else:
            sums_o[0:1, :] += gain
            sums_o[1:2, :] += shift
            sums_o[2:3, :] += up_sum
        turned = jnp.transpose(n2[...])
        for j in range(count + 1):
            part = slice(j * chunk, (j + 1) * chunk)
            if j < count:
                total = dot_nn(turned, dh_s[:, part])
            else:
                total = dot_tn(att[...], dmid)
            if not first:
                total = acc1[:, part] + total
            if last:
                if j > 1:
                    for save in saves1(j - 2):
                        save.wait()
                stage1[j % 2] = total.astype(BF16).reshape(d // (2 * unit1), 2, unit1, chunk)
                for save in saves1(j):
                    save.start()
            else:
                acc1[:, part] = total
        if last:
            for j in range(max(count - 2, 0), count):
                for save in saves2(j):
                    save.wait()
            for j in range(max(count - 1, 0), count + 1):
                for save in saves1(j):
                    save.wait()

    if cpd == 1:
        step(True, True)
    else:

        @pl.when(r == 0)
        def _():
            step(True, False)

        @pl.when((r > 0) & (r < cpd - 1))
        def _():
            step(False, False)

        @pl.when(r == cpd - 1)
        def _():
            step(False, True)


def mlp_back(info, cot, cot_others, h, n2, mid, att, vec, w1, w2, parts):
    clips, rp, d = cot.shape
    cpd, rows, ff = h.shape
    pieces = 1 + len(cot_others)
    unit1 = d // parts
    unit2 = ff // parts
    once = lambda a: pl.BlockSpec(a.shape, lambda c, s: (0, 0), pipeline_mode=pl.Buffered(1))
    held = lambda shape: pl.BlockSpec(shape, lambda c, s: (0, 0))
    by_clip = lambda w: pl.BlockSpec((None, rows, w), lambda c, s: (c, 0, 0))
    halves = [(d // (2 * unit1), unit1, ff + d), (ff // (2 * unit2), unit2, d)]
    return pl.pallas_call(
        functools.partial(mlp_back_kernel, pieces, cpd),
        grid_spec=pltpu.PrefetchScalarGridSpec(
            num_scalar_prefetch=1,
            grid=(cpd,),
            in_specs=[pl.BlockSpec((None, rp, d), lambda c, s: (s[0] * cpd + c, 0, 0))]
            + [pl.BlockSpec((None, rp, d), lambda c, s: (c, 0, 0))] * (pieces - 1)
            + [by_clip(ff), by_clip(d), by_clip(d), by_clip(d), once(vec), once(w1), once(w2)],
            out_specs=[by_clip(d), held((8, d)), held((8, ff))]
            + [pl.BlockSpec(memory_space=pl.ANY)] * 4,
            scratch_shapes=[
                pltpu.VMEM((d, ff + d), F32),
                pltpu.VMEM((ff, d), F32),
                pltpu.VMEM((rows, ff), BF16),
                pltpu.VMEM((2, d // (2 * unit1), 2, unit1, d), BF16),
                pltpu.VMEM((2, d // (2 * unit2), 2, unit2, d), BF16),
                pltpu.SemaphoreType.DMA((2, 2)),
                pltpu.SemaphoreType.DMA((2, 2)),
            ],
        ),
        out_shape=[
            jax.ShapeDtypeStruct((cpd, rows, d), BF16),
            jax.ShapeDtypeStruct((8, d), F32),
            jax.ShapeDtypeStruct((8, ff), F32),
        ]
        + [jax.ShapeDtypeStruct(halves[1], BF16)] * 2
        + [jax.ShapeDtypeStruct(halves[0], BF16)] * 2,
        compiler_params=pltpu.CompilerParams(vmem_limit_bytes=62 * MIB),
        cost_estimate=pl.CostEstimate(
            flops=8 * cpd * rows * d * ff,
            bytes_accessed=cpd * rows * (14 * d + 2 * ff) + 8 * d * ff,
            transcendentals=2 * cpd * rows * ff,
        ),
        name="mlp_back",
    )(info, cot, *cot_others, h, n2, mid, att, vec, w1, w2)


def attn_back_kernel(c, pieces, cpd, info, *refs):
    xs = refs[:pieces]
    keep, dmid, qkv, att, lse, vec, wqkv, wproj = refs[pieces : pieces + 8]
    dqkv_o, sums_o, gtok, do_s, delta_s, dqt_s, sems = refs[-7:]
    dqkv_out, sums_out, own_out, *others_out = refs[-9 - pieces : -7]
    rp, d = xs[0].shape
    rows = rp * pieces
    hw = d // HEADS
    full = info[1 + c] == 1
    targets = [(dqkv_o, dqkv_out.at[c]), (sums_o, sums_out.at[c])]
    targets += [(gtok.at[0], own_out.at[info[0] * cpd + c])]
    targets += [(gtok.at[1 + i], o) for i, o in enumerate(others_out)]
    saves = copies_of(targets, sems)
    low_mid = dmid[...]
    do_s[...] = dot_nt(low_mid, wproj[...]).astype(BF16)
    prod = (do_s[...].astype(F32) * att[...].astype(F32)).astype(BF16)
    head_of = lax.broadcasted_iota(jnp.int32, (16, d), 1) // hw
    select = (head_of == lax.broadcasted_iota(jnp.int32, (16, d), 0)).astype(BF16)
    delta_s[...] = dot_nt(select, prod)
    scale = hw**-0.5
    scale2 = scale * LOG2E
    bias = jnp.where(row_valid(rows, rp, full), 0.0, -1e30).astype(BF16)
    lane = lax.broadcasted_iota(jnp.int32, (1, 2 * hw), 1)

    def pair(p, carry):
        at = p * 2 * hw
        q = qkv[:, pl.ds(at, 2 * hw)]
        k = qkv[:, pl.ds(d + at, 2 * hw)]
        v = qkv[:, pl.ds(2 * d + at, 2 * hw)]
        do = do_s[:, pl.ds(at, 2 * hw)]
        kt = jnp.transpose(k)
        zero = jnp.zeros_like(q)
        dk = dv = None
        for e in range(2):
            mine = (lane < hw) if e == 0 else (lane >= hw)
            spare = lane == hw * (1 - e)
            one = jnp.where(spare, 1.0, 0.0).astype(BF16)
            qm = jnp.where(mine, q, one)
            km = jnp.where(spare, bias, k)
            st = dot_nt(km, qm)
            pt = jnp.exp2(st * scale2 - lse[pl.ds(2 * p + e, 1), :])
            vm = jnp.where(mine, v, zero)
            dpt = dot_nt(vm, do)
            dst = (pt * (dpt - delta_s[pl.ds(2 * p + e, 1), :])).astype(BF16)
            dom = jnp.where(mine, do, zero)
            qz = jnp.where(mine, q, zero)
            dv_e = dot_nn(pt.astype(BF16), dom)
            dk_e = dot_nn(dst, qz)
            dv = dv_e if dv is None else dv + dv_e
            dk = dk_e if dk is None else dk + dk_e
            dqt_s[pl.ds(at + e * hw, hw), :] = dot_nn(
                kt[e * hw : (e + 1) * hw, :], dst
            )
        dqkv_o[:, pl.ds(d + at, 2 * hw)] = (dk * scale).astype(BF16)
        dqkv_o[:, pl.ds(2 * d + at, 2 * hw)] = dv.astype(BF16)
        return carry

    for p in range(HEADS // 2):
        pair(p, 0)
    dqkv_o[:, 0:d] = jnp.transpose((dqt_s[...] * scale).astype(BF16))
    saves[0].start()
    dn1 = dot_nt(dqkv_o[...], wqkv[...])
    sums_o[...] = jnp.zeros_like(sums_o)
    sums_o[0:1, :] = jnp.sum(dqkv_o[:, 0:d].astype(F32), axis=0, keepdims=True)
    sums_o[1:2, :] = jnp.sum(dqkv_o[:, 2 * d : 3 * d].astype(F32), axis=0, keepdims=True)
    sums_o[2:3, :] = jnp.sum(low_mid.astype(F32), axis=0, keepdims=True)
    for i in range(pieces):
        part = slice(i * rp, (i + 1) * rp)
        dx, gain, shift = norm_back(dn1[part, :], xs[i][...].astype(F32), vec[0:1, :])
        entered = low_mid[part, :].astype(F32) + dx
        kept = entered * keep[part, :]
        gtok[i] = kept.astype(BF16)
        saves[2 + i].start()
        sums_o[3:4, :] += gain
        sums_o[4:5, :] += shift
        sums_o[5:6, :] += jnp.sum(entered - kept, axis=0, keepdims=True)
    saves[1].start()
    for save in saves:
        save.wait()


def attn_back(c, info, own, others, keep, dmid, qkv, att, lse, vec, wqkv, wproj, held, clips):
    cpd, rp, d = own.shape
    pieces = 1 + len(others)
    rows = rp * pieces
    whole = lambda a: pl.BlockSpec(a.shape, lambda i, s: (0,) * a.ndim)
    at_clip = lambda shape: pl.BlockSpec((None,) + shape, lambda i, s: (c, 0, 0))
    in_specs = (
        [at_clip((rp, d))]
        + [whole(o) for o in others]
        + [
            at_clip((rows, 1)),
            at_clip((rows, d)),
            at_clip((rows, 3 * d)),
            at_clip((rows, d)),
            at_clip((16, rows)),
            whole(vec),
            whole(wqkv),
            whole(wproj),
        ]
    )
    operands = [own, *others, keep, dmid, qkv, att, lse, vec, wqkv, wproj]
    aliases = {}
    if held is not None:
        aliases = {1 + len(operands) + i: i for i in range(3)}
        in_specs = in_specs + [pl.BlockSpec(memory_space=pl.ANY)] * 3
        operands = operands + list(held)
    return pl.pallas_call(
        functools.partial(attn_back_kernel, c, pieces, cpd),
        grid_spec=pltpu.PrefetchScalarGridSpec(
            num_scalar_prefetch=1,
            grid=(1,),
            in_specs=in_specs,
            out_specs=[pl.BlockSpec(memory_space=pl.ANY)] * (2 + pieces),
            scratch_shapes=[
                pltpu.VMEM((rows, 3 * d), BF16),
                pltpu.VMEM((8, d), F32),
                pltpu.VMEM((pieces, rp, d), BF16),
                pltpu.VMEM((rows, d), BF16),
                pltpu.VMEM((16, rows), F32),
                pltpu.VMEM((d, rows), F32),
                pltpu.SemaphoreType.DMA((2 + pieces,)),
            ],
        ),
        out_shape=[
            jax.ShapeDtypeStruct((cpd, rows, 3 * d), BF16),
            jax.ShapeDtypeStruct((cpd, 8, d), F32),
            jax.ShapeDtypeStruct((clips, rp, d), BF16),
        ]
        + [jax.ShapeDtypeStruct((rp, d), BF16)] * (pieces - 1),
        input_output_aliases=aliases,
        compiler_params=pltpu.CompilerParams(vmem_limit_bytes=40 * MIB),
        cost_estimate=pl.CostEstimate(
            flops=2 * rows * d * 4 * d + 40 * HEADS * rows * rows * (d // HEADS),
            bytes_accessed=rows * d * 28 + 8 * d * d,
            transcendentals=HEADS * rows * rows,
        ),
        name="attn_back",
    )(info, *operands)


def weight_grad_kernel(a, b, o):
    o[...] = dot_tn(a[...].astype(BF16), b[...].astype(BF16)).astype(BF16)


def weight_grad(a, b, chunk):
    rows, m = a.shape
    n = b.shape[1]
    return pl.pallas_call(
        weight_grad_kernel,
        grid=(n // chunk,),
        in_specs=[
            pl.BlockSpec((rows, m), lambda j: (0, 0), pipeline_mode=pl.Buffered(1)),
            pl.BlockSpec((rows, chunk), lambda j: (0, j)),
        ],
        out_specs=pl.BlockSpec((m, chunk), lambda j: (0, j)),
        out_shape=jax.ShapeDtypeStruct((m, n), BF16),
        compiler_params=pltpu.CompilerParams(vmem_limit_bytes=48 * MIB),
        cost_estimate=pl.CostEstimate(
            flops=2 * rows * m * n, bytes_accessed=2 * (rows * m + rows * n + m * n), transcendentals=0
        ),
        name="weight_grad",
    )(a, b)


def power_of_two(n):
    return n & (n - 1) == 0


class ScatterSum:
    def __init__(self, x, wide, narrow, first=(), halves=None):
        rows, cols = x.shape if halves is None else (2 * halves[0].shape[0] * halves[0].shape[1], halves[0].shape[2])
        self.block = (rows // (wide * narrow), cols)
        self.sums = None
        if not (power_of_two(wide) and power_of_two(narrow)):
            self.order = []
            self.sums = lax.psum_scatter(
                x.astype(F32), ("wide", "narrow"), scatter_dimension=0, tiled=True
            )
            return
        bits_w, bits_n = wide.bit_length() - 1, narrow.bit_length() - 1
        self.order = [("wide", b, bits_w - 1 - b, wide) for b in range(bits_w)]
        self.order += [("narrow", b, bits_w + bits_n - 1 - b, narrow) for b in range(bits_n)]
        ahead = [o for key in first for o in self.order if o[:2] == key]
        self.order = ahead + [o for o in self.order if o not in ahead]
        shape = (2,) * (bits_w + bits_n) + self.block
        if halves is None:
            self.send_next(x.reshape(shape))
            return
        axis, bit, dim, size = self.order.pop(0)
        shape = shape[:dim] + (1,) + shape[dim + 1 :]
        self.keep, self.sent = (half.reshape(shape) for half in halves)
        self.got = lax.ppermute(self.sent, axis, [(i, i ^ (1 << bit)) for i in range(size)])

    def send_next(self, t):
        if not self.order:
            self.sums = t
            return
        axis, bit, dim, size = self.order.pop(0)
        mine = (lax.axis_index(axis) >> bit) & 1
        self.keep = lax.dynamic_slice_in_dim(t, mine, 1, dim)
        self.sent = lax.dynamic_slice_in_dim(t, 1 - mine, 1, dim)
        self.got = lax.ppermute(self.sent, axis, [(i, i ^ (1 << bit)) for i in range(size)])

    def step(self, behind=None):
        if self.sums is not None:
            return self.sums
        if behind is not None:
            self.keep = after(self.keep, behind)
        t = self.keep.astype(F32) + self.got.astype(F32)
        self.send_next(t.astype(BF16) if self.order else t)
        return self.sent if self.sums is None else self.sums

    def finish(self):
        while self.sums is None:
            self.step()
        return self.sums.reshape(self.block).astype(F32)


def after(value, *others):
    return lax.optimization_barrier((value, others))[0]


def body(
    wide,
    narrow,
    tokens,
    masked,
    resolution,
    mask_embed,
    gains,
    biases,
    w_qkv,
    w_proj,
    w_fc1,
    fc1_bias,
    w_fc2,
    cotangent,
):
    clips, freq_rows, cols, d = tokens.shape
    rp = freq_rows * cols
    cpd = clips // narrow
    rows = rp * narrow
    ff = w_fc1.shape[1]
    me = lax.axis_index("narrow")
    flat_tokens = tokens.reshape(clips, rp, d)
    flat_cot = cotangent.reshape(clips, rp, d)
    is_masked = masked.reshape(clips, rp) == 1

    def block_of(array, rank, at, count):
        return lax.dynamic_slice_in_dim(array, rank * cpd + at, count, 0)

    def entered_of(rank, at, count):
        return jnp.where(
            block_of(is_masked, rank, at, count)[:, :, None],
            mask_embed[None, None, :],
            block_of(flat_tokens, rank, at, count),
        )

    def to_rank(array, k):
        return lax.ppermute(array, "narrow", [(i, (i + k) % narrow) for i in range(narrow)])

    def from_rank(array, k):
        return lax.ppermute(array, "narrow", [(i, (i - k) % narrow) for i in range(narrow)])

    core = lax.axis_index("wide") & 1
    info = jnp.concatenate([me[None], block_of(resolution, me, 0, cpd), core[None]])
    vec = jnp.concatenate([gains.astype(F32).T, biases.astype(F32).T], axis=0)
    bias_row = fc1_bias.astype(F32)[None, :]

    shifts = range(1, narrow)
    others = []
    for c in range(cpd):
        send = [entered_of((me + k) % narrow, c, 1)[0] for k in shifts]
        if c > 0:
            send = after(send, others[-1])
        others.append([to_rank(send[k - 1], k) for k in shifts])
    keep_cols = [block_of(masked.reshape(clips, rp), me, 0, cpd)]
    keep_cols += [to_rank(block_of(masked.reshape(clips, rp), (me + k) % narrow, 0, cpd), k) for k in shifts]
    keep = (jnp.concatenate(keep_cols, axis=1) != 1).astype(F32)[:, :, None]
    own = entered_of(me, 0, cpd)
    cot_send = [block_of(flat_cot, (me + k) % narrow, 0, cpd) for k in shifts]

    held = None
    for c in range(cpd):
        here = after(info, keep) if c == 1 else info
        held = attn_fwd(c, here, own, others[c], vec, w_qkv, w_proj, held)
    cot_send = after(cot_send, others[-1])
    cot_others = [to_rank(cot_send[k - 1], k) for k in shifts]
    n1, qkv, att, lse, mid, n2 = held

    out, *rest = mlp_fwd(info, mid, n2, vec, w_fc1, bias_row, w_fc2, clips, narrow)
    out_others, h = rest[:-1], rest[-1]
    out_back = [from_rank(out_others[k - 1], k) for k in shifts]

    dmid, two_sums, fc1_sums, *halves = mlp_back(
        info, flat_cot, cot_others, h, n2, mid, att, vec, w_fc1, w_fc2, wide
    )
    fc2_chain = ScatterSum(None, wide, narrow, halves=halves[:2])
    fc1_chain = ScatterSum(None, wide, narrow, halves=halves[2:])

    held = None
    tok_back = []
    for c in range(cpd):
        behind = held[1] if c > 0 else two_sums
        ready = [fc2_chain.step(behind), fc1_chain.step(behind)] if c > 0 else []
        if c == 0:
            ready.append(out_back)
        if c > 1:
            ready.append(tok_back[c - 2])
        here = after(info, *ready)
        *held, = attn_back(
            c, here, own, others[c], keep, dmid, qkv, att, lse, vec, w_qkv, w_proj, held, clips
        )
        tok_back.append([from_rank(g, k) for k, g in zip(shifts, held[3:])])
        held = held[:3]
    dqkv, one_sums, grad_tokens = held
    one = jnp.sum(one_sums, axis=0)
    n1 = after(n1, fc2_chain.step(one_sums), fc1_chain.step(one_sums))
    g_qkv = weight_grad(n1.reshape(cpd * rows, d), dqkv.reshape(cpd * rows, 3 * d), d)
    rows_of = jnp.concatenate(
        [
            one[5:6],
            one[3:4],
            two_sums[0:1],
            one[0:1],
            one[1:2],
            one[2:3],
            two_sums[2:3],
            one[4:5],
            two_sums[1:2],
        ],
        axis=0,
    )
    small = jnp.concatenate([rows_of.T, fc1_sums[0].reshape(d, ff // d)], axis=1)
    small = jnp.pad(small, ((0, 0), (0, -small.shape[1] % 128))).astype(BF16)
    cut = 10 * d // 6 // 128 * 128
    chains = [
        ScatterSum(g_qkv[:, :cut], wide, narrow),
        ScatterSum(
            jnp.concatenate([g_qkv[:, cut:], small], axis=1),
            wide,
            narrow,
            (("wide", 0), ("wide", 2), ("wide", 1), ("narrow", 0)),
        ),
    ]
    while any(chain.sums is None for chain in chains):
        for chain in chains:
            chain.step()
    last = jnp.concatenate([chain.finish() for chain in chains], axis=1)
    grad_fc2 = fc2_chain.finish()
    fc1_proj = fc1_chain.finish()
    grad_fc1, grad_proj = fc1_proj[:, :ff], fc1_proj[:, ff:]
    grad_qkv = last[:, : 3 * d]
    vectors = last[:, 3 * d :]

    for k in shifts:
        rank = (me + k) % narrow
        out = lax.dynamic_update_slice_in_dim(out, out_back[k - 1], rank * cpd, 0)
    for c in range(cpd):
        for k in shifts:
            rank = (me + k) % narrow
            grad_tokens = lax.dynamic_update_slice_in_dim(
                grad_tokens, tok_back[c][k - 1][None], rank * cpd + c, 0
            )
    return (
        out.reshape(tokens.shape),
        grad_tokens.reshape(tokens.shape),
        vectors[:, 0],
        vectors[:, 1:3],
        vectors[:, 3:9],
        grad_qkv,
        grad_proj,
        grad_fc1,
        vectors[:, 9 : 9 + ff // d].reshape(-1),
        grad_fc2,
    )


def solution(mesh):
    split = P("wide", None, "narrow", None)
    every = P(("wide", "narrow"))
    rows = P(("wide", "narrow"), None)
    return jax.shard_map(
        functools.partial(body, mesh.shape["wide"], mesh.shape["narrow"]),
        mesh=mesh,
        in_specs=(split, P("wide", None, "narrow"), P("wide")) + (P(),) * 8 + (split,),
        out_specs=(split, split, every, rows, rows, rows, rows, rows, every, rows),
        check_vma=False,
    )
```

```python
import functools

import jax
import jax.numpy as jnp
from jax import lax
from jax.experimental import pallas as pl
from jax.experimental.pallas import tpu as pltpu
from jax.sharding import PartitionSpec as P

HEADS = 12
EPS = 1e-06
LOG2E = 1.4426950408889634
F32 = jnp.float32
BF16 = jnp.bfloat16
MIB = 1 << 20


def dot_nn(a, b):
    return jnp.dot(a, b, preferred_element_type=F32)


def dot_nt(a, b):
    return lax.dot_general(a, b, (((1,), (1,)), ((), ())), preferred_element_type=F32)


def dot_tn(a, b):
    return lax.dot_general(a, b, (((0,), (0,)), ((), ())), preferred_element_type=F32)


def norm_stats(x):
    centred = x - jnp.mean(x, axis=-1, keepdims=True)
    rstd = lax.rsqrt(jnp.mean(centred * centred, axis=-1, keepdims=True) + EPS)
    return centred * rstd, rstd


def norm_back(grad, x, gain):
    xhat, rstd = norm_stats(x)
    scaled = grad * gain
    inner = jnp.mean(scaled * xhat, axis=-1, keepdims=True)
    outer = jnp.mean(scaled, axis=-1, keepdims=True)
    dx = rstd * (scaled - outer - xhat * inner)
    return dx, jnp.sum(grad * xhat, axis=0, keepdims=True), jnp.sum(grad, axis=0, keepdims=True)


def copies_of(pairs, sems):
    return [pltpu.make_async_copy(a, b, sems.at[i]) for i, (a, b) in enumerate(pairs)]


def row_valid(rows, piece_rows, full):
    at = lax.broadcasted_iota(jnp.int32, (rows, 1), 0) % piece_rows
    return (at < piece_rows // 2) | full


def attn_fwd_kernel(c, pieces, info, *refs):
    xs = refs[:pieces]
    vec, wqkv, wproj = refs[pieces : pieces + 3]
    made = refs[-8:-2]
    n1_o, qkv_o, att_o, lse_o, mid_o, n2_o = made
    lse_s, sems = refs[-2:]
    saves = copies_of([(m, o.at[c]) for m, o in zip(made, refs[-14:-8])], sems)
    rp, d = xs[0].shape
    rows = rp * pieces
    hw = d // HEADS
    full = info[1 + c] == 1
    for i in range(pieces):
        xhat, _ = norm_stats(xs[i][...].astype(F32))
        n1_o[i * rp : (i + 1) * rp, :] = (xhat * vec[0:1, :] + vec[6:7, :]).astype(BF16)
    saves[0].start()
    n1 = n1_o[...]
    qkv_o[:, 0:d] = (dot_nn(n1, wqkv[:, 0:d]) + vec[2:3, :]).astype(BF16)
    qkv_o[:, d : 2 * d] = dot_nn(n1, wqkv[:, d : 2 * d]).astype(BF16)
    qkv_o[:, 2 * d : 3 * d] = (dot_nn(n1, wqkv[:, 2 * d : 3 * d]) + vec[3:4, :]).astype(BF16)
    saves[1].start()
    scale2 = hw**-0.5 * LOG2E
    bias = jnp.where(row_valid(rows, rp, full), 0.0, -1e30).astype(BF16)
    lane = lax.broadcasted_iota(jnp.int32, (1, 2 * hw), 1)
    head_lane = lax.broadcasted_iota(jnp.int32, (1, 128), 1)
    lse_s[...] = jnp.zeros_like(lse_s)

    def pair(p, carry):
        at = p * 2 * hw
        q = qkv_o[:, pl.ds(at, 2 * hw)]
        k = qkv_o[:, pl.ds(d + at, 2 * hw)]
        v = qkv_o[:, pl.ds(2 * d + at, 2 * hw)]
        outs = []
        tops = []
        for e in range(2):
            mine = (lane < hw) if e == 0 else (lane >= hw)
            spare = lane == hw * (1 - e)
            one = jnp.where(spare, 1.0, 0.0).astype(BF16)
            qm = jnp.where(mine, q, one)
            km = jnp.where(spare, bias, k)
            s = dot_nt(qm, km)
            top = jnp.max(s, axis=-1, keepdims=True)
            pr = jnp.exp2((s - top) * scale2).astype(BF16)
            vm = jnp.where(mine, v, jnp.ones_like(v))
            outs.append(dot_nn(pr, vm))
            tops.append(top)
        low = lane < hw
        total = pltpu.roll(jnp.where(low, outs[1], outs[0]), hw, 1)
        att_o[:, pl.ds(at, 2 * hw)] = (jnp.where(low, outs[0], outs[1]) / total).astype(BF16)
        log_total = jnp.log2(total) + scale2 * jnp.where(low, tops[0], tops[1])
        first = jnp.broadcast_to(log_total[:, 0:1], (rows, 128))
        second = jnp.broadcast_to(log_total[:, hw : hw + 1], (rows, 128))
        lse_s[...] = jnp.where(
            head_lane == 2 * p, first, jnp.where(head_lane == 2 * p + 1, second, lse_s[...])
        )
        return carry

    for p in range(HEADS // 2):
        pair(p, 0)
    lse_o[...] = jnp.transpose(lse_s[...])[0:16, :]
    saves[2].start()
    saves[3].start()
    branch = dot_nn(att_o[...], wproj[...]) + vec[4:5, :]
    for i in range(pieces):
        part = slice(i * rp, (i + 1) * rp)
        middle = xs[i][...].astype(F32) + branch[part, :]
        mid_o[part, :] = middle.astype(BF16)
        xhat, _ = norm_stats(middle)
        n2_o[part, :] = (xhat * vec[1:2, :] + vec[7:8, :]).astype(BF16)
    saves[4].start()
    saves[5].start()
    for save in saves:
        save.wait()


def attn_fwd(c, info, own, others, vec, wqkv, wproj, held):
    cpd, rp, d = own.shape
    pieces = 1 + len(others)
    rows = rp * pieces
    whole = lambda a: pl.BlockSpec(a.shape, lambda i, s: (0,) * a.ndim)
    at_clip = lambda shape: pl.BlockSpec((None,) + shape, lambda i, s: (c, 0, 0))
    shapes = [
        ((rows, d), BF16),
        ((rows, 3 * d), BF16),
        ((rows, d), BF16),
        ((16, rows), F32),
        ((rows, d), BF16),
        ((rows, d), BF16),
    ]
    in_specs = [at_clip((rp, d))] + [whole(o) for o in others] + [whole(vec), whole(wqkv), whole(wproj)]
    operands = [own, *others, vec, wqkv, wproj]
    aliases = {}
    if held is not None:
        aliases = {1 + len(operands) + i: i for i in range(6)}
        in_specs = in_specs + [pl.BlockSpec(memory_space=pl.ANY)] * 6
        operands = operands + list(held)
    return pl.pallas_call(
        functools.partial(attn_fwd_kernel, c, pieces),
        grid_spec=pltpu.PrefetchScalarGridSpec(
            num_scalar_prefetch=1,
            grid=(1,),
            in_specs=in_specs,
            out_specs=[pl.BlockSpec(memory_space=pl.ANY)] * len(shapes),
            scratch_shapes=[pltpu.VMEM(s, t) for s, t in shapes]
            + [pltpu.VMEM((rows, 128), F32), pltpu.SemaphoreType.DMA((len(shapes),))],
        ),
        out_shape=[jax.ShapeDtypeStruct((cpd,) + s, t) for s, t in shapes],
        input_output_aliases=aliases,
        compiler_params=pltpu.CompilerParams(vmem_limit_bytes=60 * MIB),
        cost_estimate=pl.CostEstimate(
            flops=2 * rows * d * 4 * d + 16 * HEADS * rows * rows * (d // HEADS),
            bytes_accessed=rows * d * 16 + 8 * d * d,
            transcendentals=HEADS * rows * rows,
        ),
        name="attn_fwd",
    )(info, *operands)


def mlp_fwd_kernel(pieces, info, mid, n2, vec, w1, b1, w2, *outs):
    h_o = outs[pieces]
    rows, d = n2.shape
    rp = rows // pieces
    full = info[1 + pl.program_id(0)] == 1
    ff = w1.shape[1]
    chunk = d
    x = n2[...]
    acc = mid[...].astype(F32) + vec[5:6, :]
    for j in range(ff // chunk):
        part = slice(j * chunk, (j + 1) * chunk)
        h = dot_nn(x, w1[:, part]) + b1[:, part]
        h_o[:, part] = h.astype(BF16)
        act = (h * (0.5 + 0.5 * lax.erf(h * 0.7071067811865476))).astype(BF16)
        acc = acc + dot_nn(act, w2[part, :])
    out = jnp.where(row_valid(rows, rp, full), acc, 0.0).astype(BF16)
    for i in range(pieces):
        outs[i][...] = out[i * rp : (i + 1) * rp, :]


def mlp_fwd(info, mid, n2, vec, w1, b1, w2, clips, pieces):
    cpd, rows, d = n2.shape
    ff = w1.shape[1]
    rp = rows // pieces
    by_clip = lambda w: pl.BlockSpec((None, rows, w), lambda c, s: (c, 0, 0))
    once = lambda a: pl.BlockSpec(a.shape, lambda c, s: (0, 0), pipeline_mode=pl.Buffered(1))
    return pl.pallas_call(
        functools.partial(mlp_fwd_kernel, pieces),
        grid_spec=pltpu.PrefetchScalarGridSpec(
            num_scalar_prefetch=1,
            grid=(cpd,),
            in_specs=[by_clip(d), by_clip(d), once(vec), once(w1), once(b1), once(w2)],
            out_specs=[pl.BlockSpec((None, rp, d), lambda c, s: (s[0] * cpd + c, 0, 0))]
            + [pl.BlockSpec((None, rp, d), lambda c, s: (c, 0, 0))] * (pieces - 1)
            + [by_clip(ff)],
        ),
        out_shape=[jax.ShapeDtypeStruct((clips, rp, d), BF16)]
        + [jax.ShapeDtypeStruct((cpd, rp, d), BF16)] * (pieces - 1)
        + [jax.ShapeDtypeStruct((cpd, rows, ff), BF16)],
        compiler_params=pltpu.CompilerParams(vmem_limit_bytes=60 * MIB),
        cost_estimate=pl.CostEstimate(
            flops=4 * cpd * rows * d * ff,
            bytes_accessed=cpd * rows * (8 * d + 2 * ff) + 4 * d * ff,
            transcendentals=cpd * rows * ff,
        ),
        name="mlp_fwd",
    )(info, mid, n2, vec, w1, b1, w2)


def upstream_of(cots, full):
    rp = cots[0].shape[0]
    keep = row_valid(rp, rp, full)
    return jnp.concatenate(
        [jnp.where(keep, c[...].astype(F32), 0.0) for c in cots], axis=0
    )


def mlp_back_kernel(pieces, cpd, info, *refs):
    cots = refs[:pieces]
    h, n2, mid, att, vec, w1_in, w2_in = refs[pieces : pieces + 7]
    dmid_o, sums_o, fc1_sums_o, keep2, send2, keep1, send1 = refs[pieces + 7 : pieces + 14]
    w1, w2, acc1, acc2, dn2_s, up_s, turned_s, stage1, stage2, sems_in, sems1, sems2 = refs[pieces + 14 :]
    r = pl.program_id(0)
    last = r == cpd - 1
    rows, d = mid.shape
    ff = w1.shape[1]
    chunk = d
    count = ff // chunk
    unit1 = keep1.shape[1]
    unit2 = keep2.shape[1]
    per2 = chunk // (2 * unit2)
    mine = info[1 + cpd]

    def cols_of(j):
        return pl.ds(pl.multiple_of(j * chunk, chunk), chunk)

    def loads(j):
        part = cols_of(j)
        return [
            pltpu.make_async_copy(w1_in.at[:, part], w1.at[:, part], sems_in.at[0, j]),
            pltpu.make_async_copy(w2_in.at[part], w2.at[part], sems_in.at[1, j]),
        ]

    def saves1(j, slot):
        cols = cols_of(j)
        return [
            pltpu.make_async_copy(stage1.at[slot, :, side], to.at[:, :, cols], sems1.at[slot, i])
            for i, (side, to) in enumerate(((mine, keep1), (1 - mine, send1)))
        ]

    def saves2(j, slot):
        at = pl.ds(j * per2, per2)
        return [
            pltpu.make_async_copy(stage2.at[slot, :, side], to.at[at], sems2.at[slot, i])
            for i, (side, to) in enumerate(((mine, keep2), (1 - mine, send2)))
        ]

    @pl.when(r == 0)
    def _():
        for j in range(count):
            for load in loads(j):
                load.start()
        acc1[...] = jnp.zeros_like(acc1)
        acc2[...] = jnp.zeros_like(acc2)
        sums_o[...] = jnp.zeros_like(sums_o)
        fc1_sums_o[...] = jnp.zeros_like(fc1_sums_o)

    up = upstream_of(cots, info[1 + r] == 1)
    up_s[...] = up.astype(BF16)
    sums_o[2:3, :] += jnp.sum(up, axis=0, keepdims=True)
    turned_s[...] = jnp.transpose(n2[...])
    dn2_s[...] = jnp.zeros_like(dn2_s)

    def one(j, carry):
        part = cols_of(j)

        @pl.when(r == 0)
        def _():
            for load in loads(j):
                load.wait()

        pre = h[:, part].astype(F32)
        cdf = 0.5 + 0.5 * lax.erf(pre * 0.7071067811865476)
        density = 0.3989422804014327 * jnp.exp2(pre * pre * (-0.5 * LOG2E))
        act = (pre * cdf).astype(BF16)
        grad = dot_nt(up_s[...], w2[part, :])
        dh = (grad * (cdf + pre * density)).astype(BF16)
        fc1_sums_o[0:1, part] += jnp.sum(dh.astype(F32), axis=0, keepdims=True)
        acc2[part, :] += dot_tn(act, up_s[...])
        dn2_s[...] += dot_nt(dh, w1[:, part])
        acc1[:, part] += dot_nn(turned_s[...], dh)

        @pl.when(last)
        def _():
            slot = j % 2

            @pl.when(j > 1)
            def _():
                for save in saves1(j - 2, slot) + saves2(j - 2, slot):
                    save.wait()

            stage2[slot] = acc2[part, :].astype(BF16).reshape(per2, 2, unit2, d)
            stage1[slot] = acc1[:, part].astype(BF16).reshape(d // (2 * unit1), 2, unit1, chunk)
            for save in saves1(j, slot) + saves2(j, slot):
                save.start()

        return carry

    lax.fori_loop(0, count, one, 0)
    dx, gain, shift = norm_back(dn2_s[...], mid[...].astype(F32), vec[1:2, :])
    dmid = (up_s[...].astype(F32) + dx).astype(BF16)
    dmid_o[...] = dmid
    sums_o[0:1, :] += gain
    sums_o[1:2, :] += shift
    acc1[:, ff : ff + d] += dot_tn(att[...], dmid)

    @pl.when(last)
    def _():
        for j in range(max(count - 2, 0), count):
            for save in saves1(j, j % 2) + saves2(j, j % 2):
                save.wait()
        stage1[0] = acc1[:, ff : ff + d].astype(BF16).reshape(d // (2 * unit1), 2, unit1, d)
        for save in saves1(count, 0):
            save.start()
        for save in saves1(count, 0):
            save.wait()


def mlp_back(info, cot, cot_others, h, n2, mid, att, vec, w1, w2, parts):
    clips, rp, d = cot.shape
    cpd, rows, ff = h.shape
    pieces = 1 + len(cot_others)
    unit1 = d // parts
    unit2 = ff // parts
    once = lambda a: pl.BlockSpec(a.shape, lambda c, s: (0, 0), pipeline_mode=pl.Buffered(1))
    held = lambda shape: pl.BlockSpec(shape, lambda c, s: (0, 0))
    by_clip = lambda w: pl.BlockSpec((None, rows, w), lambda c, s: (c, 0, 0))
    halves = [(d // (2 * unit1), unit1, ff + d), (ff // (2 * unit2), unit2, d)]
    return pl.pallas_call(
        functools.partial(mlp_back_kernel, pieces, cpd),
        grid_spec=pltpu.PrefetchScalarGridSpec(
            num_scalar_prefetch=1,
            grid=(cpd,),
            in_specs=[pl.BlockSpec((None, rp, d), lambda c, s: (s[0] * cpd + c, 0, 0))]
            + [pl.BlockSpec((None, rp, d), lambda c, s: (c, 0, 0))] * (pieces - 1)
            + [by_clip(ff), by_clip(d), by_clip(d), by_clip(d), once(vec)]
            + [pl.BlockSpec(memory_space=pl.ANY)] * 2,
            out_specs=[by_clip(d), held((8, d)), held((8, ff))]
            + [pl.BlockSpec(memory_space=pl.ANY)] * 4,
            scratch_shapes=[
                pltpu.VMEM(w1.shape, BF16),
                pltpu.VMEM(w2.shape, BF16),
                pltpu.VMEM((d, ff + d), F32),
                pltpu.VMEM((ff, d), F32),
                pltpu.VMEM((rows, d), F32),
                pltpu.VMEM((rows, d), BF16),
                pltpu.VMEM((d, rows), BF16),
                pltpu.VMEM((2, d // (2 * unit1), 2, unit1, d), BF16),
                pltpu.VMEM((2, d // (2 * unit2), 2, unit2, d), BF16),
                pltpu.SemaphoreType.DMA((2, ff // d)),
                pltpu.SemaphoreType.DMA((2, 2)),
                pltpu.SemaphoreType.DMA((2, 2)),
            ],
        ),
        out_shape=[
            jax.ShapeDtypeStruct((cpd, rows, d), BF16),
            jax.ShapeDtypeStruct((8, d), F32),
            jax.ShapeDtypeStruct((8, ff), F32),
        ]
        + [jax.ShapeDtypeStruct(halves[1], BF16)] * 2
        + [jax.ShapeDtypeStruct(halves[0], BF16)] * 2,
        compiler_params=pltpu.CompilerParams(vmem_limit_bytes=62 * MIB),
        cost_estimate=pl.CostEstimate(
            flops=8 * cpd * rows * d * ff,
            bytes_accessed=cpd * rows * (14 * d + 2 * ff) + 8 * d * ff,
            transcendentals=2 * cpd * rows * ff,
        ),
        name="mlp_back",
    )(info, cot, *cot_others, h, n2, mid, att, vec, w1, w2)


def attn_back_kernel(c, pieces, cpd, info, *refs):
    xs = refs[:pieces]
    keep, dmid, qkv, att, lse, vec, wqkv, wproj = refs[pieces : pieces + 8]
    dqkv_o, sums_o, gtok, do_s, delta_s, dqt_s, sems = refs[-7:]
    dqkv_out, sums_out, own_out, *others_out = refs[-9 - pieces : -7]
    rp, d = xs[0].shape
    rows = rp * pieces
    hw = d // HEADS
    full = info[1 + c] == 1
    targets = [(dqkv_o, dqkv_out.at[c]), (sums_o, sums_out.at[c])]
    targets += [(gtok.at[0], own_out.at[info[0] * cpd + c])]
    targets += [(gtok.at[1 + i], o) for i, o in enumerate(others_out)]
    saves = copies_of(targets, sems)
    low_mid = dmid[...]
    do_s[...] = dot_nt(low_mid, wproj[...]).astype(BF16)
    prod = (do_s[...].astype(F32) * att[...].astype(F32)).astype(BF16)
    head_of = lax.broadcasted_iota(jnp.int32, (16, d), 1) // hw
    select = (head_of == lax.broadcasted_iota(jnp.int32, (16, d), 0)).astype(BF16)
    delta_s[...] = dot_nt(select, prod)
    scale = hw**-0.5
    scale2 = scale * LOG2E
    bias = jnp.where(row_valid(rows, rp, full), 0.0, -1e30).astype(BF16)
    lane = lax.broadcasted_iota(jnp.int32, (1, 2 * hw), 1)

    def pair(p, carry):
        at = p * 2 * hw
        q = qkv[:, pl.ds(at, 2 * hw)]
        k = qkv[:, pl.ds(d + at, 2 * hw)]
        v = qkv[:, pl.ds(2 * d + at, 2 * hw)]
        do = do_s[:, pl.ds(at, 2 * hw)]
        kt = jnp.transpose(k)
        zero = jnp.zeros_like(q)
        dk = dv = None
        for e in range(2):
            mine = (lane < hw) if e == 0 else (lane >= hw)
            spare = lane == hw * (1 - e)
            one = jnp.where(spare, 1.0, 0.0).astype(BF16)
            qm = jnp.where(mine, q, one)
            km = jnp.where(spare, bias, k)
            st = dot_nt(km, qm)
            pt = jnp.exp2(st * scale2 - lse[pl.ds(2 * p + e, 1), :])
            vm = jnp.where(mine, v, zero)
            dpt = dot_nt(vm, do)
            dst = (pt * (dpt - delta_s[pl.ds(2 * p + e, 1), :])).astype(BF16)
            dom = jnp.where(mine, do, zero)
            qz = jnp.where(mine, q, zero)
            dv_e = dot_nn(pt.astype(BF16), dom)
            dk_e = dot_nn(dst, qz)
            dv = dv_e if dv is None else dv + dv_e
            dk = dk_e if dk is None else dk + dk_e
            dqt_s[pl.ds(at + e * hw, hw), :] = dot_nn(
                kt[e * hw : (e + 1) * hw, :], dst
            )
        dqkv_o[:, pl.ds(d + at, 2 * hw)] = (dk * scale).astype(BF16)
        dqkv_o[:, pl.ds(2 * d + at, 2 * hw)] = dv.astype(BF16)
        return carry

    for p in range(HEADS // 2):
        pair(p, 0)
    dqkv_o[:, 0:d] = jnp.transpose((dqt_s[...] * scale).astype(BF16))
    saves[0].start()
    dn1 = dot_nt(dqkv_o[...], wqkv[...])
    sums_o[...] = jnp.zeros_like(sums_o)
    sums_o[0:1, :] = jnp.sum(dqkv_o[:, 0:d].astype(F32), axis=0, keepdims=True)
    sums_o[1:2, :] = jnp.sum(dqkv_o[:, 2 * d : 3 * d].astype(F32), axis=0, keepdims=True)
    sums_o[2:3, :] = jnp.sum(low_mid.astype(F32), axis=0, keepdims=True)
    for i in range(pieces):
        part = slice(i * rp, (i + 1) * rp)
        dx, gain, shift = norm_back(dn1[part, :], xs[i][...].astype(F32), vec[0:1, :])
        entered = low_mid[part, :].astype(F32) + dx
        kept = entered * keep[part, :]
        gtok[i] = kept.astype(BF16)
        saves[2 + i].start()
        sums_o[3:4, :] += gain
        sums_o[4:5, :] += shift
        sums_o[5:6, :] += jnp.sum(entered - kept, axis=0, keepdims=True)
    saves[1].start()
    for save in saves:
        save.wait()


def attn_back(c, info, own, others, keep, dmid, qkv, att, lse, vec, wqkv, wproj, held, clips):
    cpd, rp, d = own.shape
    pieces = 1 + len(others)
    rows = rp * pieces
    whole = lambda a: pl.BlockSpec(a.shape, lambda i, s: (0,) * a.ndim)
    at_clip = lambda shape: pl.BlockSpec((None,) + shape, lambda i, s: (c, 0, 0))
    in_specs = (
        [at_clip((rp, d))]
        + [whole(o) for o in others]
        + [
            at_clip((rows, 1)),
            at_clip((rows, d)),
            at_clip((rows, 3 * d)),
            at_clip((rows, d)),
            at_clip((16, rows)),
            whole(vec),
            whole(wqkv),
            whole(wproj),
        ]
    )
    operands = [own, *others, keep, dmid, qkv, att, lse, vec, wqkv, wproj]
    aliases = {}
    if held is not None:
        aliases = {1 + len(operands) + i: i for i in range(3)}
        in_specs = in_specs + [pl.BlockSpec(memory_space=pl.ANY)] * 3
        operands = operands + list(held)
    return pl.pallas_call(
        functools.partial(attn_back_kernel, c, pieces, cpd),
        grid_spec=pltpu.PrefetchScalarGridSpec(
            num_scalar_prefetch=1,
            grid=(1,),
            in_specs=in_specs,
            out_specs=[pl.BlockSpec(memory_space=pl.ANY)] * (2 + pieces),
            scratch_shapes=[
                pltpu.VMEM((rows, 3 * d), BF16),
                pltpu.VMEM((8, d), F32),
                pltpu.VMEM((pieces, rp, d), BF16),
                pltpu.VMEM((rows, d), BF16),
                pltpu.VMEM((16, rows), F32),
                pltpu.VMEM((d, rows), F32),
                pltpu.SemaphoreType.DMA((2 + pieces,)),
            ],
        ),
        out_shape=[
            jax.ShapeDtypeStruct((cpd, rows, 3 * d), BF16),
            jax.ShapeDtypeStruct((cpd, 8, d), F32),
            jax.ShapeDtypeStruct((clips, rp, d), BF16),
        ]
        + [jax.ShapeDtypeStruct((rp, d), BF16)] * (pieces - 1),
        input_output_aliases=aliases,
        compiler_params=pltpu.CompilerParams(vmem_limit_bytes=60 * MIB),
        cost_estimate=pl.CostEstimate(
            flops=2 * rows * d * 4 * d + 40 * HEADS * rows * rows * (d // HEADS),
            bytes_accessed=rows * d * 28 + 8 * d * d,
            transcendentals=HEADS * rows * rows,
        ),
        name="attn_back",
    )(info, *operands)


def weight_grad_kernel(a, b, o):
    o[...] = dot_tn(a[...].astype(BF16), b[...].astype(BF16)).astype(BF16)


def weight_grad(a, b, chunk):
    rows, m = a.shape
    n = b.shape[1]
    return pl.pallas_call(
        weight_grad_kernel,
        grid=(n // chunk,),
        in_specs=[
            pl.BlockSpec((rows, m), lambda j: (0, 0), pipeline_mode=pl.Buffered(1)),
            pl.BlockSpec((rows, chunk), lambda j: (0, j)),
        ],
        out_specs=pl.BlockSpec((m, chunk), lambda j: (0, j)),
        out_shape=jax.ShapeDtypeStruct((m, n), BF16),
        compiler_params=pltpu.CompilerParams(vmem_limit_bytes=60 * MIB),
        cost_estimate=pl.CostEstimate(
            flops=2 * rows * m * n, bytes_accessed=2 * (rows * m + rows * n + m * n), transcendentals=0
        ),
        name="weight_grad",
    )(a, b)


def power_of_two(n):
    return n & (n - 1) == 0


class ScatterSum:
    def __init__(self, x, wide, narrow, first=(), halves=None):
        rows, cols = x.shape if halves is None else (2 * halves[0].shape[0] * halves[0].shape[1], halves[0].shape[2])
        self.block = (rows // (wide * narrow), cols)
        self.sums = None
        if not (power_of_two(wide) and power_of_two(narrow)):
            self.order = []
            self.sums = lax.psum_scatter(
                x.astype(F32), ("wide", "narrow"), scatter_dimension=0, tiled=True
            )
            return
        bits_w, bits_n = wide.bit_length() - 1, narrow.bit_length() - 1
        self.order = [("wide", b, bits_w - 1 - b, wide) for b in range(bits_w)]
        self.order += [("narrow", b, bits_w + bits_n - 1 - b, narrow) for b in range(bits_n)]
        ahead = [o for key in first for o in self.order if o[:2] == key]
        self.order = ahead + [o for o in self.order if o not in ahead]
        shape = (2,) * (bits_w + bits_n) + self.block
        if halves is None:
            self.send_next(x.reshape(shape))
            return
        axis, bit, dim, size = self.order.pop(0)
        shape = shape[:dim] + (1,) + shape[dim + 1 :]
        self.keep, self.sent = (half.reshape(shape) for half in halves)
        self.got = lax.ppermute(self.sent, axis, [(i, i ^ (1 << bit)) for i in range(size)])

    def send_next(self, t):
        if not self.order:
            self.sums = t
            return
        axis, bit, dim, size = self.order.pop(0)
        mine = (lax.axis_index(axis) >> bit) & 1
        self.keep = lax.dynamic_slice_in_dim(t, mine, 1, dim)
        self.sent = lax.dynamic_slice_in_dim(t, 1 - mine, 1, dim)
        self.got = lax.ppermute(self.sent, axis, [(i, i ^ (1 << bit)) for i in range(size)])

    def step(self, behind=None):
        if self.sums is not None:
            return self.sums
        if behind is not None:
            self.keep = after(self.keep, behind)
        t = self.keep.astype(F32) + self.got.astype(F32)
        self.send_next(t.astype(BF16) if self.order else t)
        return self.sent if self.sums is None else self.sums

    def finish(self, behind=None):
        while self.sums is None:
            self.step(behind)
        return self.sums.reshape(self.block).astype(F32)


def after(value, *others):
    return lax.optimization_barrier((value, others))[0]


def body(
    wide,
    narrow,
    tokens,
    masked,
    resolution,
    mask_embed,
    gains,
    biases,
    w_qkv,
    w_proj,
    w_fc1,
    fc1_bias,
    w_fc2,
    cotangent,
):
    clips, freq_rows, cols, d = tokens.shape
    rp = freq_rows * cols
    cpd = clips // narrow
    rows = rp * narrow
    ff = w_fc1.shape[1]
    me = lax.axis_index("narrow")
    flat_tokens = tokens.reshape(clips, rp, d)
    flat_cot = cotangent.reshape(clips, rp, d)
    is_masked = masked.reshape(clips, rp) == 1

    def block_of(array, rank, at, count):
        return lax.dynamic_slice_in_dim(array, rank * cpd + at, count, 0)

    def entered_of(rank, at, count):
        return jnp.where(
            block_of(is_masked, rank, at, count)[:, :, None],
            mask_embed[None, None, :],
            block_of(flat_tokens, rank, at, count),
        )

    def to_rank(array, k):
        return lax.ppermute(array, "narrow", [(i, (i + k) % narrow) for i in range(narrow)])

    def from_rank(array, k):
        return lax.ppermute(array, "narrow", [(i, (i - k) % narrow) for i in range(narrow)])

    core = lax.axis_index("wide") & 1
    info = jnp.concatenate([me[None], block_of(resolution, me, 0, cpd), core[None]])
    vec = jnp.concatenate([gains.astype(F32).T, biases.astype(F32).T], axis=0)
    bias_row = fc1_bias.astype(F32)[None, :]

    shifts = range(1, narrow)
    others = []
    for c in range(cpd):
        send = [entered_of((me + k) % narrow, c, 1)[0] for k in shifts]
        if c > 0:
            send = after(send, others[-1])
        others.append([to_rank(send[k - 1], k) for k in shifts])
    keep_cols = [block_of(masked.reshape(clips, rp), me, 0, cpd)]
    keep_cols += [to_rank(block_of(masked.reshape(clips, rp), (me + k) % narrow, 0, cpd), k) for k in shifts]
    keep = (jnp.concatenate(keep_cols, axis=1) != 1).astype(F32)[:, :, None]
    own = entered_of(me, 0, cpd)
    cot_send = [block_of(flat_cot, (me + k) % narrow, 0, cpd) for k in shifts]

    held = None
    for c in range(cpd):
        here = after(info, keep) if c == 1 else info
        held = attn_fwd(c, here, own, others[c], vec, w_qkv, w_proj, held)
    cot_send = after(cot_send, others[-1])
    cot_others = [to_rank(cot_send[k - 1], k) for k in shifts]
    n1, qkv, att, lse, mid, n2 = held

    out, *rest = mlp_fwd(info, mid, n2, vec, w_fc1, bias_row, w_fc2, clips, narrow)
    out_others, h = rest[:-1], rest[-1]
    out_back = [from_rank(out_others[k - 1], k) for k in shifts]

    dmid, two_sums, fc1_sums, *halves = mlp_back(
        info, flat_cot, cot_others, h, n2, mid, att, vec, w_fc1, w_fc2, wide
    )
    fc2_chain = ScatterSum(None, wide, narrow, halves=halves[:2])
    z_first = (("wide", 0), ("wide", 2), ("wide", 1), ("narrow", 0))
    fc1_chain = ScatterSum(None, wide, narrow, z_first, halves[2:])

    held = None
    tok_back = []
    for c in range(cpd):
        behind = held[1] if c > 0 else two_sums
        ready = [fc2_chain.step(behind), fc1_chain.step(behind)] if c in (1, 3) else []
        if c == 0:
            ready.append(out_back)
        if c > 1:
            tok_back[c - 2] = after(tok_back[c - 2], behind)
            ready.append(tok_back[c - 2])
        here = after(info, *ready)
        *held, = attn_back(
            c, here, own, others[c], keep, dmid, qkv, att, lse, vec, w_qkv, w_proj, held, clips
        )
        tok_back.append([from_rank(g, k) for k, g in zip(shifts, held[3:])])
        held = held[:3]
    dqkv, one_sums, grad_tokens = held
    one = jnp.sum(one_sums, axis=0)
    n1 = after(n1, fc2_chain.step(one_sums), fc1_chain.step(one_sums))
    g_qkv = weight_grad(n1.reshape(cpd * rows, d), dqkv.reshape(cpd * rows, 3 * d), d)
    rows_of = jnp.concatenate(
        [
            one[5:6],
            one[3:4],
            two_sums[0:1],
            one[0:1],
            one[1:2],
            one[2:3],
            two_sums[2:3],
            one[4:5],
            two_sums[1:2],
        ],
        axis=0,
    )
    small = jnp.concatenate([rows_of.T, fc1_sums[0].reshape(d, ff // d)], axis=1)
    small = jnp.pad(small, ((0, 0), (0, -small.shape[1] % 128))).astype(BF16)
    cut = 10 * d // 6 // 128 * 128
    chains = [
        ScatterSum(g_qkv[:, :cut], wide, narrow),
        ScatterSum(
            jnp.concatenate([g_qkv[:, cut:], small], axis=1),
            wide,
            narrow,
            z_first,
        ),
    ]
    while any(chain.sums is None for chain in chains):
        for chain in chains:
            chain.step()
    last = jnp.concatenate([chain.finish() for chain in chains], axis=1)
    grad_fc2 = fc2_chain.finish(g_qkv)
    fc1_proj = fc1_chain.finish(g_qkv)
    tok_back = after(tok_back, g_qkv)
    grad_fc1, grad_proj = fc1_proj[:, :ff], fc1_proj[:, ff:]
    grad_qkv = last[:, : 3 * d]
    vectors = last[:, 3 * d :]

    for k in shifts:
        rank = (me + k) % narrow
        out = lax.dynamic_update_slice_in_dim(out, out_back[k - 1], rank * cpd, 0)
    for c in range(cpd):
        for k in shifts:
            rank = (me + k) % narrow
            grad_tokens = lax.dynamic_update_slice_in_dim(
                grad_tokens, tok_back[c][k - 1][None], rank * cpd + c, 0
            )
    return (
        out.reshape(tokens.shape),
        grad_tokens.reshape(tokens.shape),
        vectors[:, 0],
        vectors[:, 1:3],
        vectors[:, 3:9],
        grad_qkv,
        grad_proj,
        grad_fc1,
        vectors[:, 9 : 9 + ff // d].reshape(-1),
        grad_fc2,
    )


def solution(mesh):
    split = P("wide", None, "narrow", None)
    every = P(("wide", "narrow"))
    rows = P(("wide", "narrow"), None)
    return jax.shard_map(
        functools.partial(body, mesh.shape["wide"], mesh.shape["narrow"]),
        mesh=mesh,
        in_specs=(split, P("wide", None, "narrow"), P("wide")) + (P(),) * 8 + (split,),
        out_specs=(split, split, every, rows, rows, rows, rows, rows, every, rows),
        check_vma=False,
    )
```

```python
import functools

import jax
import jax.numpy as jnp
from jax import lax
from jax.experimental import pallas as pl
from jax.experimental.pallas import tpu as pltpu
from jax.sharding import PartitionSpec as P

HEADS = 12
EPS = 1e-06
LOG2E = 1.4426950408889634
F32 = jnp.float32
BF16 = jnp.bfloat16
MIB = 1 << 20


def dot_nn(a, b):
    return jnp.dot(a, b, preferred_element_type=F32)


def dot_nt(a, b):
    return lax.dot_general(a, b, (((1,), (1,)), ((), ())), preferred_element_type=F32)


def dot_tn(a, b):
    return lax.dot_general(a, b, (((0,), (0,)), ((), ())), preferred_element_type=F32)


def norm_stats(x):
    centred = x - jnp.mean(x, axis=-1, keepdims=True)
    rstd = lax.rsqrt(jnp.mean(centred * centred, axis=-1, keepdims=True) + EPS)
    return centred * rstd, rstd


def norm_back(grad, x, gain):
    xhat, rstd = norm_stats(x)
    scaled = grad * gain
    inner = jnp.mean(scaled * xhat, axis=-1, keepdims=True)
    outer = jnp.mean(scaled, axis=-1, keepdims=True)
    dx = rstd * (scaled - outer - xhat * inner)
    return dx, jnp.sum(grad * xhat, axis=0, keepdims=True), jnp.sum(grad, axis=0, keepdims=True)


def copies_of(pairs, sems):
    return [pltpu.make_async_copy(a, b, sems.at[i]) for i, (a, b) in enumerate(pairs)]


def row_valid(rows, piece_rows, full):
    at = lax.broadcasted_iota(jnp.int32, (rows, 1), 0) % piece_rows
    return (at < piece_rows // 2) | full


def attn_fwd_kernel(c, pieces, info, *refs):
    xs = refs[:pieces]
    vec, wqkv, wproj = refs[pieces : pieces + 3]
    made = refs[-8:-2]
    n1_o, qkv_o, att_o, lse_o, mid_o, n2_o = made
    lse_s, sems = refs[-2:]
    saves = copies_of([(m, o.at[c]) for m, o in zip(made, refs[-14:-8])], sems)
    rp, d = xs[0].shape
    rows = rp * pieces
    hw = d // HEADS
    full = info[1 + c] == 1
    for i in range(pieces):
        xhat, _ = norm_stats(xs[i][...].astype(F32))
        n1_o[i * rp : (i + 1) * rp, :] = (xhat * vec[0:1, :] + vec[6:7, :]).astype(BF16)
    saves[0].start()
    n1 = n1_o[...]
    qkv_o[:, 0:d] = (dot_nn(n1, wqkv[:, 0:d]) + vec[2:3, :]).astype(BF16)
    qkv_o[:, d : 2 * d] = dot_nn(n1, wqkv[:, d : 2 * d]).astype(BF16)
    qkv_o[:, 2 * d : 3 * d] = (dot_nn(n1, wqkv[:, 2 * d : 3 * d]) + vec[3:4, :]).astype(BF16)
    saves[1].start()
    scale2 = hw**-0.5 * LOG2E
    bias = jnp.where(row_valid(rows, rp, full), 0.0, -1e30).astype(BF16)
    lane = lax.broadcasted_iota(jnp.int32, (1, 2 * hw), 1)
    head_lane = lax.broadcasted_iota(jnp.int32, (1, 128), 1)
    lse_s[...] = jnp.zeros_like(lse_s)

    def pair(p, carry):
        at = p * 2 * hw
        q = qkv_o[:, pl.ds(at, 2 * hw)]
        k = qkv_o[:, pl.ds(d + at, 2 * hw)]
        v = qkv_o[:, pl.ds(2 * d + at, 2 * hw)]
        outs = []
        tops = []
        for e in range(2):
            mine = (lane < hw) if e == 0 else (lane >= hw)
            spare = lane == hw * (1 - e)
            one = jnp.where(spare, 1.0, 0.0).astype(BF16)
            qm = jnp.where(mine, q, one)
            km = jnp.where(spare, bias, k)
            s = dot_nt(qm, km)
            top = jnp.max(s, axis=-1, keepdims=True)
            pr = jnp.exp2((s - top) * scale2).astype(BF16)
            vm = jnp.where(mine, v, jnp.ones_like(v))
            outs.append(dot_nn(pr, vm))
            tops.append(top)
        low = lane < hw
        total = pltpu.roll(jnp.where(low, outs[1], outs[0]), hw, 1)
        att_o[:, pl.ds(at, 2 * hw)] = (jnp.where(low, outs[0], outs[1]) / total).astype(BF16)
        log_total = jnp.log2(total) + scale2 * jnp.where(low, tops[0], tops[1])
        first = jnp.broadcast_to(log_total[:, 0:1], (rows, 128))
        second = jnp.broadcast_to(log_total[:, hw : hw + 1], (rows, 128))
        lse_s[...] = jnp.where(
            head_lane == 2 * p, first, jnp.where(head_lane == 2 * p + 1, second, lse_s[...])
        )
        return carry

    for p in range(HEADS // 2):
        pair(p, 0)
    lse_o[...] = jnp.transpose(lse_s[...])[0:16, :]
    saves[2].start()
    saves[3].start()
    branch = dot_nn(att_o[...], wproj[...]) + vec[4:5, :]
    for i in range(pieces):
        part = slice(i * rp, (i + 1) * rp)
        middle = xs[i][...].astype(F32) + branch[part, :]
        mid_o[part, :] = middle.astype(BF16)
        xhat, _ = norm_stats(middle)
        n2_o[part, :] = (xhat * vec[1:2, :] + vec[7:8, :]).astype(BF16)
    saves[4].start()
    saves[5].start()
    for save in saves:
        save.wait()


def attn_fwd(c, info, own, others, vec, wqkv, wproj, held):
    cpd, rp, d = own.shape
    pieces = 1 + len(others)
    rows = rp * pieces
    whole = lambda a: pl.BlockSpec(a.shape, lambda i, s: (0,) * a.ndim)
    at_clip = lambda shape: pl.BlockSpec((None,) + shape, lambda i, s: (c, 0, 0))
    shapes = [
        ((rows, d), BF16),
        ((rows, 3 * d), BF16),
        ((rows, d), BF16),
        ((16, rows), F32),
        ((rows, d), BF16),
        ((rows, d), BF16),
    ]
    in_specs = [at_clip((rp, d))] + [whole(o) for o in others] + [whole(vec), whole(wqkv), whole(wproj)]
    operands = [own, *others, vec, wqkv, wproj]
    aliases = {}
    if held is not None:
        aliases = {1 + len(operands) + i: i for i in range(6)}
        in_specs = in_specs + [pl.BlockSpec(memory_space=pl.ANY)] * 6
        operands = operands + list(held)
    return pl.pallas_call(
        functools.partial(attn_fwd_kernel, c, pieces),
        grid_spec=pltpu.PrefetchScalarGridSpec(
            num_scalar_prefetch=1,
            grid=(1,),
            in_specs=in_specs,
            out_specs=[pl.BlockSpec(memory_space=pl.ANY)] * len(shapes),
            scratch_shapes=[pltpu.VMEM(s, t) for s, t in shapes]
            + [pltpu.VMEM((rows, 128), F32), pltpu.SemaphoreType.DMA((len(shapes),))],
        ),
        out_shape=[jax.ShapeDtypeStruct((cpd,) + s, t) for s, t in shapes],
        input_output_aliases=aliases,
        compiler_params=pltpu.CompilerParams(vmem_limit_bytes=60 * MIB),
        cost_estimate=pl.CostEstimate(
            flops=2 * rows * d * 4 * d + 16 * HEADS * rows * rows * (d // HEADS),
            bytes_accessed=rows * d * 16 + 8 * d * d,
            transcendentals=HEADS * rows * rows,
        ),
        name="attn_fwd",
    )(info, *operands)


def mlp_fwd_kernel(pieces, info, mid, n2, vec, w1, b1, w2, *outs):
    h_o = outs[pieces]
    rows, d = n2.shape
    rp = rows // pieces
    full = info[1 + pl.program_id(0)] == 1
    ff = w1.shape[1]
    chunk = d
    x = n2[...]
    acc = mid[...].astype(F32) + vec[5:6, :]
    for j in range(ff // chunk):
        part = slice(j * chunk, (j + 1) * chunk)
        h = dot_nn(x, w1[:, part]) + b1[:, part]
        h_o[:, part] = h.astype(BF16)
        act = (h * (0.5 + 0.5 * lax.erf(h * 0.7071067811865476))).astype(BF16)
        acc = acc + dot_nn(act, w2[part, :])
    out = jnp.where(row_valid(rows, rp, full), acc, 0.0).astype(BF16)
    for i in range(pieces):
        outs[i][...] = out[i * rp : (i + 1) * rp, :]


def mlp_fwd(info, mid, n2, vec, w1, b1, w2, clips, pieces):
    cpd, rows, d = n2.shape
    ff = w1.shape[1]
    rp = rows // pieces
    by_clip = lambda w: pl.BlockSpec((None, rows, w), lambda c, s: (c, 0, 0))
    once = lambda a: pl.BlockSpec(a.shape, lambda c, s: (0, 0), pipeline_mode=pl.Buffered(1))
    return pl.pallas_call(
        functools.partial(mlp_fwd_kernel, pieces),
        grid_spec=pltpu.PrefetchScalarGridSpec(
            num_scalar_prefetch=1,
            grid=(cpd,),
            in_specs=[by_clip(d), by_clip(d), once(vec), once(w1), once(b1), once(w2)],
            out_specs=[pl.BlockSpec((None, rp, d), lambda c, s: (s[0] * cpd + c, 0, 0))]
            + [pl.BlockSpec((None, rp, d), lambda c, s: (c, 0, 0))] * (pieces - 1)
            + [by_clip(ff)],
        ),
        out_shape=[jax.ShapeDtypeStruct((clips, rp, d), BF16)]
        + [jax.ShapeDtypeStruct((cpd, rp, d), BF16)] * (pieces - 1)
        + [jax.ShapeDtypeStruct((cpd, rows, ff), BF16)],
        compiler_params=pltpu.CompilerParams(vmem_limit_bytes=60 * MIB),
        cost_estimate=pl.CostEstimate(
            flops=4 * cpd * rows * d * ff,
            bytes_accessed=cpd * rows * (8 * d + 2 * ff) + 4 * d * ff,
            transcendentals=cpd * rows * ff,
        ),
        name="mlp_fwd",
    )(info, mid, n2, vec, w1, b1, w2)


def upstream_of(cots, full):
    rp = cots[0].shape[0]
    keep = row_valid(rp, rp, full)
    return jnp.concatenate(
        [jnp.where(keep, c[...].astype(F32), 0.0) for c in cots], axis=0
    )


def mlp_back_kernel(pieces, cpd, info, *refs):
    cots = refs[:pieces]
    h, n2, mid, att, vec, w1_in, w2_in = refs[pieces : pieces + 7]
    dmid_o, sums_o, fc1_sums_o, keep2, send2, keep1, send1 = refs[pieces + 7 : pieces + 14]
    w1, w2, acc1, acc2, dn2_s, up_s, turned_s, stage1, stage2, sems_in, sems1, sems2 = refs[pieces + 14 :]
    r = pl.program_id(0)
    last = r == cpd - 1
    rows, d = mid.shape
    ff = w1.shape[1]
    chunk = d
    count = ff // chunk
    unit1 = keep1.shape[1]
    unit2 = keep2.shape[1]
    per2 = chunk // (2 * unit2)
    mine = info[1 + cpd]

    def cols_of(j):
        return pl.ds(pl.multiple_of(j * chunk, chunk), chunk)

    def loads(j):
        part = cols_of(j)
        return [
            pltpu.make_async_copy(w1_in.at[:, part], w1.at[:, part], sems_in.at[0, j]),
            pltpu.make_async_copy(w2_in.at[part], w2.at[part], sems_in.at[1, j]),
        ]

    def saves1(j, slot):
        cols = cols_of(j)
        return [
            pltpu.make_async_copy(stage1.at[slot, :, side], to.at[:, :, cols], sems1.at[slot, i])
            for i, (side, to) in enumerate(((mine, keep1), (1 - mine, send1)))
        ]

    def saves2(j, slot):
        at = pl.ds(j * per2, per2)
        return [
            pltpu.make_async_copy(stage2.at[slot, :, side], to.at[at], sems2.at[slot, i])
            for i, (side, to) in enumerate(((mine, keep2), (1 - mine, send2)))
        ]

    @pl.when(r == 0)
    def _():
        for j in range(count):
            for load in loads(j):
                load.start()
        acc1[...] = jnp.zeros_like(acc1)
        acc2[...] = jnp.zeros_like(acc2)
        sums_o[...] = jnp.zeros_like(sums_o)
        fc1_sums_o[...] = jnp.zeros_like(fc1_sums_o)

    up = upstream_of(cots, info[1 + r] == 1)
    up_s[...] = up.astype(BF16)
    sums_o[2:3, :] += jnp.sum(up, axis=0, keepdims=True)
    turned_s[...] = jnp.transpose(n2[...])
    dn2_s[...] = jnp.zeros_like(dn2_s)

    def one(j, carry):
        part = cols_of(j)

        @pl.when(r == 0)
        def _():
            for load in loads(j):
                load.wait()

        pre = h[:, part].astype(F32)
        cdf = 0.5 + 0.5 * lax.erf(pre * 0.7071067811865476)
        density = 0.3989422804014327 * jnp.exp2(pre * pre * (-0.5 * LOG2E))
        act = (pre * cdf).astype(BF16)
        grad = dot_nt(up_s[...], w2[part, :])
        dh = (grad * (cdf + pre * density)).astype(BF16)
        fc1_sums_o[0:1, part] += jnp.sum(dh.astype(F32), axis=0, keepdims=True)
        acc2[part, :] += dot_tn(act, up_s[...])
        dn2_s[...] += dot_nt(dh, w1[:, part])
        acc1[:, part] += dot_nn(turned_s[...], dh)

        @pl.when(last)
        def _():
            slot = j % 2

            @pl.when(j > 1)
            def _():
                for save in saves1(j - 2, slot) + saves2(j - 2, slot):
                    save.wait()

            stage2[slot] = acc2[part, :].astype(BF16).reshape(per2, 2, unit2, d)
            stage1[slot] = acc1[:, part].astype(BF16).reshape(d // (2 * unit1), 2, unit1, chunk)
            for save in saves1(j, slot) + saves2(j, slot):
                save.start()

        return carry

    lax.fori_loop(0, count, one, 0)
    dx, gain, shift = norm_back(dn2_s[...], mid[...].astype(F32), vec[1:2, :])
    dmid = (up_s[...].astype(F32) + dx).astype(BF16)
    dmid_o[...] = dmid
    sums_o[0:1, :] += gain
    sums_o[1:2, :] += shift
    acc1[:, ff : ff + d] += dot_tn(att[...], dmid)

    @pl.when(last)
    def _():
        for j in range(max(count - 2, 0), count):
            for save in saves1(j, j % 2) + saves2(j, j % 2):
                save.wait()
        stage1[0] = acc1[:, ff : ff + d].astype(BF16).reshape(d // (2 * unit1), 2, unit1, d)
        for save in saves1(count, 0):
            save.start()
        for save in saves1(count, 0):
            save.wait()


def mlp_back(info, cot, cot_others, h, n2, mid, att, vec, w1, w2, parts):
    clips, rp, d = cot.shape
    cpd, rows, ff = h.shape
    pieces = 1 + len(cot_others)
    unit1 = d // parts
    unit2 = ff // parts
    once = lambda a: pl.BlockSpec(a.shape, lambda c, s: (0, 0), pipeline_mode=pl.Buffered(1))
    held = lambda shape: pl.BlockSpec(shape, lambda c, s: (0, 0))
    by_clip = lambda w: pl.BlockSpec((None, rows, w), lambda c, s: (c, 0, 0))
    halves = [(d // (2 * unit1), unit1, ff + d), (ff // (2 * unit2), unit2, d)]
    return pl.pallas_call(
        functools.partial(mlp_back_kernel, pieces, cpd),
        grid_spec=pltpu.PrefetchScalarGridSpec(
            num_scalar_prefetch=1,
            grid=(cpd,),
            in_specs=[pl.BlockSpec((None, rp, d), lambda c, s: (s[0] * cpd + c, 0, 0))]
            + [pl.BlockSpec((None, rp, d), lambda c, s: (c, 0, 0))] * (pieces - 1)
            + [by_clip(ff), by_clip(d), by_clip(d), by_clip(d), once(vec)]
            + [pl.BlockSpec(memory_space=pl.ANY)] * 2,
            out_specs=[by_clip(d), held((8, d)), held((8, ff))]
            + [pl.BlockSpec(memory_space=pl.ANY)] * 4,
            scratch_shapes=[
                pltpu.VMEM(w1.shape, BF16),
                pltpu.VMEM(w2.shape, BF16),
                pltpu.VMEM((d, ff + d), F32),
                pltpu.VMEM((ff, d), F32),
                pltpu.VMEM((rows, d), F32),
                pltpu.VMEM((rows, d), BF16),
                pltpu.VMEM((d, rows), BF16),
                pltpu.VMEM((2, d // (2 * unit1), 2, unit1, d), BF16),
                pltpu.VMEM((2, d // (2 * unit2), 2, unit2, d), BF16),
                pltpu.SemaphoreType.DMA((2, ff // d)),
                pltpu.SemaphoreType.DMA((2, 2)),
                pltpu.SemaphoreType.DMA((2, 2)),
            ],
        ),
        out_shape=[
            jax.ShapeDtypeStruct((cpd, rows, d), BF16),
            jax.ShapeDtypeStruct((8, d), F32),
            jax.ShapeDtypeStruct((8, ff), F32),
        ]
        + [jax.ShapeDtypeStruct(halves[1], BF16)] * 2
        + [jax.ShapeDtypeStruct(halves[0], BF16)] * 2,
        compiler_params=pltpu.CompilerParams(vmem_limit_bytes=62 * MIB),
        cost_estimate=pl.CostEstimate(
            flops=8 * cpd * rows * d * ff,
            bytes_accessed=cpd * rows * (14 * d + 2 * ff) + 8 * d * ff,
            transcendentals=2 * cpd * rows * ff,
        ),
        name="mlp_back",
    )(info, cot, *cot_others, h, n2, mid, att, vec, w1, w2)


def attn_back_kernel(c, pieces, cpd, info, *refs):
    xs = refs[:pieces]
    keep, dmid, qkv, att, lse, vec, wqkv, wproj = refs[pieces : pieces + 8]
    dqkv_o, sums_o, gtok, do_s, delta_s, dqt_s, sems = refs[-7:]
    dqkv_out, sums_out, own_out, *others_out = refs[-9 - pieces : -7]
    rp, d = xs[0].shape
    rows = rp * pieces
    hw = d // HEADS
    full = info[1 + c] == 1
    targets = [(dqkv_o, dqkv_out.at[c]), (sums_o, sums_out.at[c])]
    targets += [(gtok.at[0], own_out.at[info[0] * cpd + c])]
    targets += [(gtok.at[1 + i], o) for i, o in enumerate(others_out)]
    saves = copies_of(targets, sems)
    low_mid = dmid[...]
    do_s[...] = dot_nt(low_mid, wproj[...]).astype(BF16)
    prod = (do_s[...].astype(F32) * att[...].astype(F32)).astype(BF16)
    head_of = lax.broadcasted_iota(jnp.int32, (16, d), 1) // hw
    select = (head_of == lax.broadcasted_iota(jnp.int32, (16, d), 0)).astype(BF16)
    delta_s[...] = dot_nt(select, prod)
    scale = hw**-0.5
    scale2 = scale * LOG2E
    bias = jnp.where(row_valid(rows, rp, full), 0.0, -1e30).astype(BF16)
    lane = lax.broadcasted_iota(jnp.int32, (1, 2 * hw), 1)

    def pair(p, carry):
        at = p * 2 * hw
        q = qkv[:, pl.ds(at, 2 * hw)]
        k = qkv[:, pl.ds(d + at, 2 * hw)]
        v = qkv[:, pl.ds(2 * d + at, 2 * hw)]
        do = do_s[:, pl.ds(at, 2 * hw)]
        kt = jnp.transpose(k)
        zero = jnp.zeros_like(q)
        dk = dv = None
        for e in range(2):
            mine = (lane < hw) if e == 0 else (lane >= hw)
            spare = lane == hw * (1 - e)
            one = jnp.where(spare, 1.0, 0.0).astype(BF16)
            qm = jnp.where(mine, q, one)
            km = jnp.where(spare, bias, k)
            st = dot_nt(km, qm)
            pt = jnp.exp2(st * scale2 - lse[pl.ds(2 * p + e, 1), :])
            vm = jnp.where(mine, v, zero)
            dpt = dot_nt(vm, do)
            dst = (pt * (dpt - delta_s[pl.ds(2 * p + e, 1), :])).astype(BF16)
            dom = jnp.where(mine, do, zero)
            qz = jnp.where(mine, q, zero)
            dv_e = dot_nn(pt.astype(BF16), dom)
            dk_e = dot_nn(dst, qz)
            dv = dv_e if dv is None else dv + dv_e
            dk = dk_e if dk is None else dk + dk_e
            dqt_s[pl.ds(at + e * hw, hw), :] = dot_nn(
                kt[e * hw : (e + 1) * hw, :], dst
            )
        dqkv_o[:, pl.ds(d + at, 2 * hw)] = (dk * scale).astype(BF16)
        dqkv_o[:, pl.ds(2 * d + at, 2 * hw)] = dv.astype(BF16)
        return carry

    for p in range(HEADS // 2):
        pair(p, 0)
    dqkv_o[:, 0:d] = jnp.transpose((dqt_s[...] * scale).astype(BF16))
    saves[0].start()
    dn1 = dot_nt(dqkv_o[...], wqkv[...])
    sums_o[...] = jnp.zeros_like(sums_o)
    sums_o[0:1, :] = jnp.sum(dqkv_o[:, 0:d].astype(F32), axis=0, keepdims=True)
    sums_o[1:2, :] = jnp.sum(dqkv_o[:, 2 * d : 3 * d].astype(F32), axis=0, keepdims=True)
    sums_o[2:3, :] = jnp.sum(low_mid.astype(F32), axis=0, keepdims=True)
    for i in range(pieces):
        part = slice(i * rp, (i + 1) * rp)
        dx, gain, shift = norm_back(dn1[part, :], xs[i][...].astype(F32), vec[0:1, :])
        entered = low_mid[part, :].astype(F32) + dx
        kept = entered * keep[part, :]
        gtok[i] = kept.astype(BF16)
        saves[2 + i].start()
        sums_o[3:4, :] += gain
        sums_o[4:5, :] += shift
        sums_o[5:6, :] += jnp.sum(entered - kept, axis=0, keepdims=True)
    saves[1].start()
    for save in saves:
        save.wait()


def attn_back(c, info, own, others, keep, dmid, qkv, att, lse, vec, wqkv, wproj, held, clips):
    cpd, rp, d = own.shape
    pieces = 1 + len(others)
    rows = rp * pieces
    whole = lambda a: pl.BlockSpec(a.shape, lambda i, s: (0,) * a.ndim)
    at_clip = lambda shape: pl.BlockSpec((None,) + shape, lambda i, s: (c, 0, 0))
    in_specs = (
        [at_clip((rp, d))]
        + [whole(o) for o in others]
        + [
            at_clip((rows, 1)),
            at_clip((rows, d)),
            at_clip((rows, 3 * d)),
            at_clip((rows, d)),
            at_clip((16, rows)),
            whole(vec),
            whole(wqkv),
            whole(wproj),
        ]
    )
    operands = [own, *others, keep, dmid, qkv, att, lse, vec, wqkv, wproj]
    aliases = {}
    if held is not None:
        aliases = {1 + len(operands) + i: i for i in range(3)}
        in_specs = in_specs + [pl.BlockSpec(memory_space=pl.ANY)] * 3
        operands = operands + list(held)
    return pl.pallas_call(
        functools.partial(attn_back_kernel, c, pieces, cpd),
        grid_spec=pltpu.PrefetchScalarGridSpec(
            num_scalar_prefetch=1,
            grid=(1,),
            in_specs=in_specs,
            out_specs=[pl.BlockSpec(memory_space=pl.ANY)] * (2 + pieces),
            scratch_shapes=[
                pltpu.VMEM((rows, 3 * d), BF16),
                pltpu.VMEM((8, d), F32),
                pltpu.VMEM((pieces, rp, d), BF16),
                pltpu.VMEM((rows, d), BF16),
                pltpu.VMEM((16, rows), F32),
                pltpu.VMEM((d, rows), F32),
                pltpu.SemaphoreType.DMA((2 + pieces,)),
            ],
        ),
        out_shape=[
            jax.ShapeDtypeStruct((cpd, rows, 3 * d), BF16),
            jax.ShapeDtypeStruct((cpd, 8, d), F32),
            jax.ShapeDtypeStruct((clips, rp, d), BF16),
        ]
        + [jax.ShapeDtypeStruct((rp, d), BF16)] * (pieces - 1),
        input_output_aliases=aliases,
        compiler_params=pltpu.CompilerParams(vmem_limit_bytes=60 * MIB),
        cost_estimate=pl.CostEstimate(
            flops=2 * rows * d * 4 * d + 40 * HEADS * rows * rows * (d // HEADS),
            bytes_accessed=rows * d * 28 + 8 * d * d,
            transcendentals=HEADS * rows * rows,
        ),
        name="attn_back",
    )(info, *operands)


def finish_kernel(cpd, narrow, cut, moved, info, *refs):
    n1, dqkv, one_sums, two_sums, small = refs[:5]
    moving = refs[7 : 7 + moved]
    keep_a, send_a, keep_b, send_b, out, tok = refs[7 + moved : 13 + moved]
    acc, turned_s, rows_s, stage, tail, sems, sems_move = refs[13 + moved : 20 + moved]
    held = refs[20 + moved :]
    r = pl.program_id(0)
    last = r == pl.num_programs(0) - 1
    d = turned_s.shape[0]
    rows = n1.shape[1]
    unit = keep_a.shape[1]
    piece = stage.shape[-1] // 3
    mine = info[1 + cpd]
    moves = []
    for k in range(1, narrow):
        rank = lax.rem(info[0] + k, narrow)
        moves.append((moving[k - 1], out.at[pl.ds(rank * cpd, cpd)]))
        for c in range(cpd - 1):
            moves.append((moving[(c + 1) * (narrow - 1) + k - 1], tok.at[rank * cpd + c]))
    order = [k - 1 for k in range(1, narrow)]
    order = [i for k in order for i in [k] + [(c + 1) * (narrow - 1) + k for c in range(cpd - 1)]]
    arrivals = copies_of([(moving[i], held[i]) for i in order], sems_move)
    moves = copies_of([(held[i], to) for i, (_, to) in zip(order, moves)], sems_move)

    groups = d // (2 * unit)
    per = n1.shape[0]

    @pl.when(r == 0)
    def _():
        for arrival in arrivals:
            arrival.start()
        acc[...] = jnp.zeros_like(acc)

    @pl.when(last)
    def _():
        for arrival in arrivals:
            arrival.wait()
        for move in moves:
            move.start()
        one_total = jnp.sum(one_sums[...], axis=0)
        rows_s[...] = jnp.zeros_like(rows_s)
        picked = [
            one_total[5:6, :],
            one_total[3:4, :],
            two_sums[0:1, :],
            one_total[0:1, :],
            one_total[1:2, :],
            one_total[2:3, :],
            two_sums[2:3, :],
            one_total[4:5, :],
            two_sums[1:2, :],
        ]
        for i, row in enumerate(picked):
            rows_s[i : i + 1, :] = row
        vectors = (jnp.transpose(rows_s[...]) + small[...]).astype(BF16)
        tail[...] = vectors.reshape(groups, 2, unit, rows_s.shape[0])

    for i in range(per):
        turned_s[:, i * rows : (i + 1) * rows] = jnp.transpose(n1[i])

    ends = [
        pltpu.make_async_copy(
            tail.at[:, side], half.at[:, :, pl.ds(3 * d - cut, rows_s.shape[0])], sems.at[9, i]
        )
        for i, (side, half) in enumerate(((mine, keep_b), (1 - mine, send_b)))
    ]

    def saves(j, sub, at, to):
        cols = pl.ds(sub * piece, piece)
        return [
            pltpu.make_async_copy(
                stage.at[j, :, side, :, cols], half.at[:, :, pl.ds(at, piece)], sems.at[3 * j + sub, i]
            )
            for i, (side, half) in enumerate(((mine, to[0]), (1 - mine, to[1])))
        ]

    for j in range(3):
        part = slice(j * d, (j + 1) * d)
        cols = jnp.concatenate([dqkv[i, :, part] for i in range(per)], axis=0)
        acc[:, part] += dot_nn(turned_s[...], cols)

        @pl.when(last)
        def _():
            stage[j] = acc[:, part].astype(BF16).reshape(groups, 2, unit, d)
            for sub in range(3):
                at = j * d + sub * piece
                to, at = ((keep_a, send_a), at) if at < cut else ((keep_b, send_b), at - cut)
                for save in saves(j, sub, at, to):
                    save.start()

    @pl.when(last)
    def _():
        for end in ends:
            end.start()
        for j in range(3):
            for sub in range(3):
                at = j * d + sub * piece
                to, at = ((keep_a, send_a), at) if at < cut else ((keep_b, send_b), at - cut)
                for save in saves(j, sub, at, to):
                    save.wait()
        for end in ends:
            end.wait()
        for move in moves:
            move.wait()


def finish(info, n1, dqkv, one_sums, two_sums, small, out, out_back, tok, tok_back, parts):
    cpd, rows, d = n1.shape
    width = dqkv.shape[2]
    narrow = 1 + len(out_back)
    unit = d // parts
    piece = d // 3
    cut = 5 * piece
    groups = d // (2 * unit)
    per = 2 if cpd % 2 == 0 else 1
    moving = list(out_back) + [t for back in tok_back[: cpd - 1] for t in back]
    held = lambda a: pl.BlockSpec(a.shape, lambda c, s: (0,) * a.ndim)
    anywhere = pl.BlockSpec(memory_space=pl.ANY)
    half = lambda cols: jax.ShapeDtypeStruct((groups, unit, cols), BF16)
    lanes = small.shape[1]
    return pl.pallas_call(
        functools.partial(finish_kernel, cpd, narrow, cut, len(moving)),
        grid_spec=pltpu.PrefetchScalarGridSpec(
            num_scalar_prefetch=1,
            grid=(cpd // per,),
            in_specs=[
                pl.BlockSpec((per, rows, d), lambda c, s: (c, 0, 0)),
                pl.BlockSpec((per, rows, width), lambda c, s: (c, 0, 0)),
                held(one_sums),
                held(two_sums),
                held(small),
            ]
            + [anywhere] * (2 + len(moving)),
            out_specs=[anywhere] * 6,
            scratch_shapes=[
                pltpu.VMEM((d, width), F32),
                pltpu.VMEM((d, per * rows), BF16),
                pltpu.VMEM((lanes, d), F32),
                pltpu.VMEM((3, groups, 2, unit, d), BF16),
                pltpu.VMEM((groups, 2, unit, lanes), BF16),
                pltpu.SemaphoreType.DMA((10, 2)),
                pltpu.SemaphoreType.DMA((max(len(moving), 1),)),
            ]
            + [pltpu.VMEM(m.shape, BF16) for m in moving],
        ),
        out_shape=[half(cut), half(cut), half(width - cut + lanes), half(width - cut + lanes)]
        + [jax.ShapeDtypeStruct(out.shape, BF16), jax.ShapeDtypeStruct(tok.shape, BF16)],
        input_output_aliases={6: 4, 7: 5},
        compiler_params=pltpu.CompilerParams(vmem_limit_bytes=60 * MIB),
        cost_estimate=pl.CostEstimate(
            flops=2 * cpd * rows * d * width,
            bytes_accessed=2 * (cpd * rows * (d + width) + d * width),
            transcendentals=0,
        ),
        name="finish",
    )(info, n1, dqkv, one_sums, two_sums, small, out, tok, *moving)


class ScatterSum:
    def __init__(self, keep, send, wide, narrow, first=(("wide", 0),)):
        rows, cols = 2 * keep.shape[0] * keep.shape[1], keep.shape[2]
        self.block = (rows // (wide * narrow), cols)
        bits_w, bits_n = wide.bit_length() - 1, narrow.bit_length() - 1
        order = [("wide", b, bits_w - 1 - b, wide) for b in range(bits_w)]
        order += [("narrow", b, bits_w + bits_n - 1 - b, narrow) for b in range(bits_n)]
        ahead = [o for key in first for o in order if o[:2] == key]
        self.order = ahead + [o for o in order if o not in ahead]
        axis, bit, dim, size = self.order.pop(0)
        shape = [2] * (bits_w + bits_n)
        shape[dim] = 1
        self.sums = None
        self.keep = keep.reshape(tuple(shape) + self.block)
        self.exchange(send.reshape(self.keep.shape), axis, bit, size)

    def exchange(self, sent, axis, bit, size):
        self.sent = sent
        self.got = lax.ppermute(sent, axis, [(i, i ^ (1 << bit)) for i in range(size)])

    def step(self, behind=None):
        if self.sums is not None:
            return self.sums
        keep, got = self.keep, self.got
        if behind is not None:
            keep = after(keep, behind)
        if not self.order:
            self.sums = keep.astype(F32) + got.astype(F32)
            return self.sums
        axis, bit, dim, size = self.order.pop(0)
        mine = (lax.axis_index(axis) >> bit) & 1

        def part(at):
            pieces = [lax.dynamic_slice_in_dim(x, at, 1, dim).astype(F32) for x in (keep, got)]
            return (pieces[0] + pieces[1]).astype(BF16)

        self.exchange(part(1 - mine), axis, bit, size)
        self.keep = part(mine)
        return self.sent

    def finish(self, behind=None):
        while self.sums is None:
            self.step(behind)
        return self.sums.reshape(self.block)


def after(value, *others):
    return lax.optimization_barrier((value, others))[0]


def body(
    wide,
    narrow,
    tokens,
    masked,
    resolution,
    mask_embed,
    gains,
    biases,
    w_qkv,
    w_proj,
    w_fc1,
    fc1_bias,
    w_fc2,
    cotangent,
):
    clips, freq_rows, cols, d = tokens.shape
    rp = freq_rows * cols
    cpd = clips // narrow
    rows = rp * narrow
    ff = w_fc1.shape[1]
    me = lax.axis_index("narrow")
    flat_tokens = tokens.reshape(clips, rp, d)
    flat_cot = cotangent.reshape(clips, rp, d)
    is_masked = masked.reshape(clips, rp) == 1

    def block_of(array, rank, at, count):
        return lax.dynamic_slice_in_dim(array, rank * cpd + at, count, 0)

    def entered_of(rank, at, count):
        return jnp.where(
            block_of(is_masked, rank, at, count)[:, :, None],
            mask_embed[None, None, :],
            block_of(flat_tokens, rank, at, count),
        )

    def to_rank(array, k):
        return lax.ppermute(array, "narrow", [(i, (i + k) % narrow) for i in range(narrow)])

    def from_rank(array, k):
        return lax.ppermute(array, "narrow", [(i, (i - k) % narrow) for i in range(narrow)])

    core = lax.axis_index("wide") & 1
    info = jnp.concatenate([me[None], block_of(resolution, me, 0, cpd), core[None]])
    vec = jnp.concatenate([gains.astype(F32).T, biases.astype(F32).T], axis=0)
    bias_row = fc1_bias.astype(F32)[None, :]

    shifts = range(1, narrow)
    others = []
    for c in range(cpd):
        send = [entered_of((me + k) % narrow, c, 1)[0] for k in shifts]
        if c > 0:
            send = after(send, others[-1])
        others.append([to_rank(send[k - 1], k) for k in shifts])
    keep_sent = [block_of(masked.reshape(clips, rp), (me + k) % narrow, 0, cpd) for k in shifts]
    keep_sent = after(keep_sent, others[0])
    keep_cols = [block_of(masked.reshape(clips, rp), me, 0, cpd)]
    keep_cols += [to_rank(keep_sent[k - 1], k) for k in shifts]
    keep = (jnp.concatenate(keep_cols, axis=1) != 1).astype(F32)[:, :, None]
    own = entered_of(me, 0, cpd)
    cot_send = [block_of(flat_cot, (me + k) % narrow, 0, cpd) for k in shifts]

    held = None
    for c in range(cpd):
        here = after(info, keep) if c == 1 else info
        held = attn_fwd(c, here, own, others[c], vec, w_qkv, w_proj, held)
    cot_send = after(cot_send, others[-1])
    cot_others = [to_rank(cot_send[k - 1], k) for k in shifts]
    n1, qkv, att, lse, mid, n2 = held

    out, *rest = mlp_fwd(info, mid, n2, vec, w_fc1, bias_row, w_fc2, clips, narrow)
    out_others, h = rest[:-1], rest[-1]
    out_back = [from_rank(out_others[k - 1], k) for k in shifts]

    dmid, two_sums, fc1_sums, *halves = mlp_back(
        info, flat_cot, cot_others, h, n2, mid, att, vec, w_fc1, w_fc2, wide
    )
    z_first = (("wide", 0), ("wide", 2), ("wide", 1), ("narrow", 0))
    fc2_chain = ScatterSum(*halves[:2], wide, narrow)
    fc1_chain = ScatterSum(*halves[2:], wide, narrow, z_first)
    small = fc1_sums[0].reshape(d, ff // d)
    small = jnp.pad(small, ((0, 0), (9, 119 - small.shape[1])))

    held = None
    tok_back = []
    for c in range(cpd):
        behind = held[1] if c > 0 else two_sums
        ready = [fc2_chain.step(behind), fc1_chain.step(behind)] if c in (1, 3) else []
        if False:
            ready.append(out_back)
        if c > 1:
            tok_back[c - 2] = after(tok_back[c - 2], behind)
            ready.append(tok_back[c - 2])
        here = after(info, *ready)
        *held, = attn_back(
            c, here, own, others[c], keep, dmid, qkv, att, lse, vec, w_qkv, w_proj, held, clips
        )
        tok_back.append([from_rank(g, k) for k, g in zip(shifts, held[3:])])
        held = held[:3]
    dqkv, one_sums, grad_tokens = held
    n1 = after(n1, fc2_chain.step(one_sums), fc1_chain.step(one_sums))
    *halves, out, grad_tokens = finish(
        info, n1, dqkv, one_sums, two_sums, small, out, out_back, grad_tokens, tok_back, wide
    )
    chains = [
        ScatterSum(*halves[:2], wide, narrow),
        ScatterSum(*halves[2:], wide, narrow, z_first),
    ]
    sent = [chain.step(halves[0]) for chain in (fc2_chain, fc1_chain)]
    sent = [chain.step(sent) for chain in chains]
    sent = [chain.step(sent) for chain in chains]
    grad_fc2 = fc2_chain.finish(sent)
    fc1_proj = fc1_chain.finish(sent)
    grad_fc1, grad_proj = fc1_proj[:, :ff], fc1_proj[:, ff:]
    for k in shifts:
        rank = (me + k) % narrow
        returned = after(tok_back[-1][k - 1], sent)
        grad_tokens = lax.dynamic_update_slice_in_dim(
            grad_tokens, returned[None], rank * cpd + cpd - 1, 0
        )
    while any(chain.sums is None for chain in chains):
        sent = [chain.step(sent) for chain in chains]
    last = jnp.concatenate([chain.finish() for chain in chains], axis=1)
    grad_qkv = last[:, : 3 * d]
    vectors = last[:, 3 * d :]
    return (
        out.reshape(tokens.shape),
        grad_tokens.reshape(tokens.shape),
        vectors[:, 0],
        vectors[:, 1:3],
        vectors[:, 3:9],
        grad_qkv,
        grad_proj,
        grad_fc1,
        vectors[:, 9 : 9 + ff // d].reshape(-1),
        grad_fc2,
    )


def solution(mesh):
    split = P("wide", None, "narrow", None)
    every = P(("wide", "narrow"))
    rows = P(("wide", "narrow"), None)
    return jax.shard_map(
        functools.partial(body, mesh.shape["wide"], mesh.shape["narrow"]),
        mesh=mesh,
        in_specs=(split, P("wide", None, "narrow"), P("wide")) + (P(),) * 8 + (split,),
        out_specs=(split, split, every, rows, rows, rows, rows, rows, every, rows),
        check_vma=False,
    )
```

```python
import functools

import jax
import jax.numpy as jnp
from jax import lax
from jax.experimental import pallas as pl
from jax.experimental.pallas import tpu as pltpu
from jax.sharding import PartitionSpec as P

HEADS = 12
EPS = 1e-06
LOG2E = 1.4426950408889634
F32 = jnp.float32
BF16 = jnp.bfloat16
MIB = 1 << 20


def dot_nn(a, b):
    return jnp.dot(a, b, preferred_element_type=F32)


def dot_nt(a, b):
    return lax.dot_general(a, b, (((1,), (1,)), ((), ())), preferred_element_type=F32)


def dot_tn(a, b):
    return lax.dot_general(a, b, (((0,), (0,)), ((), ())), preferred_element_type=F32)


def norm_stats(x):
    centred = x - jnp.mean(x, axis=-1, keepdims=True)
    rstd = lax.rsqrt(jnp.mean(centred * centred, axis=-1, keepdims=True) + EPS)
    return centred * rstd, rstd


def norm_back(grad, x, gain):
    xhat, rstd = norm_stats(x)
    scaled = grad * gain
    inner = jnp.mean(scaled * xhat, axis=-1, keepdims=True)
    outer = jnp.mean(scaled, axis=-1, keepdims=True)
    dx = rstd * (scaled - outer - xhat * inner)
    return dx, jnp.sum(grad * xhat, axis=0, keepdims=True), jnp.sum(grad, axis=0, keepdims=True)


def copies_of(pairs, sems):
    return [pltpu.make_async_copy(a, b, sems.at[i]) for i, (a, b) in enumerate(pairs)]


def row_valid(rows, piece_rows, full):
    at = lax.broadcasted_iota(jnp.int32, (rows, 1), 0) % piece_rows
    return (at < piece_rows // 2) | full


def attn_fwd_kernel(c, pieces, info, *refs):
    xs = refs[:pieces]
    vec, wqkv, wproj = refs[pieces : pieces + 3]
    made = refs[-8:-2]
    n1_o, qkv_o, att_o, lse_o, mid_o, n2_o = made
    lse_s, sems = refs[-2:]
    saves = copies_of([(m, o.at[c]) for m, o in zip(made, refs[-14:-8])], sems)
    rp, d = xs[0].shape
    rows = rp * pieces
    hw = d // HEADS
    full = info[1 + c] == 1
    for i in range(pieces):
        xhat, _ = norm_stats(xs[i][...].astype(F32))
        n1_o[i * rp : (i + 1) * rp, :] = (xhat * vec[0:1, :] + vec[6:7, :]).astype(BF16)
    saves[0].start()
    n1 = n1_o[...]
    qkv_o[:, 0:d] = (dot_nn(n1, wqkv[:, 0:d]) + vec[2:3, :]).astype(BF16)
    qkv_o[:, d : 2 * d] = dot_nn(n1, wqkv[:, d : 2 * d]).astype(BF16)
    qkv_o[:, 2 * d : 3 * d] = (dot_nn(n1, wqkv[:, 2 * d : 3 * d]) + vec[3:4, :]).astype(BF16)
    saves[1].start()
    scale2 = hw**-0.5 * LOG2E
    bias = jnp.where(row_valid(rows, rp, full), 0.0, -1e30).astype(BF16)
    lane = lax.broadcasted_iota(jnp.int32, (1, 2 * hw), 1)
    head_lane = lax.broadcasted_iota(jnp.int32, (1, 128), 1)
    lse_s[...] = jnp.zeros_like(lse_s)

    def pair(p, carry):
        at = p * 2 * hw
        q = qkv_o[:, pl.ds(at, 2 * hw)]
        k = qkv_o[:, pl.ds(d + at, 2 * hw)]
        v = qkv_o[:, pl.ds(2 * d + at, 2 * hw)]
        outs = []
        tops = []
        for e in range(2):
            mine = (lane < hw) if e == 0 else (lane >= hw)
            spare = lane == hw * (1 - e)
            one = jnp.where(spare, 1.0, 0.0).astype(BF16)
            qm = jnp.where(mine, q, one)
            km = jnp.where(spare, bias, k)
            s = dot_nt(qm, km)
            top = jnp.max(s, axis=-1, keepdims=True)
            pr = jnp.exp2((s - top) * scale2).astype(BF16)
            vm = jnp.where(mine, v, jnp.ones_like(v))
            outs.append(dot_nn(pr, vm))
            tops.append(top)
        low = lane < hw
        total = pltpu.roll(jnp.where(low, outs[1], outs[0]), hw, 1)
        att_o[:, pl.ds(at, 2 * hw)] = (jnp.where(low, outs[0], outs[1]) / total).astype(BF16)
        log_total = jnp.log2(total) + scale2 * jnp.where(low, tops[0], tops[1])
        first = jnp.broadcast_to(log_total[:, 0:1], (rows, 128))
        second = jnp.broadcast_to(log_total[:, hw : hw + 1], (rows, 128))
        lse_s[...] = jnp.where(
            head_lane == 2 * p, first, jnp.where(head_lane == 2 * p + 1, second, lse_s[...])
        )
        return carry

    for p in range(HEADS // 2):
        pair(p, 0)
    lse_o[...] = jnp.transpose(lse_s[...])[0:16, :]
    saves[2].start()
    saves[3].start()
    branch = dot_nn(att_o[...], wproj[...]) + vec[4:5, :]
    for i in range(pieces):
        part = slice(i * rp, (i + 1) * rp)
        middle = xs[i][...].astype(F32) + branch[part, :]
        mid_o[part, :] = middle.astype(BF16)
        xhat, _ = norm_stats(middle)
        n2_o[part, :] = (xhat * vec[1:2, :] + vec[7:8, :]).astype(BF16)
    saves[4].start()
    saves[5].start()
    for save in saves:
        save.wait()


def attn_fwd(c, info, own, others, vec, wqkv, wproj, held):
    cpd, rp, d = own.shape
    pieces = 1 + len(others)
    rows = rp * pieces
    whole = lambda a: pl.BlockSpec(a.shape, lambda i, s: (0,) * a.ndim)
    at_clip = lambda shape: pl.BlockSpec((None,) + shape, lambda i, s: (c, 0, 0))
    shapes = [
        ((rows, d), BF16),
        ((rows, 3 * d), BF16),
        ((rows, d), BF16),
        ((16, rows), F32),
        ((rows, d), BF16),
        ((rows, d), BF16),
    ]
    in_specs = [at_clip((rp, d))] + [whole(o) for o in others] + [whole(vec), whole(wqkv), whole(wproj)]
    operands = [own, *others, vec, wqkv, wproj]
    aliases = {}
    if held is not None:
        aliases = {1 + len(operands) + i: i for i in range(6)}
        in_specs = in_specs + [pl.BlockSpec(memory_space=pl.ANY)] * 6
        operands = operands + list(held)
    return pl.pallas_call(
        functools.partial(attn_fwd_kernel, c, pieces),
        grid_spec=pltpu.PrefetchScalarGridSpec(
            num_scalar_prefetch=1,
            grid=(1,),
            in_specs=in_specs,
            out_specs=[pl.BlockSpec(memory_space=pl.ANY)] * len(shapes),
            scratch_shapes=[pltpu.VMEM(s, t) for s, t in shapes]
            + [pltpu.VMEM((rows, 128), F32), pltpu.SemaphoreType.DMA((len(shapes),))],
        ),
        out_shape=[jax.ShapeDtypeStruct((cpd,) + s, t) for s, t in shapes],
        input_output_aliases=aliases,
        compiler_params=pltpu.CompilerParams(vmem_limit_bytes=60 * MIB),
        cost_estimate=pl.CostEstimate(
            flops=2 * rows * d * 4 * d + 16 * HEADS * rows * rows * (d // HEADS),
            bytes_accessed=rows * d * 16 + 8 * d * d,
            transcendentals=HEADS * rows * rows,
        ),
        name="attn_fwd",
    )(info, *operands)


def mlp_fwd_kernel(pieces, info, mid, n2, vec, w1, b1, w2, *outs):
    h_o = outs[pieces]
    rows, d = n2.shape
    rp = rows // pieces
    full = info[1 + pl.program_id(0)] == 1
    ff = w1.shape[1]
    chunk = d
    x = n2[...]
    acc = mid[...].astype(F32) + vec[5:6, :]
    for j in range(ff // chunk):
        part = slice(j * chunk, (j + 1) * chunk)
        h = dot_nn(x, w1[:, part]) + b1[:, part]
        h_o[:, part] = h.astype(BF16)
        act = (h * (0.5 + 0.5 * lax.erf(h * 0.7071067811865476))).astype(BF16)
        acc = acc + dot_nn(act, w2[part, :])
    out = jnp.where(row_valid(rows, rp, full), acc, 0.0).astype(BF16)
    for i in range(pieces):
        outs[i][...] = out[i * rp : (i + 1) * rp, :]


def mlp_fwd(info, mid, n2, vec, w1, b1, w2, clips, pieces):
    cpd, rows, d = n2.shape
    ff = w1.shape[1]
    rp = rows // pieces
    by_clip = lambda w: pl.BlockSpec((None, rows, w), lambda c, s: (c, 0, 0))
    once = lambda a: pl.BlockSpec(a.shape, lambda c, s: (0, 0), pipeline_mode=pl.Buffered(1))
    return pl.pallas_call(
        functools.partial(mlp_fwd_kernel, pieces),
        grid_spec=pltpu.PrefetchScalarGridSpec(
            num_scalar_prefetch=1,
            grid=(cpd,),
            in_specs=[by_clip(d), by_clip(d), once(vec), once(w1), once(b1), once(w2)],
            out_specs=[pl.BlockSpec((None, rp, d), lambda c, s: (s[0] * cpd + c, 0, 0))]
            + [pl.BlockSpec((None, rp, d), lambda c, s: (c, 0, 0))] * (pieces - 1)
            + [by_clip(ff)],
        ),
        out_shape=[jax.ShapeDtypeStruct((clips, rp, d), BF16)]
        + [jax.ShapeDtypeStruct((cpd, rp, d), BF16)] * (pieces - 1)
        + [jax.ShapeDtypeStruct((cpd, rows, ff), BF16)],
        compiler_params=pltpu.CompilerParams(vmem_limit_bytes=60 * MIB),
        cost_estimate=pl.CostEstimate(
            flops=4 * cpd * rows * d * ff,
            bytes_accessed=cpd * rows * (8 * d + 2 * ff) + 4 * d * ff,
            transcendentals=cpd * rows * ff,
        ),
        name="mlp_fwd",
    )(info, mid, n2, vec, w1, b1, w2)


def upstream_of(cots, full):
    rp = cots[0].shape[0]
    keep = row_valid(rp, rp, full)
    return jnp.concatenate(
        [jnp.where(keep, c[...].astype(F32), 0.0) for c in cots], axis=0
    )


def mlp_back_kernel(pieces, cpd, info, *refs):
    cots = refs[:pieces]
    h, n2, mid, att, vec, w1_in, w2_in = refs[pieces : pieces + 7]
    dmid_o, sums_o, fc1_sums_o, keep2, send2, keep1, send1 = refs[pieces + 7 : pieces + 14]
    w1, w2, acc1, acc2, dn2_s, up_s, turned_s, stage1, stage2, sems_in, sems1, sems2 = refs[pieces + 14 :]
    r = pl.program_id(0)
    last = r == cpd - 1
    rows, d = mid.shape
    ff = w1.shape[1]
    chunk = d
    count = ff // chunk
    unit1 = keep1.shape[1]
    unit2 = keep2.shape[1]
    per2 = chunk // (2 * unit2)
    mine = info[1 + cpd]

    def cols_of(j):
        return pl.ds(pl.multiple_of(j * chunk, chunk), chunk)

    def loads(j):
        part = cols_of(j)
        return [
            pltpu.make_async_copy(w1_in.at[:, part], w1.at[:, part], sems_in.at[0, j]),
            pltpu.make_async_copy(w2_in.at[part], w2.at[part], sems_in.at[1, j]),
        ]

    def saves1(j, slot):
        cols = cols_of(j)
        return [
            pltpu.make_async_copy(stage1.at[slot, :, side], to.at[:, :, cols], sems1.at[slot, i])
            for i, (side, to) in enumerate(((mine, keep1), (1 - mine, send1)))
        ]

    def saves2(j, slot):
        at = pl.ds(j * per2, per2)
        return [
            pltpu.make_async_copy(stage2.at[slot, :, side], to.at[at], sems2.at[slot, i])
            for i, (side, to) in enumerate(((mine, keep2), (1 - mine, send2)))
        ]

    @pl.when(r == 0)
    def _():
        for j in range(count):
            for load in loads(j):
                load.start()
        acc1[...] = jnp.zeros_like(acc1)
        acc2[...] = jnp.zeros_like(acc2)
        sums_o[...] = jnp.zeros_like(sums_o)
        fc1_sums_o[...] = jnp.zeros_like(fc1_sums_o)

    up = upstream_of(cots, info[1 + r] == 1)
    up_s[...] = up.astype(BF16)
    sums_o[2:3, :] += jnp.sum(up, axis=0, keepdims=True)
    turned_s[...] = jnp.transpose(n2[...])
    dn2_s[...] = jnp.zeros_like(dn2_s)

    def one(j, carry):
        part = cols_of(j)

        @pl.when(r == 0)
        def _():
            for load in loads(j):
                load.wait()

        pre = h[:, part].astype(F32)
        cdf = 0.5 + 0.5 * lax.erf(pre * 0.7071067811865476)
        density = 0.3989422804014327 * jnp.exp2(pre * pre * (-0.5 * LOG2E))
        act = (pre * cdf).astype(BF16)
        grad = dot_nt(up_s[...], w2[part, :])
        dh = (grad * (cdf + pre * density)).astype(BF16)
        fc1_sums_o[0:1, part] += jnp.sum(dh.astype(F32), axis=0, keepdims=True)
        acc2[part, :] += dot_tn(act, up_s[...])
        dn2_s[...] += dot_nt(dh, w1[:, part])
        acc1[:, part] += dot_nn(turned_s[...], dh)

        @pl.when(last)
        def _():
            slot = j % 2

            @pl.when(j > 1)
            def _():
                for save in saves1(j - 2, slot) + saves2(j - 2, slot):
                    save.wait()

            stage2[slot] = acc2[part, :].astype(BF16).reshape(per2, 2, unit2, d)
            stage1[slot] = acc1[:, part].astype(BF16).reshape(d // (2 * unit1), 2, unit1, chunk)
            for save in saves1(j, slot) + saves2(j, slot):
                save.start()

        return carry

    lax.fori_loop(0, count, one, 0)
    dx, gain, shift = norm_back(dn2_s[...], mid[...].astype(F32), vec[1:2, :])
    dmid = (up_s[...].astype(F32) + dx).astype(BF16)
    dmid_o[...] = dmid
    sums_o[0:1, :] += gain
    sums_o[1:2, :] += shift
    acc1[:, ff : ff + d] += dot_tn(att[...], dmid)

    @pl.when(last)
    def _():
        for j in range(max(count - 2, 0), count):
            for save in saves1(j, j % 2) + saves2(j, j % 2):
                save.wait()
        stage1[0] = acc1[:, ff : ff + d].astype(BF16).reshape(d // (2 * unit1), 2, unit1, d)
        for save in saves1(count, 0):
            save.start()
        for save in saves1(count, 0):
            save.wait()


def mlp_back(info, cot, cot_others, h, n2, mid, att, vec, w1, w2, parts):
    clips, rp, d = cot.shape
    cpd, rows, ff = h.shape
    pieces = 1 + len(cot_others)
    unit1 = d // parts
    unit2 = ff // parts
    once = lambda a: pl.BlockSpec(a.shape, lambda c, s: (0, 0), pipeline_mode=pl.Buffered(1))
    held = lambda shape: pl.BlockSpec(shape, lambda c, s: (0, 0))
    by_clip = lambda w: pl.BlockSpec((None, rows, w), lambda c, s: (c, 0, 0))
    halves = [(d // (2 * unit1), unit1, ff + d), (ff // (2 * unit2), unit2, d)]
    return pl.pallas_call(
        functools.partial(mlp_back_kernel, pieces, cpd),
        grid_spec=pltpu.PrefetchScalarGridSpec(
            num_scalar_prefetch=1,
            grid=(cpd,),
            in_specs=[pl.BlockSpec((None, rp, d), lambda c, s: (s[0] * cpd + c, 0, 0))]
            + [pl.BlockSpec((None, rp, d), lambda c, s: (c, 0, 0))] * (pieces - 1)
            + [by_clip(ff), by_clip(d), by_clip(d), by_clip(d), once(vec)]
            + [pl.BlockSpec(memory_space=pl.ANY)] * 2,
            out_specs=[by_clip(d), held((8, d)), held((8, ff))]
            + [pl.BlockSpec(memory_space=pl.ANY)] * 4,
            scratch_shapes=[
                pltpu.VMEM(w1.shape, BF16),
                pltpu.VMEM(w2.shape, BF16),
                pltpu.VMEM((d, ff + d), F32),
                pltpu.VMEM((ff, d), F32),
                pltpu.VMEM((rows, d), F32),
                pltpu.VMEM((rows, d), BF16),
                pltpu.VMEM((d, rows), BF16),
                pltpu.VMEM((2, d // (2 * unit1), 2, unit1, d), BF16),
                pltpu.VMEM((2, d // (2 * unit2), 2, unit2, d), BF16),
                pltpu.SemaphoreType.DMA((2, ff // d)),
                pltpu.SemaphoreType.DMA((2, 2)),
                pltpu.SemaphoreType.DMA((2, 2)),
            ],
        ),
        out_shape=[
            jax.ShapeDtypeStruct((cpd, rows, d), BF16),
            jax.ShapeDtypeStruct((8, d), F32),
            jax.ShapeDtypeStruct((8, ff), F32),
        ]
        + [jax.ShapeDtypeStruct(halves[1], BF16)] * 2
        + [jax.ShapeDtypeStruct(halves[0], BF16)] * 2,
        compiler_params=pltpu.CompilerParams(vmem_limit_bytes=62 * MIB),
        cost_estimate=pl.CostEstimate(
            flops=8 * cpd * rows * d * ff,
            bytes_accessed=cpd * rows * (14 * d + 2 * ff) + 8 * d * ff,
            transcendentals=2 * cpd * rows * ff,
        ),
        name="mlp_back",
    )(info, cot, *cot_others, h, n2, mid, att, vec, w1, w2)


def attn_back_kernel(c, pieces, cpd, info, *refs):
    xs = refs[:pieces]
    keep, dmid, qkv, att, lse, vec, wqkv_in, wproj = refs[pieces : pieces + 8]
    dqkv_o, sums_o, gtok, do_s, delta_s, dqt_s, x_s, wqkv, sems, sems_in = refs[-10:]
    dqkv_out, sums_out, own_out, *others_out = refs[-12 - pieces : -10]
    rp, d = x_s.shape[1:]
    sources = [(wqkv_in, wqkv), (xs[0].at[c], x_s.at[0])]
    sources += [(x, x_s.at[1 + i]) for i, x in enumerate(xs[1:])]
    loads = copies_of(sources, sems_in)
    for load in loads:
        load.start()
    rows = rp * pieces
    hw = d // HEADS
    full = info[1 + c] == 1
    targets = [(dqkv_o, dqkv_out.at[c]), (sums_o, sums_out.at[c])]
    targets += [(gtok.at[0], own_out.at[info[0] * cpd + c])]
    targets += [(gtok.at[1 + i], o) for i, o in enumerate(others_out)]
    saves = copies_of(targets, sems)
    low_mid = dmid[...]
    do_s[...] = dot_nt(low_mid, wproj[...]).astype(BF16)
    prod = (do_s[...].astype(F32) * att[...].astype(F32)).astype(BF16)
    head_of = lax.broadcasted_iota(jnp.int32, (16, d), 1) // hw
    select = (head_of == lax.broadcasted_iota(jnp.int32, (16, d), 0)).astype(BF16)
    delta_s[...] = dot_nt(select, prod)
    scale = hw**-0.5
    scale2 = scale * LOG2E
    bias = jnp.where(row_valid(rows, rp, full), 0.0, -1e30).astype(BF16)
    lane = lax.broadcasted_iota(jnp.int32, (1, 2 * hw), 1)

    def pair(p, carry):
        at = p * 2 * hw
        q = qkv[:, pl.ds(at, 2 * hw)]
        k = qkv[:, pl.ds(d + at, 2 * hw)]
        v = qkv[:, pl.ds(2 * d + at, 2 * hw)]
        do = do_s[:, pl.ds(at, 2 * hw)]
        kt = jnp.transpose(k)
        zero = jnp.zeros_like(q)
        dk = dv = None
        for e in range(2):
            mine = (lane < hw) if e == 0 else (lane >= hw)
            spare = lane == hw * (1 - e)
            one = jnp.where(spare, 1.0, 0.0).astype(BF16)
            qm = jnp.where(mine, q, one)
            km = jnp.where(spare, bias, k)
            st = dot_nt(km, qm)
            pt = jnp.exp2(st * scale2 - lse[pl.ds(2 * p + e, 1), :])
            vm = jnp.where(mine, v, zero)
            dpt = dot_nt(vm, do)
            dst = (pt * (dpt - delta_s[pl.ds(2 * p + e, 1), :])).astype(BF16)
            dom = jnp.where(mine, do, zero)
            qz = jnp.where(mine, q, zero)
            dv_e = dot_nn(pt.astype(BF16), dom)
            dk_e = dot_nn(dst, qz)
            dv = dv_e if dv is None else dv + dv_e
            dk = dk_e if dk is None else dk + dk_e
            dqt_s[pl.ds(at + e * hw, hw), :] = dot_nn(
                kt[e * hw : (e + 1) * hw, :], dst
            )
        dqkv_o[:, pl.ds(d + at, 2 * hw)] = (dk * scale).astype(BF16)
        dqkv_o[:, pl.ds(2 * d + at, 2 * hw)] = dv.astype(BF16)
        return carry

    for p in range(HEADS // 2):
        pair(p, 0)
    dqkv_o[:, 0:d] = jnp.transpose((dqt_s[...] * scale).astype(BF16))
    saves[0].start()
    for load in loads:
        load.wait()
    dn1 = dot_nt(dqkv_o[...], wqkv[...])
    sums_o[...] = jnp.zeros_like(sums_o)
    sums_o[0:1, :] = jnp.sum(dqkv_o[:, 0:d].astype(F32), axis=0, keepdims=True)
    sums_o[1:2, :] = jnp.sum(dqkv_o[:, 2 * d : 3 * d].astype(F32), axis=0, keepdims=True)
    sums_o[2:3, :] = jnp.sum(low_mid.astype(F32), axis=0, keepdims=True)
    for i in range(pieces):
        part = slice(i * rp, (i + 1) * rp)
        dx, gain, shift = norm_back(dn1[part, :], x_s[i].astype(F32), vec[0:1, :])
        entered = low_mid[part, :].astype(F32) + dx
        kept = entered * keep[part, :]
        gtok[i] = kept.astype(BF16)
        saves[2 + i].start()
        sums_o[3:4, :] += gain
        sums_o[4:5, :] += shift
        sums_o[5:6, :] += jnp.sum(entered - kept, axis=0, keepdims=True)
    saves[1].start()
    for save in saves:
        save.wait()


def attn_back(c, info, own, others, keep, dmid, qkv, att, lse, vec, wqkv, wproj, held, clips):
    cpd, rp, d = own.shape
    pieces = 1 + len(others)
    rows = rp * pieces
    whole = lambda a: pl.BlockSpec(a.shape, lambda i, s: (0,) * a.ndim)
    at_clip = lambda shape: pl.BlockSpec((None,) + shape, lambda i, s: (c, 0, 0))
    in_specs = (
        [pl.BlockSpec(memory_space=pl.ANY)] * pieces
        + [
            at_clip((rows, 1)),
            at_clip((rows, d)),
            at_clip((rows, 3 * d)),
            at_clip((rows, d)),
            at_clip((16, rows)),
            whole(vec),
            pl.BlockSpec(memory_space=pl.ANY),
            whole(wproj),
        ]
    )
    operands = [own, *others, keep, dmid, qkv, att, lse, vec, wqkv, wproj]
    aliases = {}
    if held is not None:
        aliases = {1 + len(operands) + i: i for i in range(3)}
        in_specs = in_specs + [pl.BlockSpec(memory_space=pl.ANY)] * 3
        operands = operands + list(held)
    return pl.pallas_call(
        functools.partial(attn_back_kernel, c, pieces, cpd),
        grid_spec=pltpu.PrefetchScalarGridSpec(
            num_scalar_prefetch=1,
            grid=(1,),
            in_specs=in_specs,
            out_specs=[pl.BlockSpec(memory_space=pl.ANY)] * (2 + pieces),
            scratch_shapes=[
                pltpu.VMEM((rows, 3 * d), BF16),
                pltpu.VMEM((8, d), F32),
                pltpu.VMEM((pieces, rp, d), BF16),
                pltpu.VMEM((rows, d), BF16),
                pltpu.VMEM((16, rows), F32),
                pltpu.VMEM((d, rows), F32),
                pltpu.VMEM((pieces, rp, d), BF16),
                pltpu.VMEM(wqkv.shape, BF16),
                pltpu.SemaphoreType.DMA((2 + pieces,)),
                pltpu.SemaphoreType.DMA((1 + pieces,)),
            ],
        ),
        out_shape=[
            jax.ShapeDtypeStruct((cpd, rows, 3 * d), BF16),
            jax.ShapeDtypeStruct((cpd, 8, d), F32),
            jax.ShapeDtypeStruct((clips, rp, d), BF16),
        ]
        + [jax.ShapeDtypeStruct((rp, d), BF16)] * (pieces - 1),
        input_output_aliases=aliases,
        compiler_params=pltpu.CompilerParams(vmem_limit_bytes=60 * MIB),
        cost_estimate=pl.CostEstimate(
            flops=2 * rows * d * 4 * d + 40 * HEADS * rows * rows * (d // HEADS),
            bytes_accessed=rows * d * 28 + 8 * d * d,
            transcendentals=HEADS * rows * rows,
        ),
        name="attn_back",
    )(info, *operands)


def qkv_grad_kernel(n1, dqkv, info, turned_s, acc, stage, sems, keep, send):
    r = pl.program_id(0)
    per, rows, d = n1.shape
    groups, _, unit, width = stage.shape
    mine = info[1 + pl.num_programs(0) * per]
    cut = width // 256 * 128

    @pl.when(r == 0)
    def _():
        acc[...] = jnp.zeros_like(acc)

    for i in range(per):
        turned_s[:, i * rows : (i + 1) * rows] = jnp.transpose(n1[i])
    saves = []
    for at, cols in ((0, cut), (cut, width - cut)):
        part = slice(at, at + cols)
        piece = jnp.concatenate([dqkv[i, :, part] for i in range(per)], axis=0)
        acc[:, part] += dot_nn(turned_s[...], piece)
        to = pl.ds(at, cols)
        saves += [
            pltpu.make_async_copy(
                stage.at[:, side, :, to], half.at[:, :, to], sems.at[len(saves) + i]
            )
            for i, (side, half) in enumerate(((mine, keep), (1 - mine, send)))
        ]

        @pl.when(r == pl.num_programs(0) - 1)
        def _():
            stage[:, :, :, part] = acc[:, part].astype(BF16).reshape(groups, 2, unit, cols)
            for save in saves[-2:]:
                save.start()

    return saves


def early_kernel(info, n1, dqkv, keep, send, turned_s, acc, stage, sems):
    saves = qkv_grad_kernel(n1, dqkv, info, turned_s, acc, stage, sems, keep, send)

    @pl.when(pl.program_id(0) == pl.num_programs(0) - 1)
    def _():
        for save in saves:
            save.wait()


def late_kernel(cpd, narrow, moved, info, *refs):
    n1, dqkv, one_sums, two_sums, small = refs[:5]
    moving = refs[7 : 7 + moved]
    keep, send, out, tok = refs[7 + moved : 11 + moved]
    turned_s, acc, stage, sems, rows_s, tail, sems_move = refs[11 + moved : 18 + moved]
    held = refs[18 + moved :]
    r = pl.program_id(0)
    last = r == pl.num_programs(0) - 1
    groups, _, unit, width = stage.shape
    lanes = tail.shape[-1]
    mine = info[1 + cpd]
    moves, order = [], []
    for k in range(1, narrow):
        rank = lax.rem(info[0] + k, narrow)
        order.append(k - 1)
        moves.append(out.at[pl.ds(rank * cpd, cpd)])
        for c in range(cpd - 1):
            order.append((c + 1) * (narrow - 1) + k - 1)
            moves.append(tok.at[rank * cpd + c])
    arrivals = copies_of([(moving[i], held[i]) for i in order], sems_move)
    moves = copies_of([(held[i], to) for i, to in zip(order, moves)], sems_move)

    @pl.when(r == 0)
    def _():
        for arrival in arrivals:
            arrival.start()

    ends = [
        pltpu.make_async_copy(tail.at[:, side], half.at[:, :, pl.ds(width, lanes)], sems.at[4 + i])
        for i, (side, half) in enumerate(((mine, keep), (1 - mine, send)))
    ]

    @pl.when(last)
    def _():
        for arrival in arrivals:
            arrival.wait()
        for move in moves:
            move.start()
        one_total = jnp.sum(one_sums[...], axis=0)
        rows_s[...] = jnp.zeros_like(rows_s)
        picked = [
            one_total[5:6, :],
            one_total[3:4, :],
            two_sums[0:1, :],
            one_total[0:1, :],
            one_total[1:2, :],
            one_total[2:3, :],
            two_sums[2:3, :],
            one_total[4:5, :],
            two_sums[1:2, :],
        ]
        for i, row in enumerate(picked):
            rows_s[i : i + 1, :] = row
        vectors = (jnp.transpose(rows_s[...]) + small[...]).astype(BF16)
        tail[...] = vectors.reshape(groups, 2, unit, lanes)
        for end in ends:
            end.start()

    saves = qkv_grad_kernel(n1, dqkv, info, turned_s, acc, stage, sems, keep, send)

    @pl.when(last)
    def _():
        for copy in saves + ends + moves:
            copy.wait()


def qkv_grad(which, info, n1, dqkv, parts, late=None):
    cpd, rows, d = n1.shape
    width = dqkv.shape[2] // 2
    unit = d // parts
    groups = d // (2 * unit)
    per = 2 if cpd % 2 == 0 else 1
    anywhere = pl.BlockSpec(memory_space=pl.ANY)
    held = lambda a: pl.BlockSpec(a.shape, lambda c, s: (0,) * a.ndim)
    in_specs = [
        pl.BlockSpec((per, rows, d), lambda c, s: (c, 0, 0)),
        pl.BlockSpec((per, rows, width), lambda c, s: (c, 0, which)),
    ]
    scratch = [
        pltpu.VMEM((d, per * rows), BF16),
        pltpu.VMEM((d, width), F32),
        pltpu.VMEM((groups, 2, unit, width), BF16),
        pltpu.SemaphoreType.DMA((6,)),
    ]
    operands = [n1, dqkv]
    cols, kernel, aliases, shapes = width, early_kernel, {}, []
    if late is not None:
        one_sums, two_sums, small, out, out_back, tok, tok_back = late
        moving = list(out_back) + [t for back in tok_back[: cpd - 1] for t in back]
        kernel = functools.partial(late_kernel, cpd, 1 + len(out_back), len(moving))
        in_specs += [held(one_sums), held(two_sums), held(small)] + [anywhere] * (2 + len(moving))
        operands += [one_sums, two_sums, small, out, tok, *moving]
        lanes = small.shape[1]
        cols = width + lanes
        aliases = {6: 2, 7: 3}
        shapes = [jax.ShapeDtypeStruct(out.shape, BF16), jax.ShapeDtypeStruct(tok.shape, BF16)]
        scratch += [
            pltpu.VMEM((lanes, d), F32),
            pltpu.VMEM((groups, 2, unit, lanes), BF16),
            pltpu.SemaphoreType.DMA((max(len(moving), 1),)),
        ]
        scratch += [pltpu.VMEM(m.shape, BF16) for m in moving]
    shapes = [jax.ShapeDtypeStruct((groups, unit, cols), BF16)] * 2 + shapes
    return pl.pallas_call(
        kernel,
        grid_spec=pltpu.PrefetchScalarGridSpec(
            num_scalar_prefetch=1,
            grid=(cpd // per,),
            in_specs=in_specs,
            out_specs=[anywhere] * len(shapes),
            scratch_shapes=scratch,
        ),
        out_shape=shapes,
        input_output_aliases=aliases,
        compiler_params=pltpu.CompilerParams(vmem_limit_bytes=60 * MIB),
        cost_estimate=pl.CostEstimate(
            flops=2 * cpd * rows * d * width,
            bytes_accessed=2 * (cpd * rows * (d + width) + d * width),
            transcendentals=0,
        ),
        name="finish",
    )(info, *operands)


class ScatterSum:
    def __init__(self, keep, send, wide, narrow, first=(("wide", 0),)):
        rows, cols = 2 * keep.shape[0] * keep.shape[1], keep.shape[2]
        self.block = (rows // (wide * narrow), cols)
        bits_w, bits_n = wide.bit_length() - 1, narrow.bit_length() - 1
        order = [("wide", b, bits_w - 1 - b, wide) for b in range(bits_w)]
        order += [("narrow", b, bits_w + bits_n - 1 - b, narrow) for b in range(bits_n)]
        ahead = [o for key in first for o in order if o[:2] == key]
        self.order = ahead + [o for o in order if o not in ahead]
        axis, bit, dim, size = self.order.pop(0)
        shape = [2] * (bits_w + bits_n)
        shape[dim] = 1
        self.sums = None
        self.keep = keep.reshape(tuple(shape) + self.block)
        self.exchange(send.reshape(self.keep.shape), axis, bit, size)

    def exchange(self, sent, axis, bit, size):
        self.sent = sent
        self.got = lax.ppermute(sent, axis, [(i, i ^ (1 << bit)) for i in range(size)])

    def step(self, behind=None):
        if self.sums is not None:
            return self.sums
        keep, got = self.keep, self.got
        if behind is not None:
            keep = after(keep, behind)
        if not self.order:
            self.sums = keep.astype(F32) + got.astype(F32)
            return self.sums
        axis, bit, dim, size = self.order.pop(0)
        mine = (lax.axis_index(axis) >> bit) & 1

        def part(at):
            pieces = [lax.dynamic_slice_in_dim(x, at, 1, dim).astype(F32) for x in (keep, got)]
            return (pieces[0] + pieces[1]).astype(BF16)

        self.exchange(part(1 - mine), axis, bit, size)
        self.keep = part(mine)
        return self.sent

    def finish(self, behind=None):
        while self.sums is None:
            self.step(behind)
        return self.sums.reshape(self.block)


def after(value, *others):
    return lax.optimization_barrier((value, others))[0]


def body(
    wide,
    narrow,
    tokens,
    masked,
    resolution,
    mask_embed,
    gains,
    biases,
    w_qkv,
    w_proj,
    w_fc1,
    fc1_bias,
    w_fc2,
    cotangent,
):
    clips, freq_rows, cols, d = tokens.shape
    rp = freq_rows * cols
    cpd = clips // narrow
    rows = rp * narrow
    ff = w_fc1.shape[1]
    me = lax.axis_index("narrow")
    flat_tokens = tokens.reshape(clips, rp, d)
    flat_cot = cotangent.reshape(clips, rp, d)
    is_masked = masked.reshape(clips, rp) == 1

    def block_of(array, rank, at, count):
        return lax.dynamic_slice_in_dim(array, rank * cpd + at, count, 0)

    def entered_of(rank, at, count):
        return jnp.where(
            block_of(is_masked, rank, at, count)[:, :, None],
            mask_embed[None, None, :],
            block_of(flat_tokens, rank, at, count),
        )

    def to_rank(array, k):
        return lax.ppermute(array, "narrow", [(i, (i + k) % narrow) for i in range(narrow)])

    def from_rank(array, k):
        return lax.ppermute(array, "narrow", [(i, (i - k) % narrow) for i in range(narrow)])

    core = lax.axis_index("wide") & 1
    info = jnp.concatenate([me[None], block_of(resolution, me, 0, cpd), core[None]])
    vec = jnp.concatenate([gains.astype(F32).T, biases.astype(F32).T], axis=0)
    bias_row = fc1_bias.astype(F32)[None, :]

    shifts = range(1, narrow)
    others = []
    for c in range(cpd):
        send = [entered_of((me + k) % narrow, c, 1)[0] for k in shifts]
        if c > 0:
            send = after(send, others[-1])
        others.append([to_rank(send[k - 1], k) for k in shifts])
    keep_sent = [block_of(masked.reshape(clips, rp), (me + k) % narrow, 0, cpd) for k in shifts]
    keep_sent = after(keep_sent, others[0])
    keep_cols = [block_of(masked.reshape(clips, rp), me, 0, cpd)]
    keep_cols += [to_rank(keep_sent[k - 1], k) for k in shifts]
    keep = (jnp.concatenate(keep_cols, axis=1) != 1).astype(F32)[:, :, None]
    own = entered_of(me, 0, cpd)
    cot_send = [block_of(flat_cot, (me + k) % narrow, 0, cpd) for k in shifts]

    held = None
    for c in range(cpd):
        here = after(info, keep) if c == 1 else info
        held = attn_fwd(c, here, own, others[c], vec, w_qkv, w_proj, held)
    cot_send = after(cot_send, others[-1])
    cot_others = [to_rank(cot_send[k - 1], k) for k in shifts]
    n1, qkv, att, lse, mid, n2 = held

    out, *rest = mlp_fwd(info, mid, n2, vec, w_fc1, bias_row, w_fc2, clips, narrow)
    out_others, h = rest[:-1], rest[-1]
    out_back = [from_rank(out_others[k - 1], k) for k in shifts]

    dmid, two_sums, fc1_sums, *halves = mlp_back(
        info, flat_cot, cot_others, h, n2, mid, att, vec, w_fc1, w_fc2, wide
    )
    z_first = (("wide", 0), ("wide", 2), ("wide", 1), ("narrow", 0))
    fc2_chain = ScatterSum(*halves[:2], wide, narrow)
    fc1_chain = ScatterSum(*halves[2:], wide, narrow, z_first)
    small = fc1_sums[0].reshape(d, ff // d)
    small = jnp.pad(small, ((0, 0), (9, 119 - small.shape[1])))

    held = None
    tok_back = []
    for c in range(cpd):
        behind = held[1] if c > 0 else two_sums
        ready = [fc2_chain.step(behind), fc1_chain.step(behind)] if c in (1, 3) else []
        if False:
            ready.append(out_back)
        if c > 1:
            tok_back[c - 2] = after(tok_back[c - 2], behind)
            ready.append(tok_back[c - 2])
        here = after(info, *ready)
        *held, = attn_back(
            c, here, own, others[c], keep, dmid, qkv, att, lse, vec, w_qkv, w_proj, held, clips
        )
        tok_back.append([from_rank(g, k) for k, g in zip(shifts, held[3:])])
        held = held[:3]
    dqkv, one_sums, grad_tokens = held
    old = (fc2_chain, fc1_chain)
    here = after(info, *[chain.step(one_sums) for chain in old])
    early = qkv_grad(0, here, n1, dqkv, wide)
    chains = [ScatterSum(*early, wide, narrow)]
    here = after(info, *[chain.step(early[0]) for chain in old])
    *halves, out, grad_tokens = qkv_grad(
        1, here, n1, dqkv, wide, (one_sums, two_sums, small, out, out_back, grad_tokens, tok_back)
    )
    chains.append(ScatterSum(*halves, wide, narrow, z_first))
    sent = [chains[0].step(halves[0]), chains[1].step(halves[0])]
    grad_fc2 = fc2_chain.finish(sent)
    fc1_proj = fc1_chain.finish(sent)
    grad_fc1, grad_proj = fc1_proj[:, :ff], fc1_proj[:, ff:]
    for k in shifts:
        rank = (me + k) % narrow
        returned = after(tok_back[-1][k - 1], sent)
        grad_tokens = lax.dynamic_update_slice_in_dim(
            grad_tokens, returned[None], rank * cpd + cpd - 1, 0
        )
    while any(chain.sums is None for chain in chains):
        sent = [chain.step(sent) for chain in chains]
    last = jnp.concatenate([chain.finish() for chain in chains], axis=1)
    grad_qkv = last[:, : 3 * d]
    vectors = last[:, 3 * d :]
    return (
        out.reshape(tokens.shape),
        grad_tokens.reshape(tokens.shape),
        vectors[:, 0],
        vectors[:, 1:3],
        vectors[:, 3:9],
        grad_qkv,
        grad_proj,
        grad_fc1,
        vectors[:, 9 : 9 + ff // d].reshape(-1),
        grad_fc2,
    )


def solution(mesh):
    split = P("wide", None, "narrow", None)
    every = P(("wide", "narrow"))
    rows = P(("wide", "narrow"), None)
    return jax.shard_map(
        functools.partial(body, mesh.shape["wide"], mesh.shape["narrow"]),
        mesh=mesh,
        in_specs=(split, P("wide", None, "narrow"), P("wide")) + (P(),) * 8 + (split,),
        out_specs=(split, split, every, rows, rows, rows, rows, rows, every, rows),
        check_vma=False,
    )
```

```python
import functools

import jax
import jax.numpy as jnp
from jax import lax
from jax.experimental import pallas as pl
from jax.experimental.pallas import tpu as pltpu
from jax.sharding import PartitionSpec as P

HEADS = 12
EPS = 1e-06
LOG2E = 1.4426950408889634
F32 = jnp.float32
BF16 = jnp.bfloat16
MIB = 1 << 20


def dot_nn(a, b):
    return jnp.dot(a, b, preferred_element_type=F32)


def dot_nt(a, b):
    return lax.dot_general(a, b, (((1,), (1,)), ((), ())), preferred_element_type=F32)


def dot_tn(a, b):
    return lax.dot_general(a, b, (((0,), (0,)), ((), ())), preferred_element_type=F32)


def norm_stats(x):
    centred = x - jnp.mean(x, axis=-1, keepdims=True)
    rstd = lax.rsqrt(jnp.mean(centred * centred, axis=-1, keepdims=True) + EPS)
    return centred * rstd, rstd


def norm_back(grad, x, gain):
    xhat, rstd = norm_stats(x)
    scaled = grad * gain
    inner = jnp.mean(scaled * xhat, axis=-1, keepdims=True)
    outer = jnp.mean(scaled, axis=-1, keepdims=True)
    dx = rstd * (scaled - outer - xhat * inner)
    return dx, jnp.sum(grad * xhat, axis=0, keepdims=True), jnp.sum(grad, axis=0, keepdims=True)


def copies_of(pairs, sems):
    return [pltpu.make_async_copy(a, b, sems.at[i]) for i, (a, b) in enumerate(pairs)]


def row_valid(rows, piece_rows, full):
    at = lax.broadcasted_iota(jnp.int32, (rows, 1), 0) % piece_rows
    return (at < piece_rows // 2) | full


def attn_fwd_kernel(c, pieces, info, *refs):
    xs = refs[:pieces]
    vec, wqkv, wproj = refs[pieces : pieces + 3]
    made = refs[-8:-2]
    n1_o, qkv_o, att_o, lse_o, mid_o, n2_o = made
    lse_s, sems = refs[-2:]
    saves = copies_of([(m, o.at[c]) for m, o in zip(made, refs[-14:-8])], sems)
    rp, d = xs[0].shape
    rows = rp * pieces
    hw = d // HEADS
    full = info[1 + c] == 1
    for i in range(pieces):
        xhat, _ = norm_stats(xs[i][...].astype(F32))
        n1_o[i * rp : (i + 1) * rp, :] = (xhat * vec[0:1, :] + vec[6:7, :]).astype(BF16)
    saves[0].start()
    n1 = n1_o[...]
    qkv_o[:, 0:d] = (dot_nn(n1, wqkv[:, 0:d]) + vec[2:3, :]).astype(BF16)
    qkv_o[:, d : 2 * d] = dot_nn(n1, wqkv[:, d : 2 * d]).astype(BF16)
    qkv_o[:, 2 * d : 3 * d] = (dot_nn(n1, wqkv[:, 2 * d : 3 * d]) + vec[3:4, :]).astype(BF16)
    saves[1].start()
    scale2 = hw**-0.5 * LOG2E
    bias = jnp.where(row_valid(rows, rp, full), 0.0, -1e30).astype(BF16)
    lane = lax.broadcasted_iota(jnp.int32, (1, 2 * hw), 1)
    head_lane = lax.broadcasted_iota(jnp.int32, (1, 128), 1)
    lse_s[...] = jnp.zeros_like(lse_s)

    def pair(p, carry):
        at = p * 2 * hw
        q = qkv_o[:, pl.ds(at, 2 * hw)]
        k = qkv_o[:, pl.ds(d + at, 2 * hw)]
        v = qkv_o[:, pl.ds(2 * d + at, 2 * hw)]
        outs = []
        tops = []
        for e in range(2):
            mine = (lane < hw) if e == 0 else (lane >= hw)
            spare = lane == hw * (1 - e)
            one = jnp.where(spare, 1.0, 0.0).astype(BF16)
            qm = jnp.where(mine, q, one)
            km = jnp.where(spare, bias, k)
            s = dot_nt(qm, km)
            top = jnp.max(s, axis=-1, keepdims=True)
            pr = jnp.exp2((s - top) * scale2).astype(BF16)
            vm = jnp.where(mine, v, jnp.ones_like(v))
            outs.append(dot_nn(pr, vm))
            tops.append(top)
        low = lane < hw
        total = pltpu.roll(jnp.where(low, outs[1], outs[0]), hw, 1)
        att_o[:, pl.ds(at, 2 * hw)] = (jnp.where(low, outs[0], outs[1]) / total).astype(BF16)
        log_total = jnp.log2(total) + scale2 * jnp.where(low, tops[0], tops[1])
        first = jnp.broadcast_to(log_total[:, 0:1], (rows, 128))
        second = jnp.broadcast_to(log_total[:, hw : hw + 1], (rows, 128))
        lse_s[...] = jnp.where(
            head_lane == 2 * p, first, jnp.where(head_lane == 2 * p + 1, second, lse_s[...])
        )
        return carry

    for p in range(HEADS // 2):
        pair(p, 0)
    lse_o[...] = jnp.transpose(lse_s[...])[0:16, :]
    saves[2].start()
    saves[3].start()
    branch = dot_nn(att_o[...], wproj[...]) + vec[4:5, :]
    for i in range(pieces):
        part = slice(i * rp, (i + 1) * rp)
        middle = xs[i][...].astype(F32) + branch[part, :]
        mid_o[part, :] = middle.astype(BF16)
        xhat, _ = norm_stats(middle)
        n2_o[part, :] = (xhat * vec[1:2, :] + vec[7:8, :]).astype(BF16)
    saves[4].start()
    saves[5].start()
    for save in saves:
        save.wait()


def attn_fwd(c, info, own, others, vec, wqkv, wproj, held):
    cpd, rp, d = own.shape
    pieces = 1 + len(others)
    rows = rp * pieces
    whole = lambda a: pl.BlockSpec(a.shape, lambda i, s: (0,) * a.ndim)
    at_clip = lambda shape: pl.BlockSpec((None,) + shape, lambda i, s: (c, 0, 0))
    shapes = [
        ((rows, d), BF16),
        ((rows, 3 * d), BF16),
        ((rows, d), BF16),
        ((16, rows), F32),
        ((rows, d), BF16),
        ((rows, d), BF16),
    ]
    in_specs = [at_clip((rp, d))] + [whole(o) for o in others] + [whole(vec), whole(wqkv), whole(wproj)]
    operands = [own, *others, vec, wqkv, wproj]
    aliases = {}
    if held is not None:
        aliases = {1 + len(operands) + i: i for i in range(6)}
        in_specs = in_specs + [pl.BlockSpec(memory_space=pl.ANY)] * 6
        operands = operands + list(held)
    return pl.pallas_call(
        functools.partial(attn_fwd_kernel, c, pieces),
        grid_spec=pltpu.PrefetchScalarGridSpec(
            num_scalar_prefetch=1,
            grid=(1,),
            in_specs=in_specs,
            out_specs=[pl.BlockSpec(memory_space=pl.ANY)] * len(shapes),
            scratch_shapes=[pltpu.VMEM(s, t) for s, t in shapes]
            + [pltpu.VMEM((rows, 128), F32), pltpu.SemaphoreType.DMA((len(shapes),))],
        ),
        out_shape=[jax.ShapeDtypeStruct((cpd,) + s, t) for s, t in shapes],
        input_output_aliases=aliases,
        compiler_params=pltpu.CompilerParams(vmem_limit_bytes=60 * MIB),
        cost_estimate=pl.CostEstimate(
            flops=2 * rows * d * 4 * d + 16 * HEADS * rows * rows * (d // HEADS),
            bytes_accessed=rows * d * 16 + 8 * d * d,
            transcendentals=HEADS * rows * rows,
        ),
        name="attn_fwd",
    )(info, *operands)


def mlp_fwd_kernel(pieces, info, mid, n2, vec, w1, b1, w2, *outs):
    h_o = outs[pieces]
    rows, d = n2.shape
    rp = rows // pieces
    full = info[1 + pl.program_id(0)] == 1
    ff = w1.shape[1]
    chunk = d
    x = n2[...]
    acc = mid[...].astype(F32) + vec[5:6, :]
    for j in range(ff // chunk):
        part = slice(j * chunk, (j + 1) * chunk)
        h = dot_nn(x, w1[:, part]) + b1[:, part]
        h_o[:, part] = h.astype(BF16)
        act = (h * (0.5 + 0.5 * lax.erf(h * 0.7071067811865476))).astype(BF16)
        acc = acc + dot_nn(act, w2[part, :])
    out = jnp.where(row_valid(rows, rp, full), acc, 0.0).astype(BF16)
    for i in range(pieces):
        outs[i][...] = out[i * rp : (i + 1) * rp, :]


def mlp_fwd(info, mid, n2, vec, w1, b1, w2, clips, pieces):
    cpd, rows, d = n2.shape
    ff = w1.shape[1]
    rp = rows // pieces
    by_clip = lambda w: pl.BlockSpec((None, rows, w), lambda c, s: (c, 0, 0))
    once = lambda a: pl.BlockSpec(a.shape, lambda c, s: (0, 0), pipeline_mode=pl.Buffered(1))
    return pl.pallas_call(
        functools.partial(mlp_fwd_kernel, pieces),
        grid_spec=pltpu.PrefetchScalarGridSpec(
            num_scalar_prefetch=1,
            grid=(cpd,),
            in_specs=[by_clip(d), by_clip(d), once(vec), once(w1), once(b1), once(w2)],
            out_specs=[pl.BlockSpec((None, rp, d), lambda c, s: (s[0] * cpd + c, 0, 0))]
            + [pl.BlockSpec((None, rp, d), lambda c, s: (c, 0, 0))] * (pieces - 1)
            + [by_clip(ff)],
        ),
        out_shape=[jax.ShapeDtypeStruct((clips, rp, d), BF16)]
        + [jax.ShapeDtypeStruct((cpd, rp, d), BF16)] * (pieces - 1)
        + [jax.ShapeDtypeStruct((cpd, rows, ff), BF16)],
        compiler_params=pltpu.CompilerParams(vmem_limit_bytes=60 * MIB),
        cost_estimate=pl.CostEstimate(
            flops=4 * cpd * rows * d * ff,
            bytes_accessed=cpd * rows * (8 * d + 2 * ff) + 4 * d * ff,
            transcendentals=cpd * rows * ff,
        ),
        name="mlp_fwd",
    )(info, mid, n2, vec, w1, b1, w2)


def upstream_of(cots, full):
    rp = cots[0].shape[0]
    keep = row_valid(rp, rp, full)
    return jnp.concatenate(
        [jnp.where(keep, c[...].astype(F32), 0.0) for c in cots], axis=0
    )


def mlp_back_kernel(pieces, cpd, info, *refs):
    cots = refs[:pieces]
    h, n2, mid, att, vec, w1_in, w2_in = refs[pieces : pieces + 7]
    dmid_o, sums_o, fc1_sums_o, keep2, send2, keep1, send1 = refs[pieces + 7 : pieces + 14]
    w1, w2, acc1, acc2, dn2_s, up_s, turned_s, stage1, stage2, sems_in, sems1, sems2 = refs[pieces + 14 :]
    r = pl.program_id(0)
    last = r == cpd - 1
    rows, d = mid.shape
    ff = w1.shape[1]
    chunk = d
    count = ff // chunk
    unit1 = keep1.shape[1]
    unit2 = keep2.shape[1]
    per2 = chunk // (2 * unit2)
    mine = info[1 + cpd]

    def cols_of(j):
        return pl.ds(pl.multiple_of(j * chunk, chunk), chunk)

    def loads(j):
        part = cols_of(j)
        return [
            pltpu.make_async_copy(w1_in.at[:, part], w1.at[:, part], sems_in.at[0, j]),
            pltpu.make_async_copy(w2_in.at[part], w2.at[part], sems_in.at[1, j]),
        ]

    def saves1(j, slot):
        cols = cols_of(j)
        return [
            pltpu.make_async_copy(stage1.at[slot, :, side], to.at[:, :, cols], sems1.at[slot, i])
            for i, (side, to) in enumerate(((mine, keep1), (1 - mine, send1)))
        ]

    def saves2(j, slot):
        at = pl.ds(j * per2, per2)
        return [
            pltpu.make_async_copy(stage2.at[slot, :, side], to.at[at], sems2.at[slot, i])
            for i, (side, to) in enumerate(((mine, keep2), (1 - mine, send2)))
        ]

    @pl.when(r == 0)
    def _():
        for j in range(count):
            for load in loads(j):
                load.start()
        acc1[...] = jnp.zeros_like(acc1)
        acc2[...] = jnp.zeros_like(acc2)
        sums_o[...] = jnp.zeros_like(sums_o)
        fc1_sums_o[...] = jnp.zeros_like(fc1_sums_o)

    up = upstream_of(cots, info[1 + r] == 1)
    up_s[...] = up.astype(BF16)
    sums_o[2:3, :] += jnp.sum(up, axis=0, keepdims=True)
    turned_s[...] = jnp.transpose(n2[...])
    dn2_s[...] = jnp.zeros_like(dn2_s)

    def one(j, carry):
        part = cols_of(j)

        @pl.when(r == 0)
        def _():
            for load in loads(j):
                load.wait()

        pre = h[:, part].astype(F32)
        cdf = 0.5 + 0.5 * lax.erf(pre * 0.7071067811865476)
        density = 0.3989422804014327 * jnp.exp2(pre * pre * (-0.5 * LOG2E))
        act = (pre * cdf).astype(BF16)
        grad = dot_nt(up_s[...], w2[part, :])
        dh = (grad * (cdf + pre * density)).astype(BF16)
        fc1_sums_o[0:1, part] += jnp.sum(dh.astype(F32), axis=0, keepdims=True)
        acc2[part, :] += dot_tn(act, up_s[...])
        dn2_s[...] += dot_nt(dh, w1[:, part])
        acc1[:, part] += dot_nn(turned_s[...], dh)

        @pl.when(last)
        def _():
            slot = j % 2

            @pl.when(j > 1)
            def _():
                for save in saves1(j - 2, slot) + saves2(j - 2, slot):
                    save.wait()

            stage2[slot] = acc2[part, :].astype(BF16).reshape(per2, 2, unit2, d)
            stage1[slot] = acc1[:, part].astype(BF16).reshape(d // (2 * unit1), 2, unit1, chunk)
            for save in saves1(j, slot) + saves2(j, slot):
                save.start()

        return carry

    lax.fori_loop(0, count, one, 0)
    dx, gain, shift = norm_back(dn2_s[...], mid[...].astype(F32), vec[1:2, :])
    dmid = (up_s[...].astype(F32) + dx).astype(BF16)
    dmid_o[...] = dmid
    sums_o[0:1, :] += gain
    sums_o[1:2, :] += shift
    acc1[:, ff : ff + d] += dot_tn(att[...], dmid)

    @pl.when(last)
    def _():
        for j in range(max(count - 2, 0), count):
            for save in saves1(j, j % 2) + saves2(j, j % 2):
                save.wait()
        stage1[0] = acc1[:, ff : ff + d].astype(BF16).reshape(d // (2 * unit1), 2, unit1, d)
        for save in saves1(count, 0):
            save.start()
        for save in saves1(count, 0):
            save.wait()


def mlp_back(info, cot, cot_others, h, n2, mid, att, vec, w1, w2, parts):
    clips, rp, d = cot.shape
    cpd, rows, ff = h.shape
    pieces = 1 + len(cot_others)
    unit1 = d // parts
    unit2 = ff // parts
    once = lambda a: pl.BlockSpec(a.shape, lambda c, s: (0, 0), pipeline_mode=pl.Buffered(1))
    held = lambda shape: pl.BlockSpec(shape, lambda c, s: (0, 0))
    by_clip = lambda w: pl.BlockSpec((None, rows, w), lambda c, s: (c, 0, 0))
    halves = [(d // (2 * unit1), unit1, ff + d), (ff // (2 * unit2), unit2, d)]
    return pl.pallas_call(
        functools.partial(mlp_back_kernel, pieces, cpd),
        grid_spec=pltpu.PrefetchScalarGridSpec(
            num_scalar_prefetch=1,
            grid=(cpd,),
            in_specs=[pl.BlockSpec((None, rp, d), lambda c, s: (s[0] * cpd + c, 0, 0))]
            + [pl.BlockSpec((None, rp, d), lambda c, s: (c, 0, 0))] * (pieces - 1)
            + [by_clip(ff), by_clip(d), by_clip(d), by_clip(d), once(vec)]
            + [pl.BlockSpec(memory_space=pl.ANY)] * 2,
            out_specs=[by_clip(d), held((8, d)), held((8, ff))]
            + [pl.BlockSpec(memory_space=pl.ANY)] * 4,
            scratch_shapes=[
                pltpu.VMEM(w1.shape, BF16),
                pltpu.VMEM(w2.shape, BF16),
                pltpu.VMEM((d, ff + d), F32),
                pltpu.VMEM((ff, d), F32),
                pltpu.VMEM((rows, d), F32),
                pltpu.VMEM((rows, d), BF16),
                pltpu.VMEM((d, rows), BF16),
                pltpu.VMEM((2, d // (2 * unit1), 2, unit1, d), BF16),
                pltpu.VMEM((2, d // (2 * unit2), 2, unit2, d), BF16),
                pltpu.SemaphoreType.DMA((2, ff // d)),
                pltpu.SemaphoreType.DMA((2, 2)),
                pltpu.SemaphoreType.DMA((2, 2)),
            ],
        ),
        out_shape=[
            jax.ShapeDtypeStruct((cpd, rows, d), BF16),
            jax.ShapeDtypeStruct((8, d), F32),
            jax.ShapeDtypeStruct((8, ff), F32),
        ]
        + [jax.ShapeDtypeStruct(halves[1], BF16)] * 2
        + [jax.ShapeDtypeStruct(halves[0], BF16)] * 2,
        compiler_params=pltpu.CompilerParams(vmem_limit_bytes=62 * MIB),
        cost_estimate=pl.CostEstimate(
            flops=8 * cpd * rows * d * ff,
            bytes_accessed=cpd * rows * (14 * d + 2 * ff) + 8 * d * ff,
            transcendentals=2 * cpd * rows * ff,
        ),
        name="mlp_back",
    )(info, cot, *cot_others, h, n2, mid, att, vec, w1, w2)


def attn_back_kernel(c, pieces, cpd, info, *refs):
    xs = refs[:pieces]
    keep, dmid, qkv, att, lse, vec, wqkv_in, wproj = refs[pieces : pieces + 8]
    dqkv_o, sums_o, gtok, do_s, delta_s, dqt_s, x_s, wqkv, sems, sems_in = refs[-10:]
    dqkv_out, sums_out, own_out, *others_out = refs[-12 - pieces : -10]
    rp, d = x_s.shape[1:]
    sources = [(wqkv_in, wqkv), (xs[0].at[c], x_s.at[0])]
    sources += [(x, x_s.at[1 + i]) for i, x in enumerate(xs[1:])]
    loads = copies_of(sources, sems_in)
    for load in loads:
        load.start()
    rows = rp * pieces
    hw = d // HEADS
    full = info[1 + c] == 1
    targets = [(dqkv_o, dqkv_out.at[c]), (sums_o, sums_out.at[c])]
    targets += [(gtok.at[0], own_out.at[info[0] * cpd + c])]
    targets += [(gtok.at[1 + i], o) for i, o in enumerate(others_out)]
    saves = copies_of(targets, sems)
    low_mid = dmid[...]
    do_s[...] = dot_nt(low_mid, wproj[...]).astype(BF16)
    prod = (do_s[...].astype(F32) * att[...].astype(F32)).astype(BF16)
    head_of = lax.broadcasted_iota(jnp.int32, (16, d), 1) // hw
    select = (head_of == lax.broadcasted_iota(jnp.int32, (16, d), 0)).astype(BF16)
    delta_s[...] = dot_nt(select, prod)
    scale = hw**-0.5
    scale2 = scale * LOG2E
    bias = jnp.where(row_valid(rows, rp, full), 0.0, -1e30).astype(BF16)
    lane = lax.broadcasted_iota(jnp.int32, (1, 2 * hw), 1)

    def pair(p, carry):
        at = p * 2 * hw
        q = qkv[:, pl.ds(at, 2 * hw)]
        k = qkv[:, pl.ds(d + at, 2 * hw)]
        v = qkv[:, pl.ds(2 * d + at, 2 * hw)]
        do = do_s[:, pl.ds(at, 2 * hw)]
        kt = jnp.transpose(k)
        zero = jnp.zeros_like(q)
        dk = dv = None
        for e in range(2):
            mine = (lane < hw) if e == 0 else (lane >= hw)
            spare = lane == hw * (1 - e)
            one = jnp.where(spare, 1.0, 0.0).astype(BF16)
            qm = jnp.where(mine, q, one)
            km = jnp.where(spare, bias, k)
            st = dot_nt(km, qm)
            pt = jnp.exp2(st * scale2 - lse[pl.ds(2 * p + e, 1), :])
            vm = jnp.where(mine, v, zero)
            dpt = dot_nt(vm, do)
            dst = (pt * (dpt - delta_s[pl.ds(2 * p + e, 1), :])).astype(BF16)
            dom = jnp.where(mine, do, zero)
            qz = jnp.where(mine, q, zero)
            dv_e = dot_nn(pt.astype(BF16), dom)
            dk_e = dot_nn(dst, qz)
            dv = dv_e if dv is None else dv + dv_e
            dk = dk_e if dk is None else dk + dk_e
            dqt_s[pl.ds(at + e * hw, hw), :] = dot_nn(
                kt[e * hw : (e + 1) * hw, :], dst
            )
        dqkv_o[:, pl.ds(d + at, 2 * hw)] = (dk * scale).astype(BF16)
        dqkv_o[:, pl.ds(2 * d + at, 2 * hw)] = dv.astype(BF16)
        return carry

    for p in range(HEADS // 2):
        pair(p, 0)
    dqkv_o[:, 0:d] = jnp.transpose((dqt_s[...] * scale).astype(BF16))
    saves[0].start()
    for load in loads:
        load.wait()
    dn1 = dot_nt(dqkv_o[...], wqkv[...])
    sums_o[...] = jnp.zeros_like(sums_o)
    sums_o[0:1, :] = jnp.sum(dqkv_o[:, 0:d].astype(F32), axis=0, keepdims=True)
    sums_o[1:2, :] = jnp.sum(dqkv_o[:, 2 * d : 3 * d].astype(F32), axis=0, keepdims=True)
    sums_o[2:3, :] = jnp.sum(low_mid.astype(F32), axis=0, keepdims=True)
    for i in range(pieces):
        part = slice(i * rp, (i + 1) * rp)
        dx, gain, shift = norm_back(dn1[part, :], x_s[i].astype(F32), vec[0:1, :])
        entered = low_mid[part, :].astype(F32) + dx
        kept = entered * keep[part, :]
        gtok[i] = kept.astype(BF16)
        saves[2 + i].start()
        sums_o[3:4, :] += gain
        sums_o[4:5, :] += shift
        sums_o[5:6, :] += jnp.sum(entered - kept, axis=0, keepdims=True)
    saves[1].start()
    for save in saves:
        save.wait()


def attn_back(c, info, own, others, keep, dmid, qkv, att, lse, vec, wqkv, wproj, held, clips):
    cpd, rp, d = own.shape
    pieces = 1 + len(others)
    rows = rp * pieces
    whole = lambda a: pl.BlockSpec(a.shape, lambda i, s: (0,) * a.ndim)
    at_clip = lambda shape: pl.BlockSpec((None,) + shape, lambda i, s: (c, 0, 0))
    in_specs = (
        [pl.BlockSpec(memory_space=pl.ANY)] * pieces
        + [
            at_clip((rows, 1)),
            at_clip((rows, d)),
            at_clip((rows, 3 * d)),
            at_clip((rows, d)),
            at_clip((16, rows)),
            whole(vec),
            pl.BlockSpec(memory_space=pl.ANY),
            whole(wproj),
        ]
    )
    operands = [own, *others, keep, dmid, qkv, att, lse, vec, wqkv, wproj]
    aliases = {}
    if held is not None:
        aliases = {1 + len(operands) + i: i for i in range(3)}
        in_specs = in_specs + [pl.BlockSpec(memory_space=pl.ANY)] * 3
        operands = operands + list(held)
    return pl.pallas_call(
        functools.partial(attn_back_kernel, c, pieces, cpd),
        grid_spec=pltpu.PrefetchScalarGridSpec(
            num_scalar_prefetch=1,
            grid=(1,),
            in_specs=in_specs,
            out_specs=[pl.BlockSpec(memory_space=pl.ANY)] * (2 + pieces),
            scratch_shapes=[
                pltpu.VMEM((rows, 3 * d), BF16),
                pltpu.VMEM((8, d), F32),
                pltpu.VMEM((pieces, rp, d), BF16),
                pltpu.VMEM((rows, d), BF16),
                pltpu.VMEM((16, rows), F32),
                pltpu.VMEM((d, rows), F32),
                pltpu.VMEM((pieces, rp, d), BF16),
                pltpu.VMEM(wqkv.shape, BF16),
                pltpu.SemaphoreType.DMA((2 + pieces,)),
                pltpu.SemaphoreType.DMA((1 + pieces,)),
            ],
        ),
        out_shape=[
            jax.ShapeDtypeStruct((cpd, rows, 3 * d), BF16),
            jax.ShapeDtypeStruct((cpd, 8, d), F32),
            jax.ShapeDtypeStruct((clips, rp, d), BF16),
        ]
        + [jax.ShapeDtypeStruct((rp, d), BF16)] * (pieces - 1),
        input_output_aliases=aliases,
        compiler_params=pltpu.CompilerParams(vmem_limit_bytes=60 * MIB),
        cost_estimate=pl.CostEstimate(
            flops=2 * rows * d * 4 * d + 40 * HEADS * rows * rows * (d // HEADS),
            bytes_accessed=rows * d * 28 + 8 * d * d,
            transcendentals=HEADS * rows * rows,
        ),
        name="attn_back",
    )(info, *operands)


def qkv_grad_kernel(n1, dqkv, info, turned_s, acc, stage, sems, keep, send):
    r = pl.program_id(0)
    per, rows, d = n1.shape
    groups, _, unit, width = stage.shape
    mine = info[1 + pl.num_programs(0) * per]
    cut = width // 256 * 128

    @pl.when(r == 0)
    def _():
        acc[...] = jnp.zeros_like(acc)

    for i in range(per):
        turned_s[:, i * rows : (i + 1) * rows] = jnp.transpose(n1[i])
    saves = []
    for at, cols in ((0, cut), (cut, width - cut)):
        part = slice(at, at + cols)
        piece = jnp.concatenate([dqkv[i, :, part] for i in range(per)], axis=0)
        acc[:, part] += dot_nn(turned_s[...], piece)
        to = pl.ds(at, cols)
        saves += [
            pltpu.make_async_copy(
                stage.at[:, side, :, to], half.at[:, :, to], sems.at[len(saves) + i]
            )
            for i, (side, half) in enumerate(((mine, keep), (1 - mine, send)))
        ]

        @pl.when(r == pl.num_programs(0) - 1)
        def _():
            stage[:, :, :, part] = acc[:, part].astype(BF16).reshape(groups, 2, unit, cols)
            for save in saves[-2:]:
                save.start()

    return saves


def early_kernel(info, n1, dqkv, keep, send, turned_s, acc, stage, sems):
    saves = qkv_grad_kernel(n1, dqkv, info, turned_s, acc, stage, sems, keep, send)

    @pl.when(pl.program_id(0) == pl.num_programs(0) - 1)
    def _():
        for save in saves:
            save.wait()


def late_kernel(cpd, narrow, moved, info, *refs):
    n1, dqkv, one_sums, two_sums, small = refs[:5]
    moving = refs[7 : 7 + moved]
    keep, send, out, tok = refs[7 + moved : 11 + moved]
    turned_s, acc, stage, sems, rows_s, tail, sems_move = refs[11 + moved : 18 + moved]
    held = refs[18 + moved :]
    r = pl.program_id(0)
    last = r == pl.num_programs(0) - 1
    groups, _, unit, width = stage.shape
    lanes = tail.shape[-1]
    mine = info[1 + cpd]
    moves, order = [], []
    for k in range(1, narrow):
        rank = lax.rem(info[0] + k, narrow)
        order.append(k - 1)
        moves.append(out.at[pl.ds(rank * cpd, cpd)])
        for c in range(cpd):
            order.append((c + 1) * (narrow - 1) + k - 1)
            moves.append(tok.at[rank * cpd + c])
    arrivals = copies_of([(moving[i], held[i]) for i in order], sems_move)
    moves = copies_of([(held[i], to) for i, to in zip(order, moves)], sems_move)

    @pl.when(r == 0)
    def _():
        for arrival in arrivals:
            arrival.start()

    ends = [
        pltpu.make_async_copy(tail.at[:, side], half.at[:, :, pl.ds(width, lanes)], sems.at[4 + i])
        for i, (side, half) in enumerate(((mine, keep), (1 - mine, send)))
    ]

    @pl.when(last)
    def _():
        for arrival in arrivals:
            arrival.wait()
        for move in moves:
            move.start()
        one_total = jnp.sum(one_sums[...], axis=0)
        rows_s[...] = jnp.zeros_like(rows_s)
        picked = [
            one_total[5:6, :],
            one_total[3:4, :],
            two_sums[0:1, :],
            one_total[0:1, :],
            one_total[1:2, :],
            one_total[2:3, :],
            two_sums[2:3, :],
            one_total[4:5, :],
            two_sums[1:2, :],
        ]
        for i, row in enumerate(picked):
            rows_s[i : i + 1, :] = row
        vectors = (jnp.transpose(rows_s[...]) + small[...]).astype(BF16)
        tail[...] = vectors.reshape(groups, 2, unit, lanes)
        for end in ends:
            end.start()

    saves = qkv_grad_kernel(n1, dqkv, info, turned_s, acc, stage, sems, keep, send)

    @pl.when(last)
    def _():
        for copy in saves + ends + moves:
            copy.wait()


def qkv_grad(which, info, n1, dqkv, parts, late=None):
    cpd, rows, d = n1.shape
    width = dqkv.shape[2] // 2
    unit = d // parts
    groups = d // (2 * unit)
    per = 2 if cpd % 2 == 0 else 1
    anywhere = pl.BlockSpec(memory_space=pl.ANY)
    held = lambda a: pl.BlockSpec(a.shape, lambda c, s: (0,) * a.ndim)
    in_specs = [
        pl.BlockSpec((per, rows, d), lambda c, s: (c, 0, 0)),
        pl.BlockSpec((per, rows, width), lambda c, s: (c, 0, which)),
    ]
    scratch = [
        pltpu.VMEM((d, per * rows), BF16),
        pltpu.VMEM((d, width), F32),
        pltpu.VMEM((groups, 2, unit, width), BF16),
        pltpu.SemaphoreType.DMA((6,)),
    ]
    operands = [n1, dqkv]
    cols, kernel, aliases, shapes = width, early_kernel, {}, []
    if late is not None:
        one_sums, two_sums, small, out, out_back, tok, tok_back = late
        moving = list(out_back) + [t for back in tok_back for t in back]
        kernel = functools.partial(late_kernel, cpd, 1 + len(out_back), len(moving))
        in_specs += [held(one_sums), held(two_sums), held(small)] + [anywhere] * (2 + len(moving))
        operands += [one_sums, two_sums, small, out, tok, *moving]
        lanes = small.shape[1]
        cols = width + lanes
        aliases = {6: 2, 7: 3}
        shapes = [jax.ShapeDtypeStruct(out.shape, BF16), jax.ShapeDtypeStruct(tok.shape, BF16)]
        scratch += [
            pltpu.VMEM((lanes, d), F32),
            pltpu.VMEM((groups, 2, unit, lanes), BF16),
            pltpu.SemaphoreType.DMA((max(len(moving), 1),)),
        ]
        scratch += [pltpu.VMEM(m.shape, BF16) for m in moving]
    shapes = [jax.ShapeDtypeStruct((groups, unit, cols), BF16)] * 2 + shapes
    return pl.pallas_call(
        kernel,
        grid_spec=pltpu.PrefetchScalarGridSpec(
            num_scalar_prefetch=1,
            grid=(cpd // per,),
            in_specs=in_specs,
            out_specs=[anywhere] * len(shapes),
            scratch_shapes=scratch,
        ),
        out_shape=shapes,
        input_output_aliases=aliases,
        compiler_params=pltpu.CompilerParams(vmem_limit_bytes=60 * MIB),
        cost_estimate=pl.CostEstimate(
            flops=2 * cpd * rows * d * width,
            bytes_accessed=2 * (cpd * rows * (d + width) + d * width),
            transcendentals=0,
        ),
        name="finish",
    )(info, *operands)


class ScatterSum:
    def __init__(self, keep, send, wide, narrow, first=(("wide", 0),)):
        rows, cols = 2 * keep.shape[0] * keep.shape[1], keep.shape[2]
        self.block = (rows // (wide * narrow), cols)
        bits_w, bits_n = wide.bit_length() - 1, narrow.bit_length() - 1
        order = [("wide", b, bits_w - 1 - b, wide) for b in range(bits_w)]
        order += [("narrow", b, bits_w + bits_n - 1 - b, narrow) for b in range(bits_n)]
        ahead = [o for key in first for o in order if o[:2] == key]
        self.order = ahead + [o for o in order if o not in ahead]
        axis, bit, dim, size = self.order.pop(0)
        shape = [2] * (bits_w + bits_n)
        shape[dim] = 1
        self.sums = None
        self.keep = keep.reshape(tuple(shape) + self.block)
        self.exchange(send.reshape(self.keep.shape), axis, bit, size)

    def exchange(self, sent, axis, bit, size):
        self.sent = sent
        self.got = lax.ppermute(sent, axis, [(i, i ^ (1 << bit)) for i in range(size)])

    def step(self, behind=None):
        if self.sums is not None:
            return self.sums
        keep, got = self.keep, self.got
        if behind is not None:
            keep = after(keep, behind)
        if not self.order:
            self.sums = keep.astype(F32) + got.astype(F32)
            return self.sums
        axis, bit, dim, size = self.order.pop(0)
        mine = (lax.axis_index(axis) >> bit) & 1

        def part(at):
            pieces = [lax.dynamic_slice_in_dim(x, at, 1, dim).astype(F32) for x in (keep, got)]
            return (pieces[0] + pieces[1]).astype(BF16)

        self.exchange(part(1 - mine), axis, bit, size)
        self.keep = part(mine)
        return self.sent

    def finish(self, behind=None):
        while self.sums is None:
            self.step(behind)
        return self.sums.reshape(self.block)


def after(value, *others):
    return lax.optimization_barrier((value, others))[0]


def body(
    wide,
    narrow,
    tokens,
    masked,
    resolution,
    mask_embed,
    gains,
    biases,
    w_qkv,
    w_proj,
    w_fc1,
    fc1_bias,
    w_fc2,
    cotangent,
):
    clips, freq_rows, cols, d = tokens.shape
    rp = freq_rows * cols
    cpd = clips // narrow
    rows = rp * narrow
    ff = w_fc1.shape[1]
    me = lax.axis_index("narrow")
    flat_tokens = tokens.reshape(clips, rp, d)
    flat_cot = cotangent.reshape(clips, rp, d)
    is_masked = masked.reshape(clips, rp) == 1

    def block_of(array, rank, at, count):
        return lax.dynamic_slice_in_dim(array, rank * cpd + at, count, 0)

    def entered_of(rank, at, count):
        return jnp.where(
            block_of(is_masked, rank, at, count)[:, :, None],
            mask_embed[None, None, :],
            block_of(flat_tokens, rank, at, count),
        )

    def to_rank(array, k):
        return lax.ppermute(array, "narrow", [(i, (i + k) % narrow) for i in range(narrow)])

    def from_rank(array, k):
        return lax.ppermute(array, "narrow", [(i, (i - k) % narrow) for i in range(narrow)])

    core = lax.axis_index("wide") & 1
    info = jnp.concatenate([me[None], block_of(resolution, me, 0, cpd), core[None]])
    vec = jnp.concatenate([gains.astype(F32).T, biases.astype(F32).T], axis=0)
    bias_row = fc1_bias.astype(F32)[None, :]

    shifts = range(1, narrow)
    others = []
    for c in range(cpd):
        send = [entered_of((me + k) % narrow, c, 1)[0] for k in shifts]
        if c > 0:
            send = after(send, others[-1])
        others.append([to_rank(send[k - 1], k) for k in shifts])
    keep_sent = [block_of(masked.reshape(clips, rp), (me + k) % narrow, 0, cpd) for k in shifts]
    keep_sent = after(keep_sent, others[0])
    keep_cols = [block_of(masked.reshape(clips, rp), me, 0, cpd)]
    keep_cols += [to_rank(keep_sent[k - 1], k) for k in shifts]
    keep = (jnp.concatenate(keep_cols, axis=1) != 1).astype(F32)[:, :, None]
    own = entered_of(me, 0, cpd)
    cot_send = [block_of(flat_cot, (me + k) % narrow, 0, cpd) for k in shifts]

    held = None
    for c in range(cpd):
        here = after(info, keep) if c == 1 else info
        held = attn_fwd(c, here, own, others[c], vec, w_qkv, w_proj, held)
    cot_send = after(cot_send, others[-1])
    cot_others = [to_rank(cot_send[k - 1], k) for k in shifts]
    n1, qkv, att, lse, mid, n2 = held

    out, *rest = mlp_fwd(info, mid, n2, vec, w_fc1, bias_row, w_fc2, clips, narrow)
    out_others, h = rest[:-1], rest[-1]
    out_back = [from_rank(out_others[k - 1], k) for k in shifts]

    dmid, two_sums, fc1_sums, *halves = mlp_back(
        info, flat_cot, cot_others, h, n2, mid, att, vec, w_fc1, w_fc2, wide
    )
    z_first = (("wide", 0), ("wide", 2), ("wide", 1), ("narrow", 0))
    fc2_chain = ScatterSum(*halves[:2], wide, narrow)
    fc1_chain = ScatterSum(*halves[2:], wide, narrow, z_first)
    small = fc1_sums[0].reshape(d, ff // d)
    small = jnp.pad(small, ((0, 0), (9, 119 - small.shape[1])))

    held = None
    tok_back = []
    for c in range(cpd):
        behind = held[1] if c > 0 else two_sums
        ready = [fc2_chain.step(behind), fc1_chain.step(behind)] if c in (1, 3) else []
        if False:
            ready.append(out_back)
        if c > 1:
            tok_back[c - 2] = after(tok_back[c - 2], behind)
            ready.append(tok_back[c - 2])
        here = after(info, *ready)
        *held, = attn_back(
            c, here, own, others[c], keep, dmid, qkv, att, lse, vec, w_qkv, w_proj, held, clips
        )
        tok_back.append([from_rank(g, k) for k, g in zip(shifts, held[3:])])
        held = held[:3]
    dqkv, one_sums, grad_tokens = held
    old = (fc2_chain, fc1_chain)
    here = after(info, *[chain.step(one_sums) for chain in old])
    early = qkv_grad(0, here, n1, dqkv, wide)
    chains = [ScatterSum(*early, wide, narrow)]
    here = after(info, *[chain.step(early[0]) for chain in old])
    *halves, out, grad_tokens = qkv_grad(
        1, here, n1, dqkv, wide, (one_sums, two_sums, small, out, out_back, grad_tokens, tok_back)
    )
    x_first = (("wide", 0), ("narrow", 0), ("wide", 1), ("wide", 2))
    chains.append(ScatterSum(*halves, wide, narrow, x_first))
    sent = [chains[0].step(halves[0]), chains[1].step(halves[0])]
    grad_fc2 = fc2_chain.finish(sent)
    fc1_proj = fc1_chain.finish(sent)
    grad_fc1, grad_proj = fc1_proj[:, :ff], fc1_proj[:, ff:]
    while any(chain.sums is None for chain in chains):
        sent = [chain.step(sent) for chain in chains]
    last = jnp.concatenate([chain.finish() for chain in chains], axis=1)
    grad_qkv = last[:, : 3 * d]
    vectors = last[:, 3 * d :]
    return (
        out.reshape(tokens.shape),
        grad_tokens.reshape(tokens.shape),
        vectors[:, 0],
        vectors[:, 1:3],
        vectors[:, 3:9],
        grad_qkv,
        grad_proj,
        grad_fc1,
        vectors[:, 9 : 9 + ff // d].reshape(-1),
        grad_fc2,
    )


def solution(mesh):
    split = P("wide", None, "narrow", None)
    every = P(("wide", "narrow"))
    rows = P(("wide", "narrow"), None)
    return jax.shard_map(
        functools.partial(body, mesh.shape["wide"], mesh.shape["narrow"]),
        mesh=mesh,
        in_specs=(split, P("wide", None, "narrow"), P("wide")) + (P(),) * 8 + (split,),
        out_specs=(split, split, every, rows, rows, rows, rows, rows, every, rows),
        check_vma=False,
    )
```

```python
import functools

import jax
import jax.numpy as jnp
from jax import lax
from jax.experimental import pallas as pl
from jax.experimental.pallas import tpu as pltpu
from jax.sharding import PartitionSpec as P

HEADS = 12
EPS = 1e-06
LOG2E = 1.4426950408889634
F32 = jnp.float32
BF16 = jnp.bfloat16
MIB = 1 << 20


def dot_nn(a, b):
    return jnp.dot(a, b, preferred_element_type=F32)


def dot_nt(a, b):
    return lax.dot_general(a, b, (((1,), (1,)), ((), ())), preferred_element_type=F32)


def dot_tn(a, b):
    return lax.dot_general(a, b, (((0,), (0,)), ((), ())), preferred_element_type=F32)


def norm_stats(x):
    centred = x - jnp.mean(x, axis=-1, keepdims=True)
    rstd = lax.rsqrt(jnp.mean(centred * centred, axis=-1, keepdims=True) + EPS)
    return centred * rstd, rstd


def norm_back(grad, x, gain):
    xhat, rstd = norm_stats(x)
    scaled = grad * gain
    inner = jnp.mean(scaled * xhat, axis=-1, keepdims=True)
    outer = jnp.mean(scaled, axis=-1, keepdims=True)
    dx = rstd * (scaled - outer - xhat * inner)
    return dx, jnp.sum(grad * xhat, axis=0, keepdims=True), jnp.sum(grad, axis=0, keepdims=True)


def copies_of(pairs, sems):
    return [pltpu.make_async_copy(a, b, sems.at[i]) for i, (a, b) in enumerate(pairs)]


def row_valid(rows, piece_rows, full):
    at = lax.broadcasted_iota(jnp.int32, (rows, 1), 0) % piece_rows
    return (at < piece_rows // 2) | full


def attn_fwd_kernel(c, pieces, info, *refs):
    xs = refs[:pieces]
    vec, wqkv, wproj = refs[pieces : pieces + 3]
    made = refs[-8:-2]
    n1_o, qkv_o, att_o, lse_o, mid_o, n2_o = made
    lse_s, sems = refs[-2:]
    saves = copies_of([(m, o.at[c]) for m, o in zip(made, refs[-14:-8])], sems)
    rp, d = xs[0].shape
    rows = rp * pieces
    hw = d // HEADS
    full = info[1 + c] == 1
    for i in range(pieces):
        xhat, _ = norm_stats(xs[i][...].astype(F32))
        n1_o[i * rp : (i + 1) * rp, :] = (xhat * vec[0:1, :] + vec[6:7, :]).astype(BF16)
    saves[0].start()
    n1 = n1_o[...]
    qkv_o[:, 0:d] = (dot_nn(n1, wqkv[:, 0:d]) + vec[2:3, :]).astype(BF16)
    qkv_o[:, d : 2 * d] = dot_nn(n1, wqkv[:, d : 2 * d]).astype(BF16)
    qkv_o[:, 2 * d : 3 * d] = (dot_nn(n1, wqkv[:, 2 * d : 3 * d]) + vec[3:4, :]).astype(BF16)
    saves[1].start()
    scale2 = hw**-0.5 * LOG2E
    bias = jnp.where(row_valid(rows, rp, full), 0.0, -1e30).astype(BF16)
    lane = lax.broadcasted_iota(jnp.int32, (1, 2 * hw), 1)
    head_lane = lax.broadcasted_iota(jnp.int32, (1, 128), 1)
    lse_s[...] = jnp.zeros_like(lse_s)

    def pair(p, carry):
        at = p * 2 * hw
        q = qkv_o[:, pl.ds(at, 2 * hw)]
        k = qkv_o[:, pl.ds(d + at, 2 * hw)]
        v = qkv_o[:, pl.ds(2 * d + at, 2 * hw)]
        outs = []
        tops = []
        for e in range(2):
            mine = (lane < hw) if e == 0 else (lane >= hw)
            spare = lane == hw * (1 - e)
            one = jnp.where(spare, 1.0, 0.0).astype(BF16)
            qm = jnp.where(mine, q, one)
            km = jnp.where(spare, bias, k)
            s = dot_nt(qm, km)
            top = jnp.max(s, axis=-1, keepdims=True)
            pr = jnp.exp2((s - top) * scale2).astype(BF16)
            vm = jnp.where(mine, v, jnp.ones_like(v))
            outs.append(dot_nn(pr, vm))
            tops.append(top)
        low = lane < hw
        total = pltpu.roll(jnp.where(low, outs[1], outs[0]), hw, 1)
        att_o[:, pl.ds(at, 2 * hw)] = (jnp.where(low, outs[0], outs[1]) / total).astype(BF16)
        log_total = jnp.log2(total) + scale2 * jnp.where(low, tops[0], tops[1])
        first = jnp.broadcast_to(log_total[:, 0:1], (rows, 128))
        second = jnp.broadcast_to(log_total[:, hw : hw + 1], (rows, 128))
        lse_s[...] = jnp.where(
            head_lane == 2 * p, first, jnp.where(head_lane == 2 * p + 1, second, lse_s[...])
        )
        return carry

    for p in range(HEADS // 2):
        pair(p, 0)
    lse_o[...] = jnp.transpose(lse_s[...])[0:16, :]
    saves[2].start()
    saves[3].start()
    branch = dot_nn(att_o[...], wproj[...]) + vec[4:5, :]
    for i in range(pieces):
        part = slice(i * rp, (i + 1) * rp)
        middle = xs[i][...].astype(F32) + branch[part, :]
        mid_o[part, :] = middle.astype(BF16)
        xhat, _ = norm_stats(middle)
        n2_o[part, :] = (xhat * vec[1:2, :] + vec[7:8, :]).astype(BF16)
    saves[4].start()
    saves[5].start()
    for save in saves:
        save.wait()


def attn_fwd(c, info, own, others, vec, wqkv, wproj, held):
    cpd, rp, d = own.shape
    pieces = 1 + len(others)
    rows = rp * pieces
    whole = lambda a: pl.BlockSpec(a.shape, lambda i, s: (0,) * a.ndim)
    at_clip = lambda shape: pl.BlockSpec((None,) + shape, lambda i, s: (c, 0, 0))
    shapes = [
        ((rows, d), BF16),
        ((rows, 3 * d), BF16),
        ((rows, d), BF16),
        ((16, rows), F32),
        ((rows, d), BF16),
        ((rows, d), BF16),
    ]
    in_specs = [at_clip((rp, d))] + [whole(o) for o in others] + [whole(vec), whole(wqkv), whole(wproj)]
    operands = [own, *others, vec, wqkv, wproj]
    aliases = {}
    if held is not None:
        aliases = {1 + len(operands) + i: i for i in range(6)}
        in_specs = in_specs + [pl.BlockSpec(memory_space=pl.ANY)] * 6
        operands = operands + list(held)
    return pl.pallas_call(
        functools.partial(attn_fwd_kernel, c, pieces),
        grid_spec=pltpu.PrefetchScalarGridSpec(
            num_scalar_prefetch=1,
            grid=(1,),
            in_specs=in_specs,
            out_specs=[pl.BlockSpec(memory_space=pl.ANY)] * len(shapes),
            scratch_shapes=[pltpu.VMEM(s, t) for s, t in shapes]
            + [pltpu.VMEM((rows, 128), F32), pltpu.SemaphoreType.DMA((len(shapes),))],
        ),
        out_shape=[jax.ShapeDtypeStruct((cpd,) + s, t) for s, t in shapes],
        input_output_aliases=aliases,
        compiler_params=pltpu.CompilerParams(vmem_limit_bytes=60 * MIB),
        cost_estimate=pl.CostEstimate(
            flops=2 * rows * d * 4 * d + 16 * HEADS * rows * rows * (d // HEADS),
            bytes_accessed=rows * d * 16 + 8 * d * d,
            transcendentals=HEADS * rows * rows,
        ),
        name="attn_fwd",
    )(info, *operands)


def mlp_fwd_kernel(pieces, info, mid, n2, vec, w1, b1, w2, *outs):
    h_o = outs[pieces]
    rows, d = n2.shape
    rp = rows // pieces
    full = info[1 + pl.program_id(0)] == 1
    ff = w1.shape[1]
    chunk = d
    x = n2[...]
    acc = mid[...].astype(F32) + vec[5:6, :]
    for j in range(ff // chunk):
        part = slice(j * chunk, (j + 1) * chunk)
        h = dot_nn(x, w1[:, part]) + b1[:, part]
        h_o[:, part] = h.astype(BF16)
        act = (h * (0.5 + 0.5 * lax.erf(h * 0.7071067811865476))).astype(BF16)
        acc = acc + dot_nn(act, w2[part, :])
    out = jnp.where(row_valid(rows, rp, full), acc, 0.0).astype(BF16)
    for i in range(pieces):
        outs[i][...] = out[i * rp : (i + 1) * rp, :]


def mlp_fwd(info, mid, n2, vec, w1, b1, w2, clips, pieces):
    cpd, rows, d = n2.shape
    ff = w1.shape[1]
    rp = rows // pieces
    by_clip = lambda w: pl.BlockSpec((None, rows, w), lambda c, s: (c, 0, 0))
    once = lambda a: pl.BlockSpec(a.shape, lambda c, s: (0, 0), pipeline_mode=pl.Buffered(1))
    return pl.pallas_call(
        functools.partial(mlp_fwd_kernel, pieces),
        grid_spec=pltpu.PrefetchScalarGridSpec(
            num_scalar_prefetch=1,
            grid=(cpd,),
            in_specs=[by_clip(d), by_clip(d), once(vec), once(w1), once(b1), once(w2)],
            out_specs=[pl.BlockSpec((None, rp, d), lambda c, s: (s[0] * cpd + c, 0, 0))]
            + [pl.BlockSpec((None, rp, d), lambda c, s: (c, 0, 0))] * (pieces - 1)
            + [by_clip(ff)],
        ),
        out_shape=[jax.ShapeDtypeStruct((clips, rp, d), BF16)]
        + [jax.ShapeDtypeStruct((cpd, rp, d), BF16)] * (pieces - 1)
        + [jax.ShapeDtypeStruct((cpd, rows, ff), BF16)],
        compiler_params=pltpu.CompilerParams(vmem_limit_bytes=60 * MIB),
        cost_estimate=pl.CostEstimate(
            flops=4 * cpd * rows * d * ff,
            bytes_accessed=cpd * rows * (8 * d + 2 * ff) + 4 * d * ff,
            transcendentals=cpd * rows * ff,
        ),
        name="mlp_fwd",
    )(info, mid, n2, vec, w1, b1, w2)


def upstream_of(cots, full):
    rp = cots[0].shape[0]
    keep = row_valid(rp, rp, full)
    return jnp.concatenate(
        [jnp.where(keep, c[...].astype(F32), 0.0) for c in cots], axis=0
    )


def mlp_back_kernel(pieces, cpd, info, *refs):
    cots = refs[:pieces]
    h, n2, mid, att, vec, w1_in, w2_in = refs[pieces : pieces + 7]
    dmid_o, sums_o, fc1_sums_o, keep2, send2, keep1, send1 = refs[pieces + 7 : pieces + 14]
    w1, w2, acc1, acc2, dn2_s, up_s, turned_s, stage1, stage2, sems_in, sems1, sems2 = refs[pieces + 14 :]
    r = pl.program_id(0)
    last = r == cpd - 1
    rows, d = mid.shape
    ff = w1.shape[1]
    chunk = d
    count = ff // chunk
    unit1 = keep1.shape[1]
    unit2 = keep2.shape[1]
    per2 = chunk // (2 * unit2)
    mine = info[1 + cpd]

    def cols_of(j):
        return pl.ds(pl.multiple_of(j * chunk, chunk), chunk)

    def loads(j):
        part = cols_of(j)
        return [
            pltpu.make_async_copy(w1_in.at[:, part], w1.at[:, part], sems_in.at[0, j]),
            pltpu.make_async_copy(w2_in.at[part], w2.at[part], sems_in.at[1, j]),
        ]

    def saves1(j, slot):
        cols = cols_of(j)
        return [
            pltpu.make_async_copy(stage1.at[slot, :, side], to.at[:, :, cols], sems1.at[slot, i])
            for i, (side, to) in enumerate(((mine, keep1), (1 - mine, send1)))
        ]

    def saves2(j, slot):
        at = pl.ds(j * per2, per2)
        return [
            pltpu.make_async_copy(stage2.at[slot, :, side], to.at[at], sems2.at[slot, i])
            for i, (side, to) in enumerate(((mine, keep2), (1 - mine, send2)))
        ]

    @pl.when(r == 0)
    def _():
        for j in range(count):
            for load in loads(j):
                load.start()
        acc1[...] = jnp.zeros_like(acc1)
        acc2[...] = jnp.zeros_like(acc2)
        sums_o[...] = jnp.zeros_like(sums_o)
        fc1_sums_o[...] = jnp.zeros_like(fc1_sums_o)

    up = upstream_of(cots, info[1 + r] == 1)
    up_s[...] = up.astype(BF16)
    sums_o[2:3, :] += jnp.sum(up, axis=0, keepdims=True)
    turned_s[...] = jnp.transpose(n2[...])
    dn2_s[...] = jnp.zeros_like(dn2_s)

    def one(j, carry):
        part = cols_of(j)

        @pl.when(r == 0)
        def _():
            for load in loads(j):
                load.wait()

        pre = h[:, part].astype(F32)
        cdf = 0.5 + 0.5 * lax.erf(pre * 0.7071067811865476)
        density = 0.3989422804014327 * jnp.exp2(pre * pre * (-0.5 * LOG2E))
        act = (pre * cdf).astype(BF16)
        grad = dot_nt(up_s[...], w2[part, :])
        dh = (grad * (cdf + pre * density)).astype(BF16)
        fc1_sums_o[0:1, part] += jnp.sum(dh.astype(F32), axis=0, keepdims=True)
        acc2[part, :] += dot_tn(act, up_s[...])
        dn2_s[...] += dot_nt(dh, w1[:, part])
        acc1[:, part] += dot_nn(turned_s[...], dh)

        @pl.when(last)
        def _():
            slot = j % 2

            @pl.when(j > 1)
            def _():
                for save in saves1(j - 2, slot) + saves2(j - 2, slot):
                    save.wait()

            stage2[slot] = acc2[part, :].astype(BF16).reshape(per2, 2, unit2, d)
            stage1[slot] = acc1[:, part].astype(BF16).reshape(d // (2 * unit1), 2, unit1, chunk)
            for save in saves1(j, slot) + saves2(j, slot):
                save.start()

        return carry

    lax.fori_loop(0, count, one, 0)
    dx, gain, shift = norm_back(dn2_s[...], mid[...].astype(F32), vec[1:2, :])
    dmid = (up_s[...].astype(F32) + dx).astype(BF16)
    dmid_o[...] = dmid
    sums_o[0:1, :] += gain
    sums_o[1:2, :] += shift
    acc1[:, ff : ff + d] += dot_tn(att[...], dmid)

    @pl.when(last)
    def _():
        for j in range(max(count - 2, 0), count):
            for save in saves1(j, j % 2) + saves2(j, j % 2):
                save.wait()
        stage1[0] = acc1[:, ff : ff + d].astype(BF16).reshape(d // (2 * unit1), 2, unit1, d)
        for save in saves1(count, 0):
            save.start()
        for save in saves1(count, 0):
            save.wait()


def mlp_back(info, cot, cot_others, h, n2, mid, att, vec, w1, w2, parts):
    clips, rp, d = cot.shape
    cpd, rows, ff = h.shape
    pieces = 1 + len(cot_others)
    unit1 = d // parts
    unit2 = ff // parts
    once = lambda a: pl.BlockSpec(a.shape, lambda c, s: (0, 0), pipeline_mode=pl.Buffered(1))
    held = lambda shape: pl.BlockSpec(shape, lambda c, s: (0, 0))
    by_clip = lambda w: pl.BlockSpec((None, rows, w), lambda c, s: (c, 0, 0))
    halves = [(d // (2 * unit1), unit1, ff + d), (ff // (2 * unit2), unit2, d)]
    return pl.pallas_call(
        functools.partial(mlp_back_kernel, pieces, cpd),
        grid_spec=pltpu.PrefetchScalarGridSpec(
            num_scalar_prefetch=1,
            grid=(cpd,),
            in_specs=[pl.BlockSpec((None, rp, d), lambda c, s: (s[0] * cpd + c, 0, 0))]
            + [pl.BlockSpec((None, rp, d), lambda c, s: (c, 0, 0))] * (pieces - 1)
            + [by_clip(ff), by_clip(d), by_clip(d), by_clip(d), once(vec)]
            + [pl.BlockSpec(memory_space=pl.ANY)] * 2,
            out_specs=[by_clip(d), held((8, d)), held((8, ff))]
            + [pl.BlockSpec(memory_space=pl.ANY)] * 4,
            scratch_shapes=[
                pltpu.VMEM(w1.shape, BF16),
                pltpu.VMEM(w2.shape, BF16),
                pltpu.VMEM((d, ff + d), F32),
                pltpu.VMEM((ff, d), F32),
                pltpu.VMEM((rows, d), F32),
                pltpu.VMEM((rows, d), BF16),
                pltpu.VMEM((d, rows), BF16),
                pltpu.VMEM((2, d // (2 * unit1), 2, unit1, d), BF16),
                pltpu.VMEM((2, d // (2 * unit2), 2, unit2, d), BF16),
                pltpu.SemaphoreType.DMA((2, ff // d)),
                pltpu.SemaphoreType.DMA((2, 2)),
                pltpu.SemaphoreType.DMA((2, 2)),
            ],
        ),
        out_shape=[
            jax.ShapeDtypeStruct((cpd, rows, d), BF16),
            jax.ShapeDtypeStruct((8, d), F32),
            jax.ShapeDtypeStruct((8, ff), F32),
        ]
        + [jax.ShapeDtypeStruct(halves[1], BF16)] * 2
        + [jax.ShapeDtypeStruct(halves[0], BF16)] * 2,
        compiler_params=pltpu.CompilerParams(vmem_limit_bytes=62 * MIB),
        cost_estimate=pl.CostEstimate(
            flops=8 * cpd * rows * d * ff,
            bytes_accessed=cpd * rows * (14 * d + 2 * ff) + 8 * d * ff,
            transcendentals=2 * cpd * rows * ff,
        ),
        name="mlp_back",
    )(info, cot, *cot_others, h, n2, mid, att, vec, w1, w2)


def attn_back_kernel(c, pieces, cpd, info, *refs):
    xs = refs[:pieces]
    keep, dmid, qkv_in, att, lse, vec, wqkv_in, wproj = refs[pieces : pieces + 8]
    dqkv_o, sums_o, gtok, do_s, delta_s, dqt_s, x_s, wqkv, qkv, sems, sems_in = refs[-11:]
    dqkv_out, sums_out, own_out, *others_out = refs[-13 - pieces : -11]
    rp, d = x_s.shape[1:]
    sources = [(qkv_in.at[c], qkv), (wqkv_in, wqkv), (xs[0].at[c], x_s.at[0])]
    sources += [(x, x_s.at[1 + i]) for i, x in enumerate(xs[1:])]
    loads = copies_of(sources, sems_in)
    for load in loads:
        load.start()
    rows = rp * pieces
    hw = d // HEADS
    full = info[1 + c] == 1
    targets = [(dqkv_o, dqkv_out.at[c]), (sums_o, sums_out.at[c])]
    targets += [(gtok.at[0], own_out.at[info[0] * cpd + c])]
    targets += [(gtok.at[1 + i], o) for i, o in enumerate(others_out)]
    saves = copies_of(targets, sems)
    low_mid = dmid[...]
    do_s[...] = dot_nt(low_mid, wproj[...]).astype(BF16)
    prod = (do_s[...].astype(F32) * att[...].astype(F32)).astype(BF16)
    head_of = lax.broadcasted_iota(jnp.int32, (16, d), 1) // hw
    select = (head_of == lax.broadcasted_iota(jnp.int32, (16, d), 0)).astype(BF16)
    delta_s[...] = dot_nt(select, prod)
    loads[0].wait()
    scale = hw**-0.5
    scale2 = scale * LOG2E
    bias = jnp.where(row_valid(rows, rp, full), 0.0, -1e30).astype(BF16)
    lane = lax.broadcasted_iota(jnp.int32, (1, 2 * hw), 1)

    def pair(p, carry):
        at = p * 2 * hw
        q = qkv[:, pl.ds(at, 2 * hw)]
        k = qkv[:, pl.ds(d + at, 2 * hw)]
        v = qkv[:, pl.ds(2 * d + at, 2 * hw)]
        do = do_s[:, pl.ds(at, 2 * hw)]
        kt = jnp.transpose(k)
        zero = jnp.zeros_like(q)
        dk = dv = None
        for e in range(2):
            mine = (lane < hw) if e == 0 else (lane >= hw)
            spare = lane == hw * (1 - e)
            one = jnp.where(spare, 1.0, 0.0).astype(BF16)
            qm = jnp.where(mine, q, one)
            km = jnp.where(spare, bias, k)
            st = dot_nt(km, qm)
            pt = jnp.exp2(st * scale2 - lse[pl.ds(2 * p + e, 1), :])
            vm = jnp.where(mine, v, zero)
            dpt = dot_nt(vm, do)
            dst = (pt * (dpt - delta_s[pl.ds(2 * p + e, 1), :])).astype(BF16)
            dom = jnp.where(mine, do, zero)
            qz = jnp.where(mine, q, zero)
            dv_e = dot_nn(pt.astype(BF16), dom)
            dk_e = dot_nn(dst, qz)
            dv = dv_e if dv is None else dv + dv_e
            dk = dk_e if dk is None else dk + dk_e
            dqt_s[pl.ds(at + e * hw, hw), :] = dot_nn(
                kt[e * hw : (e + 1) * hw, :], dst
            )
        dqkv_o[:, pl.ds(d + at, 2 * hw)] = (dk * scale).astype(BF16)
        dqkv_o[:, pl.ds(2 * d + at, 2 * hw)] = dv.astype(BF16)
        return carry

    for p in range(HEADS // 2):
        pair(p, 0)
    dqkv_o[:, 0:d] = jnp.transpose((dqt_s[...] * scale).astype(BF16))
    saves[0].start()
    for load in loads[1:]:
        load.wait()
    dn1 = dot_nt(dqkv_o[...], wqkv[...])
    sums_o[...] = jnp.zeros_like(sums_o)
    sums_o[0:1, :] = jnp.sum(dqkv_o[:, 0:d].astype(F32), axis=0, keepdims=True)
    sums_o[1:2, :] = jnp.sum(dqkv_o[:, 2 * d : 3 * d].astype(F32), axis=0, keepdims=True)
    sums_o[2:3, :] = jnp.sum(low_mid.astype(F32), axis=0, keepdims=True)
    for i in range(pieces):
        part = slice(i * rp, (i + 1) * rp)
        dx, gain, shift = norm_back(dn1[part, :], x_s[i].astype(F32), vec[0:1, :])
        entered = low_mid[part, :].astype(F32) + dx
        kept = entered * keep[part, :]
        gtok[i] = kept.astype(BF16)
        saves[2 + i].start()
        sums_o[3:4, :] += gain
        sums_o[4:5, :] += shift
        sums_o[5:6, :] += jnp.sum(entered - kept, axis=0, keepdims=True)
    saves[1].start()
    for save in saves:
        save.wait()


def attn_back(c, info, own, others, keep, dmid, qkv, att, lse, vec, wqkv, wproj, held, clips):
    cpd, rp, d = own.shape
    pieces = 1 + len(others)
    rows = rp * pieces
    whole = lambda a: pl.BlockSpec(a.shape, lambda i, s: (0,) * a.ndim)
    at_clip = lambda shape: pl.BlockSpec((None,) + shape, lambda i, s: (c, 0, 0))
    in_specs = (
        [pl.BlockSpec(memory_space=pl.ANY)] * pieces
        + [
            at_clip((rows, 1)),
            at_clip((rows, d)),
            pl.BlockSpec(memory_space=pl.ANY),
            at_clip((rows, d)),
            at_clip((16, rows)),
            whole(vec),
            pl.BlockSpec(memory_space=pl.ANY),
            whole(wproj),
        ]
    )
    operands = [own, *others, keep, dmid, qkv, att, lse, vec, wqkv, wproj]
    aliases = {}
    if held is not None:
        aliases = {1 + len(operands) + i: i for i in range(3)}
        in_specs = in_specs + [pl.BlockSpec(memory_space=pl.ANY)] * 3
        operands = operands + list(held)
    return pl.pallas_call(
        functools.partial(attn_back_kernel, c, pieces, cpd),
        grid_spec=pltpu.PrefetchScalarGridSpec(
            num_scalar_prefetch=1,
            grid=(1,),
            in_specs=in_specs,
            out_specs=[pl.BlockSpec(memory_space=pl.ANY)] * (2 + pieces),
            scratch_shapes=[
                pltpu.VMEM((rows, 3 * d), BF16),
                pltpu.VMEM((8, d), F32),
                pltpu.VMEM((pieces, rp, d), BF16),
                pltpu.VMEM((rows, d), BF16),
                pltpu.VMEM((16, rows), F32),
                pltpu.VMEM((d, rows), F32),
                pltpu.VMEM((pieces, rp, d), BF16),
                pltpu.VMEM(wqkv.shape, BF16),
                pltpu.VMEM((rows, 3 * d), BF16),
                pltpu.SemaphoreType.DMA((2 + pieces,)),
                pltpu.SemaphoreType.DMA((2 + pieces,)),
            ],
        ),
        out_shape=[
            jax.ShapeDtypeStruct((cpd, rows, 3 * d), BF16),
            jax.ShapeDtypeStruct((cpd, 8, d), F32),
            jax.ShapeDtypeStruct((clips, rp, d), BF16),
        ]
        + [jax.ShapeDtypeStruct((rp, d), BF16)] * (pieces - 1),
        input_output_aliases=aliases,
        compiler_params=pltpu.CompilerParams(vmem_limit_bytes=60 * MIB),
        cost_estimate=pl.CostEstimate(
            flops=2 * rows * d * 4 * d + 40 * HEADS * rows * rows * (d // HEADS),
            bytes_accessed=rows * d * 28 + 8 * d * d,
            transcendentals=HEADS * rows * rows,
        ),
        name="attn_back",
    )(info, *operands)


def qkv_grad_kernel(n1, dqkv, info, turned_s, acc, stage, sems, keep, send):
    r = pl.program_id(0)
    per, rows, d = n1.shape
    groups, _, unit, width = stage.shape
    mine = info[1 + pl.num_programs(0) * per]
    cut = width // 256 * 128

    @pl.when(r == 0)
    def _():
        acc[...] = jnp.zeros_like(acc)

    for i in range(per):
        turned_s[:, i * rows : (i + 1) * rows] = jnp.transpose(n1[i])
    saves = []
    for at, cols in ((0, cut), (cut, width - cut)):
        part = slice(at, at + cols)
        piece = jnp.concatenate([dqkv[i, :, part] for i in range(per)], axis=0)
        acc[:, part] += dot_nn(turned_s[...], piece)
        to = pl.ds(at, cols)
        saves += [
            pltpu.make_async_copy(
                stage.at[:, side, :, to], half.at[:, :, to], sems.at[len(saves) + i]
            )
            for i, (side, half) in enumerate(((mine, keep), (1 - mine, send)))
        ]

        @pl.when(r == pl.num_programs(0) - 1)
        def _():
            stage[:, :, :, part] = acc[:, part].astype(BF16).reshape(groups, 2, unit, cols)
            for save in saves[-2:]:
                save.start()

    return saves


def early_kernel(info, n1, dqkv, keep, send, turned_s, acc, stage, sems):
    saves = qkv_grad_kernel(n1, dqkv, info, turned_s, acc, stage, sems, keep, send)

    @pl.when(pl.program_id(0) == pl.num_programs(0) - 1)
    def _():
        for save in saves:
            save.wait()


def late_kernel(cpd, narrow, moved, info, *refs):
    n1, dqkv, one_sums, two_sums, small = refs[:5]
    moving = refs[7 : 7 + moved]
    keep, send, out, tok = refs[7 + moved : 11 + moved]
    turned_s, acc, stage, sems, rows_s, tail, sems_move = refs[11 + moved : 18 + moved]
    held = refs[18 + moved :]
    r = pl.program_id(0)
    last = r == pl.num_programs(0) - 1
    groups, _, unit, width = stage.shape
    lanes = tail.shape[-1]
    mine = info[1 + cpd]
    moves, order = [], []
    for k in range(1, narrow):
        rank = lax.rem(info[0] + k, narrow)
        order.append(k - 1)
        moves.append(out.at[pl.ds(rank * cpd, cpd)])
        for c in range(cpd):
            order.append((c + 1) * (narrow - 1) + k - 1)
            moves.append(tok.at[rank * cpd + c])
    arrivals = copies_of([(moving[i], held[i]) for i in order], sems_move)
    moves = copies_of([(held[i], to) for i, to in zip(order, moves)], sems_move)

    @pl.when(r == 0)
    def _():
        for arrival in arrivals:
            arrival.start()

    ends = [
        pltpu.make_async_copy(tail.at[:, side], half.at[:, :, pl.ds(width, lanes)], sems.at[4 + i])
        for i, (side, half) in enumerate(((mine, keep), (1 - mine, send)))
    ]

    @pl.when(last)
    def _():
        for arrival in arrivals:
            arrival.wait()
        for move in moves:
            move.start()
        one_total = jnp.sum(one_sums[...], axis=0)
        rows_s[...] = jnp.zeros_like(rows_s)
        picked = [
            one_total[5:6, :],
            one_total[3:4, :],
            two_sums[0:1, :],
            one_total[0:1, :],
            one_total[1:2, :],
            one_total[2:3, :],
            two_sums[2:3, :],
            one_total[4:5, :],
            two_sums[1:2, :],
        ]
        for i, row in enumerate(picked):
            rows_s[i : i + 1, :] = row
        vectors = (jnp.transpose(rows_s[...]) + small[...]).astype(BF16)
        tail[...] = vectors.reshape(groups, 2, unit, lanes)
        for end in ends:
            end.start()

    saves = qkv_grad_kernel(n1, dqkv, info, turned_s, acc, stage, sems, keep, send)

    @pl.when(last)
    def _():
        for copy in saves + ends + moves:
            copy.wait()


def qkv_grad(which, info, n1, dqkv, parts, late=None):
    cpd, rows, d = n1.shape
    width = dqkv.shape[2] // 2
    unit = d // parts
    groups = d // (2 * unit)
    per = 2 if cpd % 2 == 0 else 1
    anywhere = pl.BlockSpec(memory_space=pl.ANY)
    held = lambda a: pl.BlockSpec(a.shape, lambda c, s: (0,) * a.ndim)
    in_specs = [
        pl.BlockSpec((per, rows, d), lambda c, s: (c, 0, 0)),
        pl.BlockSpec((per, rows, width), lambda c, s: (c, 0, which)),
    ]
    scratch = [
        pltpu.VMEM((d, per * rows), BF16),
        pltpu.VMEM((d, width), F32),
        pltpu.VMEM((groups, 2, unit, width), BF16),
        pltpu.SemaphoreType.DMA((6,)),
    ]
    operands = [n1, dqkv]
    cols, kernel, aliases, shapes = width, early_kernel, {}, []
    if late is not None:
        one_sums, two_sums, small, out, out_back, tok, tok_back = late
        moving = list(out_back) + [t for back in tok_back for t in back]
        kernel = functools.partial(late_kernel, cpd, 1 + len(out_back), len(moving))
        in_specs += [held(one_sums), held(two_sums), held(small)] + [anywhere] * (2 + len(moving))
        operands += [one_sums, two_sums, small, out, tok, *moving]
        lanes = small.shape[1]
        cols = width + lanes
        aliases = {6: 2, 7: 3}
        shapes = [jax.ShapeDtypeStruct(out.shape, BF16), jax.ShapeDtypeStruct(tok.shape, BF16)]
        scratch += [
            pltpu.VMEM((lanes, d), F32),
            pltpu.VMEM((groups, 2, unit, lanes), BF16),
            pltpu.SemaphoreType.DMA((max(len(moving), 1),)),
        ]
        scratch += [pltpu.VMEM(m.shape, BF16) for m in moving]
    shapes = [jax.ShapeDtypeStruct((groups, unit, cols), BF16)] * 2 + shapes
    return pl.pallas_call(
        kernel,
        grid_spec=pltpu.PrefetchScalarGridSpec(
            num_scalar_prefetch=1,
            grid=(cpd // per,),
            in_specs=in_specs,
            out_specs=[anywhere] * len(shapes),
            scratch_shapes=scratch,
        ),
        out_shape=shapes,
        input_output_aliases=aliases,
        compiler_params=pltpu.CompilerParams(vmem_limit_bytes=60 * MIB),
        cost_estimate=pl.CostEstimate(
            flops=2 * cpd * rows * d * width,
            bytes_accessed=2 * (cpd * rows * (d + width) + d * width),
            transcendentals=0,
        ),
        name="finish",
    )(info, *operands)


class ScatterSum:
    def __init__(self, keep, send, wide, narrow, first=(("wide", 0),)):
        rows, cols = 2 * keep.shape[0] * keep.shape[1], keep.shape[2]
        self.block = (rows // (wide * narrow), cols)
        bits_w, bits_n = wide.bit_length() - 1, narrow.bit_length() - 1
        order = [("wide", b, bits_w - 1 - b, wide) for b in range(bits_w)]
        order += [("narrow", b, bits_w + bits_n - 1 - b, narrow) for b in range(bits_n)]
        ahead = [o for key in first for o in order if o[:2] == key]
        self.order = ahead + [o for o in order if o not in ahead]
        axis, bit, dim, size = self.order.pop(0)
        shape = [2] * (bits_w + bits_n)
        shape[dim] = 1
        self.sums = None
        self.keep = keep.reshape(tuple(shape) + self.block)
        self.exchange(send.reshape(self.keep.shape), axis, bit, size)

    def exchange(self, sent, axis, bit, size):
        self.sent = sent
        self.got = lax.ppermute(sent, axis, [(i, i ^ (1 << bit)) for i in range(size)])

    def step(self, behind=None):
        if self.sums is not None:
            return self.sums
        keep, got = self.keep, self.got
        if behind is not None:
            keep = after(keep, behind)
        if not self.order:
            self.sums = keep.astype(F32) + got.astype(F32)
            return self.sums
        axis, bit, dim, size = self.order.pop(0)
        mine = (lax.axis_index(axis) >> bit) & 1

        def part(at):
            pieces = [lax.dynamic_slice_in_dim(x, at, 1, dim).astype(F32) for x in (keep, got)]
            return (pieces[0] + pieces[1]).astype(BF16)

        self.exchange(part(1 - mine), axis, bit, size)
        self.keep = part(mine)
        return self.sent

    def finish(self, behind=None):
        while self.sums is None:
            self.step(behind)
        return self.sums.reshape(self.block)


def after(value, *others):
    return lax.optimization_barrier((value, others))[0]


def body(
    wide,
    narrow,
    tokens,
    masked,
    resolution,
    mask_embed,
    gains,
    biases,
    w_qkv,
    w_proj,
    w_fc1,
    fc1_bias,
    w_fc2,
    cotangent,
):
    clips, freq_rows, cols, d = tokens.shape
    rp = freq_rows * cols
    cpd = clips // narrow
    rows = rp * narrow
    ff = w_fc1.shape[1]
    me = lax.axis_index("narrow")
    flat_tokens = tokens.reshape(clips, rp, d)
    flat_cot = cotangent.reshape(clips, rp, d)
    is_masked = masked.reshape(clips, rp) == 1

    def block_of(array, rank, at, count):
        return lax.dynamic_slice_in_dim(array, rank * cpd + at, count, 0)

    def entered_of(rank, at, count):
        return jnp.where(
            block_of(is_masked, rank, at, count)[:, :, None],
            mask_embed[None, None, :],
            block_of(flat_tokens, rank, at, count),
        )

    def to_rank(array, k):
        return lax.ppermute(array, "narrow", [(i, (i + k) % narrow) for i in range(narrow)])

    def from_rank(array, k):
        return lax.ppermute(array, "narrow", [(i, (i - k) % narrow) for i in range(narrow)])

    core = lax.axis_index("wide") & 1
    info = jnp.concatenate([me[None], block_of(resolution, me, 0, cpd), core[None]])
    vec = jnp.concatenate([gains.astype(F32).T, biases.astype(F32).T], axis=0)
    bias_row = fc1_bias.astype(F32)[None, :]

    shifts = range(1, narrow)
    others = []
    for c in range(cpd):
        send = [entered_of((me + k) % narrow, c, 1)[0] for k in shifts]
        if c > 0:
            send = after(send, others[-1])
        others.append([to_rank(send[k - 1], k) for k in shifts])
    keep_sent = [block_of(masked.reshape(clips, rp), (me + k) % narrow, 0, cpd) for k in shifts]
    keep_sent = after(keep_sent, others[0])
    keep_cols = [block_of(masked.reshape(clips, rp), me, 0, cpd)]
    keep_cols += [to_rank(keep_sent[k - 1], k) for k in shifts]
    keep = (jnp.concatenate(keep_cols, axis=1) != 1).astype(F32)[:, :, None]
    own = entered_of(me, 0, cpd)
    cot_send = [block_of(flat_cot, (me + k) % narrow, 0, cpd) for k in shifts]

    held = None
    for c in range(cpd):
        here = after(info, keep) if c == 1 else info
        held = attn_fwd(c, here, own, others[c], vec, w_qkv, w_proj, held)
    cot_send = after(cot_send, others[-1])
    cot_others = [to_rank(cot_send[k - 1], k) for k in shifts]
    n1, qkv, att, lse, mid, n2 = held

    out, *rest = mlp_fwd(info, mid, n2, vec, w_fc1, bias_row, w_fc2, clips, narrow)
    out_others, h = rest[:-1], rest[-1]
    out_back = [from_rank(out_others[k - 1], k) for k in shifts]

    dmid, two_sums, fc1_sums, *halves = mlp_back(
        info, flat_cot, cot_others, h, n2, mid, att, vec, w_fc1, w_fc2, wide
    )
    z_first = (("wide", 0), ("wide", 2), ("wide", 1), ("narrow", 0))
    fc2_chain = ScatterSum(*halves[:2], wide, narrow)
    fc1_chain = ScatterSum(*halves[2:], wide, narrow, z_first)
    small = fc1_sums[0].reshape(d, ff // d)
    small = jnp.pad(small, ((0, 0), (9, 119 - small.shape[1])))

    held = None
    tok_back = []
    for c in range(cpd):
        behind = held[1] if c > 0 else two_sums
        ready = [fc2_chain.step(behind), fc1_chain.step(behind)] if c in (1, 3) else []
        if False:
            ready.append(out_back)
        if c > 1:
            tok_back[c - 2] = after(tok_back[c - 2], behind)
            ready.append(tok_back[c - 2])
        here = after(info, *ready)
        *held, = attn_back(
            c, here, own, others[c], keep, dmid, qkv, att, lse, vec, w_qkv, w_proj, held, clips
        )
        tok_back.append([from_rank(g, k) for k, g in zip(shifts, held[3:])])
        held = held[:3]
    dqkv, one_sums, grad_tokens = held
    old = (fc2_chain, fc1_chain)
    here = after(info, *[chain.step(one_sums) for chain in old])
    early = qkv_grad(0, here, n1, dqkv, wide)
    chains = [ScatterSum(*early, wide, narrow)]
    here = after(info, *[chain.step(early[0]) for chain in old])
    *halves, out, grad_tokens = qkv_grad(
        1, here, n1, dqkv, wide, (one_sums, two_sums, small, out, out_back, grad_tokens, tok_back)
    )
    x_first = (("wide", 0), ("narrow", 0), ("wide", 1), ("wide", 2))
    chains.append(ScatterSum(*halves, wide, narrow, x_first))
    sent = [chains[0].step(halves[0]), chains[1].step(halves[0])]
    grad_fc2 = fc2_chain.finish(sent)
    fc1_proj = fc1_chain.finish(sent)
    grad_fc1, grad_proj = fc1_proj[:, :ff], fc1_proj[:, ff:]
    while any(chain.sums is None for chain in chains):
        sent = [chain.step(sent) for chain in chains]
    last = jnp.concatenate([chain.finish() for chain in chains], axis=1)
    grad_qkv = last[:, : 3 * d]
    vectors = last[:, 3 * d :]
    return (
        out.reshape(tokens.shape),
        grad_tokens.reshape(tokens.shape),
        vectors[:, 0],
        vectors[:, 1:3],
        vectors[:, 3:9],
        grad_qkv,
        grad_proj,
        grad_fc1,
        vectors[:, 9 : 9 + ff // d].reshape(-1),
        grad_fc2,
    )


def solution(mesh):
    split = P("wide", None, "narrow", None)
    every = P(("wide", "narrow"))
    rows = P(("wide", "narrow"), None)
    return jax.shard_map(
        functools.partial(body, mesh.shape["wide"], mesh.shape["narrow"]),
        mesh=mesh,
        in_specs=(split, P("wide", None, "narrow"), P("wide")) + (P(),) * 8 + (split,),
        out_specs=(split, split, every, rows, rows, rows, rows, rows, every, rows),
        check_vma=False,
    )
```

```python
import functools

import jax
import jax.numpy as jnp
from jax import lax
from jax.experimental import pallas as pl
from jax.experimental.pallas import tpu as pltpu
from jax.sharding import PartitionSpec as P

HEADS = 12
EPS = 1e-06
LOG2E = 1.4426950408889634
F32 = jnp.float32
BF16 = jnp.bfloat16
MIB = 1 << 20


def dot_nn(a, b):
    return jnp.dot(a, b, preferred_element_type=F32)


def dot_nt(a, b):
    return lax.dot_general(a, b, (((1,), (1,)), ((), ())), preferred_element_type=F32)


def dot_tn(a, b):
    return lax.dot_general(a, b, (((0,), (0,)), ((), ())), preferred_element_type=F32)


def norm_stats(x):
    centred = x - jnp.mean(x, axis=-1, keepdims=True)
    rstd = lax.rsqrt(jnp.mean(centred * centred, axis=-1, keepdims=True) + EPS)
    return centred * rstd, rstd


def norm_back(grad, x, gain):
    xhat, rstd = norm_stats(x)
    scaled = grad * gain
    inner = jnp.mean(scaled * xhat, axis=-1, keepdims=True)
    outer = jnp.mean(scaled, axis=-1, keepdims=True)
    dx = rstd * (scaled - outer - xhat * inner)
    return dx, jnp.sum(grad * xhat, axis=0, keepdims=True), jnp.sum(grad, axis=0, keepdims=True)


def copies_of(pairs, sems):
    return [pltpu.make_async_copy(a, b, sems.at[i]) for i, (a, b) in enumerate(pairs)]


def row_valid(rows, piece_rows, full):
    at = lax.broadcasted_iota(jnp.int32, (rows, 1), 0) % piece_rows
    return (at < piece_rows // 2) | full


def attn_fwd_kernel(c, pieces, info, *refs):
    xs = refs[:pieces]
    vec, wqkv, wproj = refs[pieces : pieces + 3]
    made = refs[-8:-2]
    n1_o, qkv_o, att_o, lse_o, mid_o, n2_o = made
    lse_s, sems = refs[-2:]
    saves = copies_of([(m, o.at[c]) for m, o in zip(made, refs[-14:-8])], sems)
    rp, d = xs[0].shape
    rows = rp * pieces
    hw = d // HEADS
    full = info[1 + c] == 1
    for i in range(pieces):
        xhat, _ = norm_stats(xs[i][...].astype(F32))
        n1_o[i * rp : (i + 1) * rp, :] = (xhat * vec[0:1, :] + vec[6:7, :]).astype(BF16)
    saves[0].start()
    n1 = n1_o[...]
    qkv_o[:, 0:d] = (dot_nn(n1, wqkv[:, 0:d]) + vec[2:3, :]).astype(BF16)
    qkv_o[:, d : 2 * d] = dot_nn(n1, wqkv[:, d : 2 * d]).astype(BF16)
    qkv_o[:, 2 * d : 3 * d] = (dot_nn(n1, wqkv[:, 2 * d : 3 * d]) + vec[3:4, :]).astype(BF16)
    saves[1].start()
    scale2 = hw**-0.5 * LOG2E
    bias = jnp.where(row_valid(rows, rp, full), 0.0, -1e30).astype(BF16)
    lane = lax.broadcasted_iota(jnp.int32, (1, 2 * hw), 1)
    head_lane = lax.broadcasted_iota(jnp.int32, (1, 128), 1)
    lse_s[...] = jnp.zeros_like(lse_s)

    def pair(p, carry):
        at = p * 2 * hw
        q = qkv_o[:, pl.ds(at, 2 * hw)]
        k = qkv_o[:, pl.ds(d + at, 2 * hw)]
        v = qkv_o[:, pl.ds(2 * d + at, 2 * hw)]
        outs = []
        tops = []
        for e in range(2):
            mine = (lane < hw) if e == 0 else (lane >= hw)
            spare = lane == hw * (1 - e)
            one = jnp.where(spare, 1.0, 0.0).astype(BF16)
            qm = jnp.where(mine, q, one)
            km = jnp.where(spare, bias, k)
            s = dot_nt(qm, km)
            top = jnp.max(s, axis=-1, keepdims=True)
            pr = jnp.exp2((s - top) * scale2).astype(BF16)
            vm = jnp.where(mine, v, jnp.ones_like(v))
            outs.append(dot_nn(pr, vm))
            tops.append(top)
        low = lane < hw
        total = pltpu.roll(jnp.where(low, outs[1], outs[0]), hw, 1)
        att_o[:, pl.ds(at, 2 * hw)] = (jnp.where(low, outs[0], outs[1]) / total).astype(BF16)
        log_total = jnp.log2(total) + scale2 * jnp.where(low, tops[0], tops[1])
        first = jnp.broadcast_to(log_total[:, 0:1], (rows, 128))
        second = jnp.broadcast_to(log_total[:, hw : hw + 1], (rows, 128))
        lse_s[...] = jnp.where(
            head_lane == 2 * p, first, jnp.where(head_lane == 2 * p + 1, second, lse_s[...])
        )
        return carry

    for p in range(HEADS // 2):
        pair(p, 0)
    lse_o[...] = jnp.transpose(lse_s[...])[0:16, :]
    saves[2].start()
    saves[3].start()
    branch = dot_nn(att_o[...], wproj[...]) + vec[4:5, :]
    for i in range(pieces):
        part = slice(i * rp, (i + 1) * rp)
        middle = xs[i][...].astype(F32) + branch[part, :]
        mid_o[part, :] = middle.astype(BF16)
        xhat, _ = norm_stats(middle)
        n2_o[part, :] = (xhat * vec[1:2, :] + vec[7:8, :]).astype(BF16)
    saves[4].start()
    saves[5].start()
    for save in saves:
        save.wait()


def attn_fwd(c, info, own, others, vec, wqkv, wproj, held):
    cpd, rp, d = own.shape
    pieces = 1 + len(others)
    rows = rp * pieces
    whole = lambda a: pl.BlockSpec(a.shape, lambda i, s: (0,) * a.ndim)
    at_clip = lambda shape: pl.BlockSpec((None,) + shape, lambda i, s: (c, 0, 0))
    shapes = [
        ((rows, d), BF16),
        ((rows, 3 * d), BF16),
        ((rows, d), BF16),
        ((16, rows), F32),
        ((rows, d), BF16),
        ((rows, d), BF16),
    ]
    in_specs = [at_clip((rp, d))] + [whole(o) for o in others] + [whole(vec), whole(wqkv), whole(wproj)]
    operands = [own, *others, vec, wqkv, wproj]
    aliases = {}
    if held is not None:
        aliases = {1 + len(operands) + i: i for i in range(6)}
        in_specs = in_specs + [pl.BlockSpec(memory_space=pl.ANY)] * 6
        operands = operands + list(held)
    return pl.pallas_call(
        functools.partial(attn_fwd_kernel, c, pieces),
        grid_spec=pltpu.PrefetchScalarGridSpec(
            num_scalar_prefetch=1,
            grid=(1,),
            in_specs=in_specs,
            out_specs=[pl.BlockSpec(memory_space=pl.ANY)] * len(shapes),
            scratch_shapes=[pltpu.VMEM(s, t) for s, t in shapes]
            + [pltpu.VMEM((rows, 128), F32), pltpu.SemaphoreType.DMA((len(shapes),))],
        ),
        out_shape=[jax.ShapeDtypeStruct((cpd,) + s, t) for s, t in shapes],
        input_output_aliases=aliases,
        compiler_params=pltpu.CompilerParams(vmem_limit_bytes=60 * MIB),
        cost_estimate=pl.CostEstimate(
            flops=2 * rows * d * 4 * d + 16 * HEADS * rows * rows * (d // HEADS),
            bytes_accessed=rows * d * 16 + 8 * d * d,
            transcendentals=HEADS * rows * rows,
        ),
        name="attn_fwd",
    )(info, *operands)


def mlp_fwd_kernel(pieces, info, mid, n2, vec, w1, b1, w2, *outs):
    h_o = outs[pieces]
    rows, d = n2.shape
    rp = rows // pieces
    full = info[1 + pl.program_id(0)] == 1
    ff = w1.shape[1]
    chunk = d
    x = n2[...]
    acc = mid[...].astype(F32) + vec[5:6, :]
    for j in range(ff // chunk):
        part = slice(j * chunk, (j + 1) * chunk)
        h = dot_nn(x, w1[:, part]) + b1[:, part]
        h_o[:, part] = h.astype(BF16)
        act = (h * (0.5 + 0.5 * lax.erf(h * 0.7071067811865476))).astype(BF16)
        acc = acc + dot_nn(act, w2[part, :])
    out = jnp.where(row_valid(rows, rp, full), acc, 0.0).astype(BF16)
    for i in range(pieces):
        outs[i][...] = out[i * rp : (i + 1) * rp, :]


def mlp_fwd(info, mid, n2, vec, w1, b1, w2, clips, pieces):
    cpd, rows, d = n2.shape
    ff = w1.shape[1]
    rp = rows // pieces
    by_clip = lambda w: pl.BlockSpec((None, rows, w), lambda c, s: (c, 0, 0))
    once = lambda a: pl.BlockSpec(a.shape, lambda c, s: (0, 0), pipeline_mode=pl.Buffered(1))
    return pl.pallas_call(
        functools.partial(mlp_fwd_kernel, pieces),
        grid_spec=pltpu.PrefetchScalarGridSpec(
            num_scalar_prefetch=1,
            grid=(cpd,),
            in_specs=[by_clip(d), by_clip(d), once(vec), once(w1), once(b1), once(w2)],
            out_specs=[pl.BlockSpec((None, rp, d), lambda c, s: (s[0] * cpd + c, 0, 0))]
            + [pl.BlockSpec((None, rp, d), lambda c, s: (c, 0, 0))] * (pieces - 1)
            + [by_clip(ff)],
        ),
        out_shape=[jax.ShapeDtypeStruct((clips, rp, d), BF16)]
        + [jax.ShapeDtypeStruct((cpd, rp, d), BF16)] * (pieces - 1)
        + [jax.ShapeDtypeStruct((cpd, rows, ff), BF16)],
        compiler_params=pltpu.CompilerParams(vmem_limit_bytes=60 * MIB),
        cost_estimate=pl.CostEstimate(
            flops=4 * cpd * rows * d * ff,
            bytes_accessed=cpd * rows * (8 * d + 2 * ff) + 4 * d * ff,
            transcendentals=cpd * rows * ff,
        ),
        name="mlp_fwd",
    )(info, mid, n2, vec, w1, b1, w2)


def upstream_of(cots, full):
    rp = cots[0].shape[0]
    keep = row_valid(rp, rp, full)
    return jnp.concatenate(
        [jnp.where(keep, c[...].astype(F32), 0.0) for c in cots], axis=0
    )


def mlp_back_kernel(pieces, cpd, info, *refs):
    cots = refs[:pieces]
    h, n2, mid, att, vec, w1_in, w2_in = refs[pieces : pieces + 7]
    dmid_o, sums_o, fc1_sums_o, keep2, send2, keep1, send1 = refs[pieces + 7 : pieces + 14]
    w1, w2, acc1, acc2, dn2_s, up_s, turned_s, stage1, stage2, sems_in, sems1, sems2 = refs[pieces + 14 :]
    r = pl.program_id(0)
    last = r == cpd - 1
    rows, d = mid.shape
    ff = w1.shape[1]
    chunk = d
    count = ff // chunk
    unit1 = keep1.shape[1]
    unit2 = keep2.shape[1]
    per2 = chunk // (2 * unit2)
    mine = info[1 + cpd]

    def cols_of(j):
        return pl.ds(pl.multiple_of(j * chunk, chunk), chunk)

    def loads(j):
        part = cols_of(j)
        return [
            pltpu.make_async_copy(w1_in.at[:, part], w1.at[:, part], sems_in.at[0, j]),
            pltpu.make_async_copy(w2_in.at[part], w2.at[part], sems_in.at[1, j]),
        ]

    def saves1(j, slot):
        cols = cols_of(j)
        return [
            pltpu.make_async_copy(stage1.at[slot, :, side], to.at[:, :, cols], sems1.at[slot, i])
            for i, (side, to) in enumerate(((mine, keep1), (1 - mine, send1)))
        ]

    def saves2(j, slot):
        at = pl.ds(j * per2, per2)
        return [
            pltpu.make_async_copy(stage2.at[slot, :, side], to.at[at], sems2.at[slot, i])
            for i, (side, to) in enumerate(((mine, keep2), (1 - mine, send2)))
        ]

    @pl.when(r == 0)
    def _():
        for j in range(count):
            for load in loads(j):
                load.start()
        acc1[...] = jnp.zeros_like(acc1)
        acc2[...] = jnp.zeros_like(acc2)
        sums_o[...] = jnp.zeros_like(sums_o)
        fc1_sums_o[...] = jnp.zeros_like(fc1_sums_o)

    up = upstream_of(cots, info[1 + r] == 1)
    up_s[...] = up.astype(BF16)
    sums_o[2:3, :] += jnp.sum(up, axis=0, keepdims=True)
    turned_s[...] = jnp.transpose(n2[...])
    dn2_s[...] = jnp.zeros_like(dn2_s)

    def one(j, carry):
        part = cols_of(j)

        @pl.when(r == 0)
        def _():
            for load in loads(j):
                load.wait()

        pre = h[:, part].astype(F32)
        cdf = 0.5 + 0.5 * lax.erf(pre * 0.7071067811865476)
        density = 0.3989422804014327 * jnp.exp2(pre * pre * (-0.5 * LOG2E))
        act = (pre * cdf).astype(BF16)
        grad = dot_nt(up_s[...], w2[part, :])
        dh = (grad * (cdf + pre * density)).astype(BF16)
        fc1_sums_o[0:1, part] += jnp.sum(dh.astype(F32), axis=0, keepdims=True)
        acc2[part, :] += dot_tn(act, up_s[...])
        dn2_s[...] += dot_nt(dh, w1[:, part])
        acc1[:, part] += dot_nn(turned_s[...], dh)

        @pl.when(last)
        def _():
            slot = j % 2

            @pl.when(j > 1)
            def _():
                for save in saves1(j - 2, slot) + saves2(j - 2, slot):
                    save.wait()

            stage2[slot] = acc2[part, :].astype(BF16).reshape(per2, 2, unit2, d)
            stage1[slot] = acc1[:, part].astype(BF16).reshape(d // (2 * unit1), 2, unit1, chunk)
            for save in saves1(j, slot) + saves2(j, slot):
                save.start()

        return carry

    lax.fori_loop(0, count, one, 0, unroll=2)
    dx, gain, shift = norm_back(dn2_s[...], mid[...].astype(F32), vec[1:2, :])
    dmid = (up_s[...].astype(F32) + dx).astype(BF16)
    dmid_o[...] = dmid
    sums_o[0:1, :] += gain
    sums_o[1:2, :] += shift
    acc1[:, ff : ff + d] += dot_tn(att[...], dmid)

    @pl.when(last)
    def _():
        for j in range(max(count - 2, 0), count):
            for save in saves1(j, j % 2) + saves2(j, j % 2):
                save.wait()
        stage1[0] = acc1[:, ff : ff + d].astype(BF16).reshape(d // (2 * unit1), 2, unit1, d)
        for save in saves1(count, 0):
            save.start()
        for save in saves1(count, 0):
            save.wait()


def mlp_back(info, cot, cot_others, h, n2, mid, att, vec, w1, w2, parts):
    clips, rp, d = cot.shape
    cpd, rows, ff = h.shape
    pieces = 1 + len(cot_others)
    unit1 = d // parts
    unit2 = ff // parts
    once = lambda a: pl.BlockSpec(a.shape, lambda c, s: (0, 0), pipeline_mode=pl.Buffered(1))
    held = lambda shape: pl.BlockSpec(shape, lambda c, s: (0, 0))
    by_clip = lambda w: pl.BlockSpec((None, rows, w), lambda c, s: (c, 0, 0))
    halves = [(d // (2 * unit1), unit1, ff + d), (ff // (2 * unit2), unit2, d)]
    return pl.pallas_call(
        functools.partial(mlp_back_kernel, pieces, cpd),
        grid_spec=pltpu.PrefetchScalarGridSpec(
            num_scalar_prefetch=1,
            grid=(cpd,),
            in_specs=[pl.BlockSpec((None, rp, d), lambda c, s: (s[0] * cpd + c, 0, 0))]
            + [pl.BlockSpec((None, rp, d), lambda c, s: (c, 0, 0))] * (pieces - 1)
            + [by_clip(ff), by_clip(d), by_clip(d), by_clip(d), once(vec)]
            + [pl.BlockSpec(memory_space=pl.ANY)] * 2,
            out_specs=[by_clip(d), held((8, d)), held((8, ff))]
            + [pl.BlockSpec(memory_space=pl.ANY)] * 4,
            scratch_shapes=[
                pltpu.VMEM(w1.shape, BF16),
                pltpu.VMEM(w2.shape, BF16),
                pltpu.VMEM((d, ff + d), F32),
                pltpu.VMEM((ff, d), F32),
                pltpu.VMEM((rows, d), F32),
                pltpu.VMEM((rows, d), BF16),
                pltpu.VMEM((d, rows), BF16),
                pltpu.VMEM((2, d // (2 * unit1), 2, unit1, d), BF16),
                pltpu.VMEM((2, d // (2 * unit2), 2, unit2, d), BF16),
                pltpu.SemaphoreType.DMA((2, ff // d)),
                pltpu.SemaphoreType.DMA((2, 2)),
                pltpu.SemaphoreType.DMA((2, 2)),
            ],
        ),
        out_shape=[
            jax.ShapeDtypeStruct((cpd, rows, d), BF16),
            jax.ShapeDtypeStruct((8, d), F32),
            jax.ShapeDtypeStruct((8, ff), F32),
        ]
        + [jax.ShapeDtypeStruct(halves[1], BF16)] * 2
        + [jax.ShapeDtypeStruct(halves[0], BF16)] * 2,
        compiler_params=pltpu.CompilerParams(vmem_limit_bytes=62 * MIB),
        cost_estimate=pl.CostEstimate(
            flops=8 * cpd * rows * d * ff,
            bytes_accessed=cpd * rows * (14 * d + 2 * ff) + 8 * d * ff,
            transcendentals=2 * cpd * rows * ff,
        ),
        name="mlp_back",
    )(info, cot, *cot_others, h, n2, mid, att, vec, w1, w2)


def attn_back_kernel(c, pieces, cpd, info, *refs):
    xs = refs[:pieces]
    keep, dmid, qkv_in, att, lse, vec, wqkv_in, wproj = refs[pieces : pieces + 8]
    dqkv_o, sums_o, gtok, do_s, delta_s, dqt_s, x_s, wqkv, qkv, sems, sems_in = refs[-11:]
    dqkv_out, sums_out, own_out, *others_out = refs[-13 - pieces : -11]
    rp, d = x_s.shape[1:]
    sources = [(qkv_in.at[c], qkv), (wqkv_in, wqkv), (xs[0].at[c], x_s.at[0])]
    sources += [(x, x_s.at[1 + i]) for i, x in enumerate(xs[1:])]
    loads = copies_of(sources, sems_in)
    for load in loads:
        load.start()
    rows = rp * pieces
    hw = d // HEADS
    full = info[1 + c] == 1
    targets = [(dqkv_o, dqkv_out.at[c]), (sums_o, sums_out.at[c])]
    targets += [(gtok.at[0], own_out.at[info[0] * cpd + c])]
    targets += [(gtok.at[1 + i], o) for i, o in enumerate(others_out)]
    saves = copies_of(targets, sems)
    low_mid = dmid[...]
    do_s[...] = dot_nt(low_mid, wproj[...]).astype(BF16)
    prod = (do_s[...].astype(F32) * att[...].astype(F32)).astype(BF16)
    head_of = lax.broadcasted_iota(jnp.int32, (16, d), 1) // hw
    select = (head_of == lax.broadcasted_iota(jnp.int32, (16, d), 0)).astype(BF16)
    delta_s[...] = dot_nt(select, prod)
    loads[0].wait()
    scale = hw**-0.5
    scale2 = scale * LOG2E
    bias = jnp.where(row_valid(rows, rp, full), 0.0, -1e30).astype(BF16)
    lane = lax.broadcasted_iota(jnp.int32, (1, 2 * hw), 1)

    def pair(p, carry):
        at = p * 2 * hw
        q = qkv[:, pl.ds(at, 2 * hw)]
        k = qkv[:, pl.ds(d + at, 2 * hw)]
        v = qkv[:, pl.ds(2 * d + at, 2 * hw)]
        do = do_s[:, pl.ds(at, 2 * hw)]
        kt = jnp.transpose(k)
        zero = jnp.zeros_like(q)
        dk = dv = None
        for e in range(2):
            mine = (lane < hw) if e == 0 else (lane >= hw)
            spare = lane == hw * (1 - e)
            one = jnp.where(spare, 1.0, 0.0).astype(BF16)
            qm = jnp.where(mine, q, one)
            km = jnp.where(spare, bias, k)
            st = dot_nt(km, qm)
            pt = jnp.exp2(st * scale2 - lse[pl.ds(2 * p + e, 1), :])
            vm = jnp.where(mine, v, zero)
            dpt = dot_nt(vm, do)
            dst = (pt * (dpt - delta_s[pl.ds(2 * p + e, 1), :])).astype(BF16)
            dom = jnp.where(mine, do, zero)
            qz = jnp.where(mine, q, zero)
            dv_e = dot_nn(pt.astype(BF16), dom)
            dk_e = dot_nn(dst, qz)
            dv = dv_e if dv is None else dv + dv_e
            dk = dk_e if dk is None else dk + dk_e
            dqt_s[pl.ds(at + e * hw, hw), :] = dot_nn(
                kt[e * hw : (e + 1) * hw, :], dst
            )
        dqkv_o[:, pl.ds(d + at, 2 * hw)] = (dk * scale).astype(BF16)
        dqkv_o[:, pl.ds(2 * d + at, 2 * hw)] = dv.astype(BF16)
        return carry

    for p in range(HEADS // 2):
        pair(p, 0)
    dqkv_o[:, 0:d] = jnp.transpose((dqt_s[...] * scale).astype(BF16))
    saves[0].start()
    for load in loads[1:]:
        load.wait()
    dn1 = dot_nt(dqkv_o[...], wqkv[...])
    sums_o[...] = jnp.zeros_like(sums_o)
    sums_o[0:1, :] = jnp.sum(dqkv_o[:, 0:d].astype(F32), axis=0, keepdims=True)
    sums_o[1:2, :] = jnp.sum(dqkv_o[:, 2 * d : 3 * d].astype(F32), axis=0, keepdims=True)
    sums_o[2:3, :] = jnp.sum(low_mid.astype(F32), axis=0, keepdims=True)
    for i in range(pieces):
        part = slice(i * rp, (i + 1) * rp)
        dx, gain, shift = norm_back(dn1[part, :], x_s[i].astype(F32), vec[0:1, :])
        entered = low_mid[part, :].astype(F32) + dx
        kept = entered * keep[part, :]
        gtok[i] = kept.astype(BF16)
        saves[2 + i].start()
        sums_o[3:4, :] += gain
        sums_o[4:5, :] += shift
        sums_o[5:6, :] += jnp.sum(entered - kept, axis=0, keepdims=True)
    saves[1].start()
    for save in saves:
        save.wait()


def attn_back(c, info, own, others, keep, dmid, qkv, att, lse, vec, wqkv, wproj, held, clips):
    cpd, rp, d = own.shape
    pieces = 1 + len(others)
    rows = rp * pieces
    whole = lambda a: pl.BlockSpec(a.shape, lambda i, s: (0,) * a.ndim)
    at_clip = lambda shape: pl.BlockSpec((None,) + shape, lambda i, s: (c, 0, 0))
    in_specs = (
        [pl.BlockSpec(memory_space=pl.ANY)] * pieces
        + [
            at_clip((rows, 1)),
            at_clip((rows, d)),
            pl.BlockSpec(memory_space=pl.ANY),
            at_clip((rows, d)),
            at_clip((16, rows)),
            whole(vec),
            pl.BlockSpec(memory_space=pl.ANY),
            whole(wproj),
        ]
    )
    operands = [own, *others, keep, dmid, qkv, att, lse, vec, wqkv, wproj]
    aliases = {}
    if held is not None:
        aliases = {1 + len(operands) + i: i for i in range(3)}
        in_specs = in_specs + [pl.BlockSpec(memory_space=pl.ANY)] * 3
        operands = operands + list(held)
    return pl.pallas_call(
        functools.partial(attn_back_kernel, c, pieces, cpd),
        grid_spec=pltpu.PrefetchScalarGridSpec(
            num_scalar_prefetch=1,
            grid=(1,),
            in_specs=in_specs,
            out_specs=[pl.BlockSpec(memory_space=pl.ANY)] * (2 + pieces),
            scratch_shapes=[
                pltpu.VMEM((rows, 3 * d), BF16),
                pltpu.VMEM((8, d), F32),
                pltpu.VMEM((pieces, rp, d), BF16),
                pltpu.VMEM((rows, d), BF16),
                pltpu.VMEM((16, rows), F32),
                pltpu.VMEM((d, rows), F32),
                pltpu.VMEM((pieces, rp, d), BF16),
                pltpu.VMEM(wqkv.shape, BF16),
                pltpu.VMEM((rows, 3 * d), BF16),
                pltpu.SemaphoreType.DMA((2 + pieces,)),
                pltpu.SemaphoreType.DMA((2 + pieces,)),
            ],
        ),
        out_shape=[
            jax.ShapeDtypeStruct((cpd, rows, 3 * d), BF16),
            jax.ShapeDtypeStruct((cpd, 8, d), F32),
            jax.ShapeDtypeStruct((clips, rp, d), BF16),
        ]
        + [jax.ShapeDtypeStruct((rp, d), BF16)] * (pieces - 1),
        input_output_aliases=aliases,
        compiler_params=pltpu.CompilerParams(vmem_limit_bytes=60 * MIB),
        cost_estimate=pl.CostEstimate(
            flops=2 * rows * d * 4 * d + 40 * HEADS * rows * rows * (d // HEADS),
            bytes_accessed=rows * d * 28 + 8 * d * d,
            transcendentals=HEADS * rows * rows,
        ),
        name="attn_back",
    )(info, *operands)


def qkv_grad_kernel(n1, dqkv, info, turned_s, acc, stage, sems, keep, send):
    r = pl.program_id(0)
    per, rows, d = n1.shape
    groups, _, unit, width = stage.shape
    mine = info[1 + pl.num_programs(0) * per]
    cut = width // 256 * 128

    @pl.when(r == 0)
    def _():
        acc[...] = jnp.zeros_like(acc)

    for i in range(per):
        turned_s[:, i * rows : (i + 1) * rows] = jnp.transpose(n1[i])
    saves = []
    for at, cols in ((0, cut), (cut, width - cut)):
        part = slice(at, at + cols)
        piece = jnp.concatenate([dqkv[i, :, part] for i in range(per)], axis=0)
        acc[:, part] += dot_nn(turned_s[...], piece)
        to = pl.ds(at, cols)
        saves += [
            pltpu.make_async_copy(
                stage.at[:, side, :, to], half.at[:, :, to], sems.at[len(saves) + i]
            )
            for i, (side, half) in enumerate(((mine, keep), (1 - mine, send)))
        ]

        @pl.when(r == pl.num_programs(0) - 1)
        def _():
            stage[:, :, :, part] = acc[:, part].astype(BF16).reshape(groups, 2, unit, cols)
            for save in saves[-2:]:
                save.start()

    return saves


def early_kernel(info, n1, dqkv, keep, send, turned_s, acc, stage, sems):
    saves = qkv_grad_kernel(n1, dqkv, info, turned_s, acc, stage, sems, keep, send)

    @pl.when(pl.program_id(0) == pl.num_programs(0) - 1)
    def _():
        for save in saves:
            save.wait()


def late_kernel(cpd, narrow, moved, info, *refs):
    n1, dqkv, one_sums, two_sums, small = refs[:5]
    moving = refs[7 : 7 + moved]
    keep, send, out, tok = refs[7 + moved : 11 + moved]
    turned_s, acc, stage, sems, rows_s, tail, sems_move = refs[11 + moved : 18 + moved]
    held = refs[18 + moved :]
    r = pl.program_id(0)
    last = r == pl.num_programs(0) - 1
    groups, _, unit, width = stage.shape
    lanes = tail.shape[-1]
    mine = info[1 + cpd]
    moves, order = [], []
    for k in range(1, narrow):
        rank = lax.rem(info[0] + k, narrow)
        order.append(k - 1)
        moves.append(out.at[pl.ds(rank * cpd, cpd)])
        for c in range(cpd):
            order.append((c + 1) * (narrow - 1) + k - 1)
            moves.append(tok.at[rank * cpd + c])
    arrivals = copies_of([(moving[i], held[i]) for i in order], sems_move)
    moves = copies_of([(held[i], to) for i, to in zip(order, moves)], sems_move)

    @pl.when(r == 0)
    def _():
        for arrival in arrivals:
            arrival.start()

    ends = [
        pltpu.make_async_copy(tail.at[:, side], half.at[:, :, pl.ds(width, lanes)], sems.at[4 + i])
        for i, (side, half) in enumerate(((mine, keep), (1 - mine, send)))
    ]

    @pl.when(last)
    def _():
        for arrival in arrivals:
            arrival.wait()
        for move in moves:
            move.start()
        one_total = jnp.sum(one_sums[...], axis=0)
        rows_s[...] = jnp.zeros_like(rows_s)
        picked = [
            one_total[5:6, :],
            one_total[3:4, :],
            two_sums[0:1, :],
            one_total[0:1, :],
            one_total[1:2, :],
            one_total[2:3, :],
            two_sums[2:3, :],
            one_total[4:5, :],
            two_sums[1:2, :],
        ]
        for i, row in enumerate(picked):
            rows_s[i : i + 1, :] = row
        vectors = (jnp.transpose(rows_s[...]) + small[...]).astype(BF16)
        tail[...] = vectors.reshape(groups, 2, unit, lanes)
        for end in ends:
            end.start()

    saves = qkv_grad_kernel(n1, dqkv, info, turned_s, acc, stage, sems, keep, send)

    @pl.when(last)
    def _():
        for copy in saves + ends + moves:
            copy.wait()


def qkv_grad(which, info, n1, dqkv, parts, late=None):
    cpd, rows, d = n1.shape
    width = dqkv.shape[2] // 2
    unit = d // parts
    groups = d // (2 * unit)
    per = 2 if cpd % 2 == 0 else 1
    anywhere = pl.BlockSpec(memory_space=pl.ANY)
    held = lambda a: pl.BlockSpec(a.shape, lambda c, s: (0,) * a.ndim)
    in_specs = [
        pl.BlockSpec((per, rows, d), lambda c, s: (c, 0, 0)),
        pl.BlockSpec((per, rows, width), lambda c, s: (c, 0, which)),
    ]
    scratch = [
        pltpu.VMEM((d, per * rows), BF16),
        pltpu.VMEM((d, width), F32),
        pltpu.VMEM((groups, 2, unit, width), BF16),
        pltpu.SemaphoreType.DMA((6,)),
    ]
    operands = [n1, dqkv]
    cols, kernel, aliases, shapes = width, early_kernel, {}, []
    if late is not None:
        one_sums, two_sums, small, out, out_back, tok, tok_back = late
        moving = list(out_back) + [t for back in tok_back for t in back]
        kernel = functools.partial(late_kernel, cpd, 1 + len(out_back), len(moving))
        in_specs += [held(one_sums), held(two_sums), held(small)] + [anywhere] * (2 + len(moving))
        operands += [one_sums, two_sums, small, out, tok, *moving]
        lanes = small.shape[1]
        cols = width + lanes
        aliases = {6: 2, 7: 3}
        shapes = [jax.ShapeDtypeStruct(out.shape, BF16), jax.ShapeDtypeStruct(tok.shape, BF16)]
        scratch += [
            pltpu.VMEM((lanes, d), F32),
            pltpu.VMEM((groups, 2, unit, lanes), BF16),
            pltpu.SemaphoreType.DMA((max(len(moving), 1),)),
        ]
        scratch += [pltpu.VMEM(m.shape, BF16) for m in moving]
    shapes = [jax.ShapeDtypeStruct((groups, unit, cols), BF16)] * 2 + shapes
    return pl.pallas_call(
        kernel,
        grid_spec=pltpu.PrefetchScalarGridSpec(
            num_scalar_prefetch=1,
            grid=(cpd // per,),
            in_specs=in_specs,
            out_specs=[anywhere] * len(shapes),
            scratch_shapes=scratch,
        ),
        out_shape=shapes,
        input_output_aliases=aliases,
        compiler_params=pltpu.CompilerParams(vmem_limit_bytes=60 * MIB),
        cost_estimate=pl.CostEstimate(
            flops=2 * cpd * rows * d * width,
            bytes_accessed=2 * (cpd * rows * (d + width) + d * width),
            transcendentals=0,
        ),
        name="finish",
    )(info, *operands)


class ScatterSum:
    def __init__(self, keep, send, wide, narrow, first=(("wide", 0),)):
        rows, cols = 2 * keep.shape[0] * keep.shape[1], keep.shape[2]
        self.block = (rows // (wide * narrow), cols)
        bits_w, bits_n = wide.bit_length() - 1, narrow.bit_length() - 1
        order = [("wide", b, bits_w - 1 - b, wide) for b in range(bits_w)]
        order += [("narrow", b, bits_w + bits_n - 1 - b, narrow) for b in range(bits_n)]
        ahead = [o for key in first for o in order if o[:2] == key]
        self.order = ahead + [o for o in order if o not in ahead]
        axis, bit, dim, size = self.order.pop(0)
        shape = [2] * (bits_w + bits_n)
        shape[dim] = 1
        self.sums = None
        self.keep = keep.reshape(tuple(shape) + self.block)
        self.exchange(send.reshape(self.keep.shape), axis, bit, size)

    def exchange(self, sent, axis, bit, size):
        self.sent = sent
        self.got = lax.ppermute(sent, axis, [(i, i ^ (1 << bit)) for i in range(size)])

    def step(self, behind=None):
        if self.sums is not None:
            return self.sums
        keep, got = self.keep, self.got
        if behind is not None:
            keep = after(keep, behind)
        if not self.order:
            self.sums = keep.astype(F32) + got.astype(F32)
            return self.sums
        axis, bit, dim, size = self.order.pop(0)
        mine = (lax.axis_index(axis) >> bit) & 1

        def part(at):
            pieces = [lax.dynamic_slice_in_dim(x, at, 1, dim).astype(F32) for x in (keep, got)]
            return (pieces[0] + pieces[1]).astype(BF16)

        self.exchange(part(1 - mine), axis, bit, size)
        self.keep = part(mine)
        return self.sent

    def finish(self, behind=None):
        while self.sums is None:
            self.step(behind)
        return self.sums.reshape(self.block)


def after(value, *others):
    return lax.optimization_barrier((value, others))[0]


def body(
    wide,
    narrow,
    tokens,
    masked,
    resolution,
    mask_embed,
    gains,
    biases,
    w_qkv,
    w_proj,
    w_fc1,
    fc1_bias,
    w_fc2,
    cotangent,
):
    clips, freq_rows, cols, d = tokens.shape
    rp = freq_rows * cols
    cpd = clips // narrow
    rows = rp * narrow
    ff = w_fc1.shape[1]
    me = lax.axis_index("narrow")
    flat_tokens = tokens.reshape(clips, rp, d)
    flat_cot = cotangent.reshape(clips, rp, d)
    is_masked = masked.reshape(clips, rp) == 1

    def block_of(array, rank, at, count):
        return lax.dynamic_slice_in_dim(array, rank * cpd + at, count, 0)

    def entered_of(rank, at, count):
        return jnp.where(
            block_of(is_masked, rank, at, count)[:, :, None],
            mask_embed[None, None, :],
            block_of(flat_tokens, rank, at, count),
        )

    def to_rank(array, k):
        return lax.ppermute(array, "narrow", [(i, (i + k) % narrow) for i in range(narrow)])

    def from_rank(array, k):
        return lax.ppermute(array, "narrow", [(i, (i - k) % narrow) for i in range(narrow)])

    core = lax.axis_index("wide") & 1
    info = jnp.concatenate([me[None], block_of(resolution, me, 0, cpd), core[None]])
    vec = jnp.concatenate([gains.astype(F32).T, biases.astype(F32).T], axis=0)
    bias_row = fc1_bias.astype(F32)[None, :]

    shifts = range(1, narrow)
    others = []
    for c in range(cpd):
        send = [entered_of((me + k) % narrow, c, 1)[0] for k in shifts]
        if c > 0:
            send = after(send, others[-1])
        others.append([to_rank(send[k - 1], k) for k in shifts])
    keep_sent = [block_of(masked.reshape(clips, rp), (me + k) % narrow, 0, cpd) for k in shifts]
    keep_sent = after(keep_sent, others[0])
    keep_cols = [block_of(masked.reshape(clips, rp), me, 0, cpd)]
    keep_cols += [to_rank(keep_sent[k - 1], k) for k in shifts]
    keep = (jnp.concatenate(keep_cols, axis=1) != 1).astype(F32)[:, :, None]
    own = entered_of(me, 0, cpd)
    cot_send = [block_of(flat_cot, (me + k) % narrow, 0, cpd) for k in shifts]

    held = None
    for c in range(cpd):
        here = after(info, keep) if c == 1 else info
        held = attn_fwd(c, here, own, others[c], vec, w_qkv, w_proj, held)
    cot_send = after(cot_send, others[-1])
    cot_others = [to_rank(cot_send[k - 1], k) for k in shifts]
    n1, qkv, att, lse, mid, n2 = held

    out, *rest = mlp_fwd(info, mid, n2, vec, w_fc1, bias_row, w_fc2, clips, narrow)
    out_others, h = rest[:-1], rest[-1]
    out_back = [from_rank(out_others[k - 1], k) for k in shifts]

    dmid, two_sums, fc1_sums, *halves = mlp_back(
        info, flat_cot, cot_others, h, n2, mid, att, vec, w_fc1, w_fc2, wide
    )
    z_first = (("wide", 0), ("wide", 2), ("wide", 1), ("narrow", 0))
    fc2_chain = ScatterSum(*halves[:2], wide, narrow)
    y_next = (("wide", 0), ("wide", 2), ("narrow", 0), ("wide", 1))
    fc1_chain = ScatterSum(*halves[2:], wide, narrow, y_next)
    small = fc1_sums[0].reshape(d, ff // d)
    small = jnp.pad(small, ((0, 0), (9, 119 - small.shape[1])))

    held = None
    tok_back = []
    for c in range(cpd):
        behind = held[1] if c > 0 else two_sums
        ready = [fc2_chain.step(behind), fc1_chain.step(behind)] if c in (1, 3) else []
        if False:
            ready.append(out_back)
        if c > 1:
            tok_back[c - 2] = after(tok_back[c - 2], behind)
            ready.append(tok_back[c - 2])
        here = after(info, *ready)
        *held, = attn_back(
            c, here, own, others[c], keep, dmid, qkv, att, lse, vec, w_qkv, w_proj, held, clips
        )
        tok_back.append([from_rank(g, k) for k, g in zip(shifts, held[3:])])
        held = held[:3]
    dqkv, one_sums, grad_tokens = held
    old = (fc2_chain, fc1_chain)
    here = after(info, *[chain.step(one_sums) for chain in old])
    early = qkv_grad(0, here, n1, dqkv, wide)
    chains = [ScatterSum(*early, wide, narrow)]
    here = after(info, *[chain.step(early[0]) for chain in old])
    *halves, out, grad_tokens = qkv_grad(
        1, here, n1, dqkv, wide, (one_sums, two_sums, small, out, out_back, grad_tokens, tok_back)
    )
    x_first = (("wide", 0), ("narrow", 0), ("wide", 1), ("wide", 2))
    chains.append(ScatterSum(*halves, wide, narrow, x_first))
    sent = [chains[0].step(halves[0]), chains[1].step(halves[0])]
    grad_fc2 = fc2_chain.finish(sent)
    fc1_proj = fc1_chain.finish(sent)
    grad_fc1, grad_proj = fc1_proj[:, :ff], fc1_proj[:, ff:]
    while any(chain.sums is None for chain in chains):
        sent = [chain.step(sent) for chain in chains]
    last = jnp.concatenate([chain.finish() for chain in chains], axis=1)
    grad_qkv = last[:, : 3 * d]
    vectors = last[:, 3 * d :]
    return (
        out.reshape(tokens.shape),
        grad_tokens.reshape(tokens.shape),
        vectors[:, 0],
        vectors[:, 1:3],
        vectors[:, 3:9],
        grad_qkv,
        grad_proj,
        grad_fc1,
        vectors[:, 9 : 9 + ff // d].reshape(-1),
        grad_fc2,
    )


def solution(mesh):
    split = P("wide", None, "narrow", None)
    every = P(("wide", "narrow"))
    rows = P(("wide", "narrow"), None)
    return jax.shard_map(
        functools.partial(body, mesh.shape["wide"], mesh.shape["narrow"]),
        mesh=mesh,
        in_specs=(split, P("wide", None, "narrow"), P("wide")) + (P(),) * 8 + (split,),
        out_specs=(split, split, every, rows, rows, rows, rows, rows, every, rows),
        check_vma=False,
    )
```

```python
import functools

import jax
import jax.numpy as jnp
from jax import lax
from jax.experimental import pallas as pl
from jax.experimental.pallas import tpu as pltpu
from jax.sharding import PartitionSpec as P

HEADS = 12
EPS = 1e-06
LOG2E = 1.4426950408889634
F32 = jnp.float32
BF16 = jnp.bfloat16
MIB = 1 << 20


def dot_nn(a, b):
    return jnp.dot(a, b, preferred_element_type=F32)


def dot_nt(a, b):
    return lax.dot_general(a, b, (((1,), (1,)), ((), ())), preferred_element_type=F32)


def dot_tn(a, b):
    return lax.dot_general(a, b, (((0,), (0,)), ((), ())), preferred_element_type=F32)


def norm_stats(x):
    centred = x - jnp.mean(x, axis=-1, keepdims=True)
    rstd = lax.rsqrt(jnp.mean(centred * centred, axis=-1, keepdims=True) + EPS)
    return centred * rstd, rstd


def norm_back(grad, x, gain):
    xhat, rstd = norm_stats(x)
    scaled = grad * gain
    inner = jnp.mean(scaled * xhat, axis=-1, keepdims=True)
    outer = jnp.mean(scaled, axis=-1, keepdims=True)
    dx = rstd * (scaled - outer - xhat * inner)
    return dx, jnp.sum(grad * xhat, axis=0, keepdims=True), jnp.sum(grad, axis=0, keepdims=True)


def copies_of(pairs, sems):
    return [pltpu.make_async_copy(a, b, sems.at[i]) for i, (a, b) in enumerate(pairs)]


def row_valid(rows, piece_rows, full):
    at = lax.broadcasted_iota(jnp.int32, (rows, 1), 0) % piece_rows
    return (at < piece_rows // 2) | full


def attn_fwd_kernel(c, pieces, info, *refs):
    xs = refs[:pieces]
    vec, wqkv, wproj = refs[pieces : pieces + 3]
    made = refs[-8:-2]
    n1_o, qkv_o, att_o, lse_o, mid_o, n2_o = made
    lse_s, sems = refs[-2:]
    saves = copies_of([(m, o.at[c]) for m, o in zip(made, refs[-14:-8])], sems)
    rp, d = xs[0].shape
    rows = rp * pieces
    hw = d // HEADS
    full = info[1 + c] == 1
    for i in range(pieces):
        xhat, _ = norm_stats(xs[i][...].astype(F32))
        n1_o[i * rp : (i + 1) * rp, :] = (xhat * vec[0:1, :] + vec[6:7, :]).astype(BF16)
    saves[0].start()
    n1 = n1_o[...]
    qkv_o[:, 0:d] = (dot_nn(n1, wqkv[:, 0:d]) + vec[2:3, :]).astype(BF16)
    qkv_o[:, d : 2 * d] = dot_nn(n1, wqkv[:, d : 2 * d]).astype(BF16)
    qkv_o[:, 2 * d : 3 * d] = (dot_nn(n1, wqkv[:, 2 * d : 3 * d]) + vec[3:4, :]).astype(BF16)
    saves[1].start()
    scale2 = hw**-0.5 * LOG2E
    bias = jnp.where(row_valid(rows, rp, full), 0.0, -1e30).astype(BF16)
    lane = lax.broadcasted_iota(jnp.int32, (1, 2 * hw), 1)
    head_lane = lax.broadcasted_iota(jnp.int32, (1, 128), 1)
    lse_s[...] = jnp.zeros_like(lse_s)

    def pair(p, carry):
        at = p * 2 * hw
        q = qkv_o[:, pl.ds(at, 2 * hw)]
        k = qkv_o[:, pl.ds(d + at, 2 * hw)]
        v = qkv_o[:, pl.ds(2 * d + at, 2 * hw)]
        outs = []
        tops = []
        for e in range(2):
            mine = (lane < hw) if e == 0 else (lane >= hw)
            spare = lane == hw * (1 - e)
            one = jnp.where(spare, 1.0, 0.0).astype(BF16)
            qm = jnp.where(mine, q, one)
            km = jnp.where(spare, bias, k)
            s = dot_nt(qm, km)
            top = jnp.max(s, axis=-1, keepdims=True)
            pr = jnp.exp2((s - top) * scale2).astype(BF16)
            vm = jnp.where(mine, v, jnp.ones_like(v))
            outs.append(dot_nn(pr, vm))
            tops.append(top)
        low = lane < hw
        total = pltpu.roll(jnp.where(low, outs[1], outs[0]), hw, 1)
        att_o[:, pl.ds(at, 2 * hw)] = (jnp.where(low, outs[0], outs[1]) / total).astype(BF16)
        log_total = jnp.log2(total) + scale2 * jnp.where(low, tops[0], tops[1])
        first = jnp.broadcast_to(log_total[:, 0:1], (rows, 128))
        second = jnp.broadcast_to(log_total[:, hw : hw + 1], (rows, 128))
        lse_s[...] = jnp.where(
            head_lane == 2 * p, first, jnp.where(head_lane == 2 * p + 1, second, lse_s[...])
        )
        return carry

    for p in range(HEADS // 2):
        pair(p, 0)
    lse_o[...] = jnp.transpose(lse_s[...])[0:16, :]
    saves[2].start()
    saves[3].start()
    branch = dot_nn(att_o[...], wproj[...]) + vec[4:5, :]
    for i in range(pieces):
        part = slice(i * rp, (i + 1) * rp)
        middle = xs[i][...].astype(F32) + branch[part, :]
        mid_o[part, :] = middle.astype(BF16)
        xhat, _ = norm_stats(middle)
        n2_o[part, :] = (xhat * vec[1:2, :] + vec[7:8, :]).astype(BF16)
    saves[4].start()
    saves[5].start()
    for save in saves:
        save.wait()


def attn_fwd(c, info, own, others, vec, wqkv, wproj, held):
    cpd, rp, d = own.shape
    pieces = 1 + len(others)
    rows = rp * pieces
    whole = lambda a: pl.BlockSpec(a.shape, lambda i, s: (0,) * a.ndim)
    at_clip = lambda shape: pl.BlockSpec((None,) + shape, lambda i, s: (c, 0, 0))
    shapes = [
        ((rows, d), BF16),
        ((rows, 3 * d), BF16),
        ((rows, d), BF16),
        ((16, rows), F32),
        ((rows, d), BF16),
        ((rows, d), BF16),
    ]
    in_specs = [at_clip((rp, d))] + [whole(o) for o in others] + [whole(vec), whole(wqkv), whole(wproj)]
    operands = [own, *others, vec, wqkv, wproj]
    aliases = {}
    if held is not None:
        aliases = {1 + len(operands) + i: i for i in range(6)}
        in_specs = in_specs + [pl.BlockSpec(memory_space=pl.ANY)] * 6
        operands = operands + list(held)
    return pl.pallas_call(
        functools.partial(attn_fwd_kernel, c, pieces),
        grid_spec=pltpu.PrefetchScalarGridSpec(
            num_scalar_prefetch=1,
            grid=(1,),
            in_specs=in_specs,
            out_specs=[pl.BlockSpec(memory_space=pl.ANY)] * len(shapes),
            scratch_shapes=[pltpu.VMEM(s, t) for s, t in shapes]
            + [pltpu.VMEM((rows, 128), F32), pltpu.SemaphoreType.DMA((len(shapes),))],
        ),
        out_shape=[jax.ShapeDtypeStruct((cpd,) + s, t) for s, t in shapes],
        input_output_aliases=aliases,
        compiler_params=pltpu.CompilerParams(vmem_limit_bytes=60 * MIB),
        cost_estimate=pl.CostEstimate(
            flops=2 * rows * d * 4 * d + 16 * HEADS * rows * rows * (d // HEADS),
            bytes_accessed=rows * d * 16 + 8 * d * d,
            transcendentals=HEADS * rows * rows,
        ),
        name="attn_fwd",
    )(info, *operands)


def mlp_fwd_kernel(pieces, info, mid, n2, vec, w1, b1, w2, *outs):
    h_o = outs[pieces]
    rows, d = n2.shape
    rp = rows // pieces
    full = info[1 + pl.program_id(0)] == 1
    ff = w1.shape[1]
    chunk = d
    x = n2[...]
    acc = mid[...].astype(F32) + vec[5:6, :]
    for j in range(ff // chunk):
        part = slice(j * chunk, (j + 1) * chunk)
        h = dot_nn(x, w1[:, part]) + b1[:, part]
        h_o[:, part] = h.astype(BF16)
        act = (h * (0.5 + 0.5 * lax.erf(h * 0.7071067811865476))).astype(BF16)
        acc = acc + dot_nn(act, w2[part, :])
    out = jnp.where(row_valid(rows, rp, full), acc, 0.0).astype(BF16)
    for i in range(pieces):
        outs[i][...] = out[i * rp : (i + 1) * rp, :]


def mlp_fwd(info, mid, n2, vec, w1, b1, w2, clips, pieces):
    cpd, rows, d = n2.shape
    ff = w1.shape[1]
    rp = rows // pieces
    by_clip = lambda w: pl.BlockSpec((None, rows, w), lambda c, s: (c, 0, 0))
    once = lambda a: pl.BlockSpec(a.shape, lambda c, s: (0, 0), pipeline_mode=pl.Buffered(1))
    return pl.pallas_call(
        functools.partial(mlp_fwd_kernel, pieces),
        grid_spec=pltpu.PrefetchScalarGridSpec(
            num_scalar_prefetch=1,
            grid=(cpd,),
            in_specs=[by_clip(d), by_clip(d), once(vec), once(w1), once(b1), once(w2)],
            out_specs=[pl.BlockSpec((None, rp, d), lambda c, s: (s[0] * cpd + c, 0, 0))]
            + [pl.BlockSpec((None, rp, d), lambda c, s: (c, 0, 0))] * (pieces - 1)
            + [by_clip(ff)],
        ),
        out_shape=[jax.ShapeDtypeStruct((clips, rp, d), BF16)]
        + [jax.ShapeDtypeStruct((cpd, rp, d), BF16)] * (pieces - 1)
        + [jax.ShapeDtypeStruct((cpd, rows, ff), BF16)],
        compiler_params=pltpu.CompilerParams(vmem_limit_bytes=60 * MIB),
        cost_estimate=pl.CostEstimate(
            flops=4 * cpd * rows * d * ff,
            bytes_accessed=cpd * rows * (8 * d + 2 * ff) + 4 * d * ff,
            transcendentals=cpd * rows * ff,
        ),
        name="mlp_fwd",
    )(info, mid, n2, vec, w1, b1, w2)


def upstream_of(cots, full):
    rp = cots[0].shape[0]
    keep = row_valid(rp, rp, full)
    return jnp.concatenate(
        [jnp.where(keep, c[...].astype(F32), 0.0) for c in cots], axis=0
    )


def mlp_back_kernel(pieces, cpd, info, *refs):
    cots = refs[:pieces]
    h, n2, mid, att, vec, w1_in, w2_in = refs[pieces : pieces + 7]
    dmid_o, sums_o, fc1_sums_o, keep2, send2, keep1, send1 = refs[pieces + 7 : pieces + 14]
    w1, w2, acc1, acc2, dn2_s, up_s, turned_s, stage1, stage2, sems_in, sems1, sems2 = refs[pieces + 14 :]
    r = pl.program_id(0)
    last = r == cpd - 1
    rows, d = mid.shape
    ff = w1.shape[1]
    chunk = d
    count = ff // chunk
    unit1 = keep1.shape[1]
    unit2 = keep2.shape[1]
    per2 = chunk // (2 * unit2)
    mine = info[1 + cpd]

    def cols_of(j):
        return pl.ds(pl.multiple_of(j * chunk, chunk), chunk)

    def loads(j):
        part = cols_of(j)
        return [
            pltpu.make_async_copy(w1_in.at[:, part], w1.at[:, part], sems_in.at[0, j]),
            pltpu.make_async_copy(w2_in.at[part], w2.at[part], sems_in.at[1, j]),
        ]

    def saves1(j, slot):
        cols = cols_of(j)
        return [
            pltpu.make_async_copy(stage1.at[slot, :, side], to.at[:, :, cols], sems1.at[slot, i])
            for i, (side, to) in enumerate(((mine, keep1), (1 - mine, send1)))
        ]

    def saves2(j, slot):
        at = pl.ds(j * per2, per2)
        return [
            pltpu.make_async_copy(stage2.at[slot, :, side], to.at[at], sems2.at[slot, i])
            for i, (side, to) in enumerate(((mine, keep2), (1 - mine, send2)))
        ]

    @pl.when(r == 0)
    def _():
        for j in range(count):
            for load in loads(j):
                load.start()
        acc1[...] = jnp.zeros_like(acc1)
        acc2[...] = jnp.zeros_like(acc2)
        sums_o[...] = jnp.zeros_like(sums_o)
        fc1_sums_o[...] = jnp.zeros_like(fc1_sums_o)

    up = upstream_of(cots, info[1 + r] == 1)
    up_s[...] = up.astype(BF16)
    sums_o[2:3, :] += jnp.sum(up, axis=0, keepdims=True)
    turned_s[...] = jnp.transpose(n2[...])
    dn2_s[...] = jnp.zeros_like(dn2_s)

    def one(j, carry):
        part = cols_of(j)

        @pl.when(r == 0)
        def _():
            for load in loads(j):
                load.wait()

        pre = h[:, part].astype(F32)
        cdf = 0.5 + 0.5 * lax.erf(pre * 0.7071067811865476)
        density = 0.3989422804014327 * jnp.exp2(pre * pre * (-0.5 * LOG2E))
        act = (pre * cdf).astype(BF16)
        grad = dot_nt(up_s[...], w2[part, :])
        dh = (grad * (cdf + pre * density)).astype(BF16)
        fc1_sums_o[0:1, part] += jnp.sum(dh.astype(F32), axis=0, keepdims=True)
        acc2[part, :] += dot_tn(act, up_s[...])
        dn2_s[...] += dot_nt(dh, w1[:, part])
        acc1[:, part] += dot_nn(turned_s[...], dh)

        @pl.when(last)
        def _():
            slot = j % 2

            @pl.when(j > 1)
            def _():
                for save in saves1(j - 2, slot) + saves2(j - 2, slot):
                    save.wait()

            stage2[slot] = acc2[part, :].astype(BF16).reshape(per2, 2, unit2, d)
            stage1[slot] = acc1[:, part].astype(BF16).reshape(d // (2 * unit1), 2, unit1, chunk)
            for save in saves1(j, slot) + saves2(j, slot):
                save.start()

        return carry

    lax.fori_loop(0, count, one, 0, unroll=2)
    dx, gain, shift = norm_back(dn2_s[...], mid[...].astype(F32), vec[1:2, :])
    dmid = (up_s[...].astype(F32) + dx).astype(BF16)
    dmid_o[...] = dmid
    sums_o[0:1, :] += gain
    sums_o[1:2, :] += shift
    acc1[:, ff : ff + d] += dot_tn(att[...], dmid)

    @pl.when(last)
    def _():
        for j in range(max(count - 2, 0), count):
            for save in saves1(j, j % 2) + saves2(j, j % 2):
                save.wait()
        stage1[0] = acc1[:, ff : ff + d].astype(BF16).reshape(d // (2 * unit1), 2, unit1, d)
        for save in saves1(count, 0):
            save.start()
        for save in saves1(count, 0):
            save.wait()


def mlp_back(info, cot, cot_others, h, n2, mid, att, vec, w1, w2, parts):
    clips, rp, d = cot.shape
    cpd, rows, ff = h.shape
    pieces = 1 + len(cot_others)
    unit1 = d // parts
    unit2 = ff // parts
    once = lambda a: pl.BlockSpec(a.shape, lambda c, s: (0, 0), pipeline_mode=pl.Buffered(1))
    held = lambda shape: pl.BlockSpec(shape, lambda c, s: (0, 0))
    by_clip = lambda w: pl.BlockSpec((None, rows, w), lambda c, s: (c, 0, 0))
    halves = [(d // (2 * unit1), unit1, ff + d), (ff // (2 * unit2), unit2, d)]
    return pl.pallas_call(
        functools.partial(mlp_back_kernel, pieces, cpd),
        grid_spec=pltpu.PrefetchScalarGridSpec(
            num_scalar_prefetch=1,
            grid=(cpd,),
            in_specs=[pl.BlockSpec((None, rp, d), lambda c, s: (s[0] * cpd + c, 0, 0))]
            + [pl.BlockSpec((None, rp, d), lambda c, s: (c, 0, 0))] * (pieces - 1)
            + [by_clip(ff), by_clip(d), by_clip(d), by_clip(d), once(vec)]
            + [pl.BlockSpec(memory_space=pl.ANY)] * 2,
            out_specs=[by_clip(d), held((8, d)), held((8, ff))]
            + [pl.BlockSpec(memory_space=pl.ANY)] * 4,
            scratch_shapes=[
                pltpu.VMEM(w1.shape, BF16),
                pltpu.VMEM(w2.shape, BF16),
                pltpu.VMEM((d, ff + d), F32),
                pltpu.VMEM((ff, d), F32),
                pltpu.VMEM((rows, d), F32),
                pltpu.VMEM((rows, d), BF16),
                pltpu.VMEM((d, rows), BF16),
                pltpu.VMEM((2, d // (2 * unit1), 2, unit1, d), BF16),
                pltpu.VMEM((2, d // (2 * unit2), 2, unit2, d), BF16),
                pltpu.SemaphoreType.DMA((2, ff // d)),
                pltpu.SemaphoreType.DMA((2, 2)),
                pltpu.SemaphoreType.DMA((2, 2)),
            ],
        ),
        out_shape=[
            jax.ShapeDtypeStruct((cpd, rows, d), BF16),
            jax.ShapeDtypeStruct((8, d), F32),
            jax.ShapeDtypeStruct((8, ff), F32),
        ]
        + [jax.ShapeDtypeStruct(halves[1], BF16)] * 2
        + [jax.ShapeDtypeStruct(halves[0], BF16)] * 2,
        compiler_params=pltpu.CompilerParams(vmem_limit_bytes=62 * MIB),
        cost_estimate=pl.CostEstimate(
            flops=8 * cpd * rows * d * ff,
            bytes_accessed=cpd * rows * (14 * d + 2 * ff) + 8 * d * ff,
            transcendentals=2 * cpd * rows * ff,
        ),
        name="mlp_back",
    )(info, cot, *cot_others, h, n2, mid, att, vec, w1, w2)


def attn_back_kernel(c, pieces, cpd, info, *refs):
    xs = refs[:pieces]
    keep, dmid, qkv_in, att, lse, vec, wqkv_in, wproj = refs[pieces : pieces + 8]
    dqkv_o, sums_o, gtok, do_s, delta_s, dqt_s, x_s, wqkv, qkv, sems, sems_in = refs[-11:]
    dqkv_out, sums_out, own_out, *others_out = refs[-13 - pieces : -11]
    rp, d = x_s.shape[1:]
    sources = [(qkv_in.at[c], qkv), (wqkv_in, wqkv), (xs[0].at[c], x_s.at[0])]
    sources += [(x, x_s.at[1 + i]) for i, x in enumerate(xs[1:])]
    loads = copies_of(sources, sems_in)
    for load in loads:
        load.start()
    rows = rp * pieces
    hw = d // HEADS
    full = info[1 + c] == 1
    targets = [(dqkv_o, dqkv_out.at[c]), (sums_o, sums_out.at[c])]
    targets += [(gtok.at[0], own_out.at[info[0] * cpd + c])]
    targets += [(gtok.at[1 + i], o) for i, o in enumerate(others_out)]
    saves = copies_of(targets, sems)
    low_mid = dmid[...]
    do_s[...] = dot_nt(low_mid, wproj[...]).astype(BF16)
    prod = (do_s[...].astype(F32) * att[...].astype(F32)).astype(BF16)
    head_of = lax.broadcasted_iota(jnp.int32, (16, d), 1) // hw
    select = (head_of == lax.broadcasted_iota(jnp.int32, (16, d), 0)).astype(BF16)
    delta_s[...] = dot_nt(select, prod)
    loads[0].wait()
    scale = hw**-0.5
    scale2 = scale * LOG2E
    bias = jnp.where(row_valid(rows, rp, full), 0.0, -1e30).astype(BF16)
    lane = lax.broadcasted_iota(jnp.int32, (1, 2 * hw), 1)

    def pair(p, carry):
        at = p * 2 * hw
        q = qkv[:, pl.ds(at, 2 * hw)]
        k = qkv[:, pl.ds(d + at, 2 * hw)]
        v = qkv[:, pl.ds(2 * d + at, 2 * hw)]
        do = do_s[:, pl.ds(at, 2 * hw)]
        kt = jnp.transpose(k)
        zero = jnp.zeros_like(q)
        dk = dv = None
        for e in range(2):
            mine = (lane < hw) if e == 0 else (lane >= hw)
            spare = lane == hw * (1 - e)
            one = jnp.where(spare, 1.0, 0.0).astype(BF16)
            qm = jnp.where(mine, q, one)
            km = jnp.where(spare, bias, k)
            st = dot_nt(km, qm)
            pt = jnp.exp2(st * scale2 - lse[pl.ds(2 * p + e, 1), :])
            vm = jnp.where(mine, v, zero)
            dpt = dot_nt(vm, do)
            dst = (pt * (dpt - delta_s[pl.ds(2 * p + e, 1), :])).astype(BF16)
            dom = jnp.where(mine, do, zero)
            qz = jnp.where(mine, q, zero)
            dv_e = dot_nn(pt.astype(BF16), dom)
            dk_e = dot_nn(dst, qz)
            dv = dv_e if dv is None else dv + dv_e
            dk = dk_e if dk is None else dk + dk_e
            dqt_s[pl.ds(at + e * hw, hw), :] = dot_nn(
                kt[e * hw : (e + 1) * hw, :], dst
            )
        dqkv_o[:, pl.ds(d + at, 2 * hw)] = (dk * scale).astype(BF16)
        dqkv_o[:, pl.ds(2 * d + at, 2 * hw)] = dv.astype(BF16)
        return carry

    for p in range(HEADS // 2):
        pair(p, 0)
    dqkv_o[:, 0:d] = jnp.transpose((dqt_s[...] * scale).astype(BF16))
    saves[0].start()
    for load in loads[1:]:
        load.wait()
    dn1 = dot_nt(dqkv_o[...], wqkv[...])
    sums_o[...] = jnp.zeros_like(sums_o)
    sums_o[0:1, :] = jnp.sum(dqkv_o[:, 0:d].astype(F32), axis=0, keepdims=True)
    sums_o[1:2, :] = jnp.sum(dqkv_o[:, 2 * d : 3 * d].astype(F32), axis=0, keepdims=True)
    sums_o[2:3, :] = jnp.sum(low_mid.astype(F32), axis=0, keepdims=True)
    for i in range(pieces):
        part = slice(i * rp, (i + 1) * rp)
        dx, gain, shift = norm_back(dn1[part, :], x_s[i].astype(F32), vec[0:1, :])
        entered = low_mid[part, :].astype(F32) + dx
        kept = entered * keep[part, :]
        gtok[i] = kept.astype(BF16)
        saves[2 + i].start()
        sums_o[3:4, :] += gain
        sums_o[4:5, :] += shift
        sums_o[5:6, :] += jnp.sum(entered - kept, axis=0, keepdims=True)
    saves[1].start()
    for save in saves:
        save.wait()


def attn_back(c, info, own, others, keep, dmid, qkv, att, lse, vec, wqkv, wproj, held, clips):
    cpd, rp, d = own.shape
    pieces = 1 + len(others)
    rows = rp * pieces
    whole = lambda a: pl.BlockSpec(a.shape, lambda i, s: (0,) * a.ndim)
    at_clip = lambda shape: pl.BlockSpec((None,) + shape, lambda i, s: (c, 0, 0))
    in_specs = (
        [pl.BlockSpec(memory_space=pl.ANY)] * pieces
        + [
            at_clip((rows, 1)),
            at_clip((rows, d)),
            pl.BlockSpec(memory_space=pl.ANY),
            at_clip((rows, d)),
            at_clip((16, rows)),
            whole(vec),
            pl.BlockSpec(memory_space=pl.ANY),
            whole(wproj),
        ]
    )
    operands = [own, *others, keep, dmid, qkv, att, lse, vec, wqkv, wproj]
    aliases = {}
    if held is not None:
        aliases = {1 + len(operands) + i: i for i in range(3)}
        in_specs = in_specs + [pl.BlockSpec(memory_space=pl.ANY)] * 3
        operands = operands + list(held)
    return pl.pallas_call(
        functools.partial(attn_back_kernel, c, pieces, cpd),
        grid_spec=pltpu.PrefetchScalarGridSpec(
            num_scalar_prefetch=1,
            grid=(1,),
            in_specs=in_specs,
            out_specs=[pl.BlockSpec(memory_space=pl.ANY)] * (2 + pieces),
            scratch_shapes=[
                pltpu.VMEM((rows, 3 * d), BF16),
                pltpu.VMEM((8, d), F32),
                pltpu.VMEM((pieces, rp, d), BF16),
                pltpu.VMEM((rows, d), BF16),
                pltpu.VMEM((16, rows), F32),
                pltpu.VMEM((d, rows), F32),
                pltpu.VMEM((pieces, rp, d), BF16),
                pltpu.VMEM(wqkv.shape, BF16),
                pltpu.VMEM((rows, 3 * d), BF16),
                pltpu.SemaphoreType.DMA((2 + pieces,)),
                pltpu.SemaphoreType.DMA((2 + pieces,)),
            ],
        ),
        out_shape=[
            jax.ShapeDtypeStruct((cpd, rows, 3 * d), BF16),
            jax.ShapeDtypeStruct((cpd, 8, d), F32),
            jax.ShapeDtypeStruct((clips, rp, d), BF16),
        ]
        + [jax.ShapeDtypeStruct((rp, d), BF16)] * (pieces - 1),
        input_output_aliases=aliases,
        compiler_params=pltpu.CompilerParams(vmem_limit_bytes=60 * MIB),
        cost_estimate=pl.CostEstimate(
            flops=2 * rows * d * 4 * d + 40 * HEADS * rows * rows * (d // HEADS),
            bytes_accessed=rows * d * 28 + 8 * d * d,
            transcendentals=HEADS * rows * rows,
        ),
        name="attn_back",
    )(info, *operands)


def qkv_grad_kernel(n1, dqkv, info, turned_s, acc, stage, sems, keep, send):
    r = pl.program_id(0)
    per, rows, d = n1.shape
    groups, _, unit, width = stage.shape
    mine = info[1 + pl.num_programs(0) * per]
    cut = width // 256 * 128

    @pl.when(r == 0)
    def _():
        acc[...] = jnp.zeros_like(acc)

    for i in range(per):
        turned_s[:, i * rows : (i + 1) * rows] = jnp.transpose(n1[i])
    saves = []
    for at, cols in ((0, cut), (cut, width - cut)):
        part = slice(at, at + cols)
        piece = jnp.concatenate([dqkv[i, :, part] for i in range(per)], axis=0)
        acc[:, part] += dot_nn(turned_s[...], piece)
        to = pl.ds(at, cols)
        saves += [
            pltpu.make_async_copy(
                stage.at[:, side, :, to], half.at[:, :, to], sems.at[len(saves) + i]
            )
            for i, (side, half) in enumerate(((mine, keep), (1 - mine, send)))
        ]

        @pl.when(r == pl.num_programs(0) - 1)
        def _():
            stage[:, :, :, part] = acc[:, part].astype(BF16).reshape(groups, 2, unit, cols)
            for save in saves[-2:]:
                save.start()

    return saves


def early_kernel(info, n1, dqkv, keep, send, turned_s, acc, stage, sems):
    saves = qkv_grad_kernel(n1, dqkv, info, turned_s, acc, stage, sems, keep, send)

    @pl.when(pl.program_id(0) == pl.num_programs(0) - 1)
    def _():
        for save in saves:
            save.wait()


def late_kernel(cpd, narrow, moved, info, *refs):
    n1, dqkv, one_sums, two_sums, small = refs[:5]
    moving = refs[7 : 7 + moved]
    keep, send, out, tok = refs[7 + moved : 11 + moved]
    turned_s, acc, stage, sems, rows_s, tail, sems_move = refs[11 + moved : 18 + moved]
    held = refs[18 + moved :]
    r = pl.program_id(0)
    last = r == pl.num_programs(0) - 1
    groups, _, unit, width = stage.shape
    lanes = tail.shape[-1]
    mine = info[1 + cpd]
    moves, order = [], []
    for k in range(1, narrow):
        rank = lax.rem(info[0] + k, narrow)
        order.append(k - 1)
        moves.append(out.at[pl.ds(rank * cpd, cpd)])
        for c in range(cpd):
            order.append((c + 1) * (narrow - 1) + k - 1)
            moves.append(tok.at[rank * cpd + c])
    arrivals = copies_of([(moving[i], held[i]) for i in order], sems_move)
    moves = copies_of([(held[i], to) for i, to in zip(order, moves)], sems_move)

    @pl.when(r == 0)
    def _():
        for arrival in arrivals:
            arrival.start()

    ends = [
        pltpu.make_async_copy(tail.at[:, side], half.at[:, :, pl.ds(width, lanes)], sems.at[4 + i])
        for i, (side, half) in enumerate(((mine, keep), (1 - mine, send)))
    ]

    @pl.when(last)
    def _():
        for arrival in arrivals:
            arrival.wait()
        for move in moves:
            move.start()
        one_total = jnp.sum(one_sums[...], axis=0)
        rows_s[...] = jnp.zeros_like(rows_s)
        picked = [
            one_total[5:6, :],
            one_total[3:4, :],
            two_sums[0:1, :],
            one_total[0:1, :],
            one_total[1:2, :],
            one_total[2:3, :],
            two_sums[2:3, :],
            one_total[4:5, :],
            two_sums[1:2, :],
        ]
        for i, row in enumerate(picked):
            rows_s[i : i + 1, :] = row
        vectors = (jnp.transpose(rows_s[...]) + small[...]).astype(BF16)
        tail[...] = vectors.reshape(groups, 2, unit, lanes)
        for end in ends:
            end.start()

    saves = qkv_grad_kernel(n1, dqkv, info, turned_s, acc, stage, sems, keep, send)

    @pl.when(last)
    def _():
        for copy in saves + ends + moves:
            copy.wait()


def qkv_grad(which, info, n1, dqkv, parts, late=None):
    cpd, rows, d = n1.shape
    width = dqkv.shape[2] // 2
    unit = d // parts
    groups = d // (2 * unit)
    per = 2 if cpd % 2 == 0 else 1
    anywhere = pl.BlockSpec(memory_space=pl.ANY)
    held = lambda a: pl.BlockSpec(a.shape, lambda c, s: (0,) * a.ndim)
    in_specs = [
        pl.BlockSpec((per, rows, d), lambda c, s: (c, 0, 0)),
        pl.BlockSpec((per, rows, width), lambda c, s: (c, 0, which)),
    ]
    scratch = [
        pltpu.VMEM((d, per * rows), BF16),
        pltpu.VMEM((d, width), F32),
        pltpu.VMEM((groups, 2, unit, width), BF16),
        pltpu.SemaphoreType.DMA((6,)),
    ]
    operands = [n1, dqkv]
    cols, kernel, aliases, shapes = width, early_kernel, {}, []
    if late is not None:
        one_sums, two_sums, small, out, out_back, tok, tok_back = late
        moving = list(out_back) + [t for back in tok_back for t in back]
        kernel = functools.partial(late_kernel, cpd, 1 + len(out_back), len(moving))
        in_specs += [held(one_sums), held(two_sums), held(small)] + [anywhere] * (2 + len(moving))
        operands += [one_sums, two_sums, small, out, tok, *moving]
        lanes = small.shape[1]
        cols = width + lanes
        aliases = {6: 2, 7: 3}
        shapes = [jax.ShapeDtypeStruct(out.shape, BF16), jax.ShapeDtypeStruct(tok.shape, BF16)]
        scratch += [
            pltpu.VMEM((lanes, d), F32),
            pltpu.VMEM((groups, 2, unit, lanes), BF16),
            pltpu.SemaphoreType.DMA((max(len(moving), 1),)),
        ]
        scratch += [pltpu.VMEM(m.shape, BF16) for m in moving]
    shapes = [jax.ShapeDtypeStruct((groups, unit, cols), BF16)] * 2 + shapes
    return pl.pallas_call(
        kernel,
        grid_spec=pltpu.PrefetchScalarGridSpec(
            num_scalar_prefetch=1,
            grid=(cpd // per,),
            in_specs=in_specs,
            out_specs=[anywhere] * len(shapes),
            scratch_shapes=scratch,
        ),
        out_shape=shapes,
        input_output_aliases=aliases,
        compiler_params=pltpu.CompilerParams(vmem_limit_bytes=60 * MIB),
        cost_estimate=pl.CostEstimate(
            flops=2 * cpd * rows * d * width,
            bytes_accessed=2 * (cpd * rows * (d + width) + d * width),
            transcendentals=0,
        ),
        name="finish",
    )(info, *operands)


class ScatterSum:
    def __init__(self, keep, send, wide, narrow, first=(("wide", 0),)):
        rows, cols = 2 * keep.shape[0] * keep.shape[1], keep.shape[2]
        self.block = (rows // (wide * narrow), cols)
        bits_w, bits_n = wide.bit_length() - 1, narrow.bit_length() - 1
        order = [("wide", b, bits_w - 1 - b, wide) for b in range(bits_w)]
        order += [("narrow", b, bits_w + bits_n - 1 - b, narrow) for b in range(bits_n)]
        ahead = [o for key in first for o in order if o[:2] == key]
        self.order = ahead + [o for o in order if o not in ahead]
        axis, bit, dim, size = self.order.pop(0)
        shape = [2] * (bits_w + bits_n)
        shape[dim] = 1
        self.sums = None
        self.keep = keep.reshape(tuple(shape) + self.block)
        self.exchange(send.reshape(self.keep.shape), axis, bit, size)

    def exchange(self, sent, axis, bit, size):
        self.sent = sent
        self.got = lax.ppermute(sent, axis, [(i, i ^ (1 << bit)) for i in range(size)])

    def step(self, behind=None):
        if self.sums is not None:
            return self.sums
        keep, got = self.keep, self.got
        if behind is not None:
            keep = after(keep, behind)
        if not self.order:
            self.sums = keep.astype(F32) + got.astype(F32)
            return self.sums
        axis, bit, dim, size = self.order.pop(0)
        mine = (lax.axis_index(axis) >> bit) & 1

        def part(at):
            pieces = [lax.dynamic_slice_in_dim(x, at, 1, dim).astype(F32) for x in (keep, got)]
            return (pieces[0] + pieces[1]).astype(BF16)

        self.exchange(part(1 - mine), axis, bit, size)
        self.keep = part(mine)
        return self.sent

    def finish(self, behind=None):
        while self.sums is None:
            self.step(behind)
        return self.sums.reshape(self.block)


def after(value, *others):
    return lax.optimization_barrier((value, others))[0]


def body(
    wide,
    narrow,
    tokens,
    masked,
    resolution,
    mask_embed,
    gains,
    biases,
    w_qkv,
    w_proj,
    w_fc1,
    fc1_bias,
    w_fc2,
    cotangent,
):
    clips, freq_rows, cols, d = tokens.shape
    rp = freq_rows * cols
    cpd = clips // narrow
    rows = rp * narrow
    ff = w_fc1.shape[1]
    me = lax.axis_index("narrow")
    flat_tokens = tokens.reshape(clips, rp, d)
    flat_cot = cotangent.reshape(clips, rp, d)
    is_masked = masked.reshape(clips, rp) == 1

    def block_of(array, rank, at, count):
        return lax.dynamic_slice_in_dim(array, rank * cpd + at, count, 0)

    def entered_of(rank, at, count):
        return jnp.where(
            block_of(is_masked, rank, at, count)[:, :, None],
            mask_embed[None, None, :],
            block_of(flat_tokens, rank, at, count),
        )

    def to_rank(array, k):
        return lax.ppermute(array, "narrow", [(i, (i + k) % narrow) for i in range(narrow)])

    def from_rank(array, k):
        return lax.ppermute(array, "narrow", [(i, (i - k) % narrow) for i in range(narrow)])

    core = lax.axis_index("wide") & 1
    info = jnp.concatenate([me[None], block_of(resolution, me, 0, cpd), core[None]])
    vec = jnp.concatenate([gains.astype(F32).T, biases.astype(F32).T], axis=0)
    bias_row = fc1_bias.astype(F32)[None, :]

    shifts = range(1, narrow)
    others = []
    for c in range(cpd):
        send = [entered_of((me + k) % narrow, c, 1)[0] for k in shifts]
        if c > 0:
            send = after(send, others[-1])
        others.append([to_rank(send[k - 1], k) for k in shifts])
    keep_sent = [block_of(masked.reshape(clips, rp), (me + k) % narrow, 0, cpd) for k in shifts]
    keep_sent = after(keep_sent, others[0])
    keep_cols = [block_of(masked.reshape(clips, rp), me, 0, cpd)]
    keep_cols += [to_rank(keep_sent[k - 1], k) for k in shifts]
    keep = (jnp.concatenate(keep_cols, axis=1) != 1).astype(F32)[:, :, None]
    own = entered_of(me, 0, cpd)
    cot_send = [block_of(flat_cot, (me + k) % narrow, 0, cpd) for k in shifts]

    held = None
    for c in range(cpd):
        here = after(info, keep) if c == 1 else info
        held = attn_fwd(c, here, own, others[c], vec, w_qkv, w_proj, held)
    cot_send = after(cot_send, others[-1])
    cot_others = [to_rank(cot_send[k - 1], k) for k in shifts]
    n1, qkv, att, lse, mid, n2 = held

    out, *rest = mlp_fwd(info, mid, n2, vec, w_fc1, bias_row, w_fc2, clips, narrow)
    out_others, h = rest[:-1], rest[-1]
    out_back = [from_rank(out_others[k - 1], k) for k in shifts]

    dmid, two_sums, fc1_sums, *halves = mlp_back(
        info, flat_cot, cot_others, h, n2, mid, att, vec, w_fc1, w_fc2, wide
    )
    z_first = (("wide", 0), ("wide", 2), ("wide", 1), ("narrow", 0))
    fc2_chain = ScatterSum(*halves[:2], wide, narrow)
    y_next = (("wide", 0), ("wide", 2), ("narrow", 0), ("wide", 1))
    fc1_chain = ScatterSum(*halves[2:], wide, narrow, y_next)
    small = fc1_sums[0].reshape(d, ff // d)
    small = jnp.pad(small, ((0, 0), (9, 119 - small.shape[1])))

    held = None
    tok_back = []
    for c in range(cpd):
        behind = held[1] if c > 0 else two_sums
        ready = [fc2_chain.step(behind), fc1_chain.step(behind)] if c in (1, 3) else []
        if False:
            ready.append(out_back)
        if c > 1:
            tok_back[c - 2] = after(tok_back[c - 2], behind)
            ready.append(tok_back[c - 2])
        here = after(info, *ready)
        *held, = attn_back(
            c, here, own, others[c], keep, dmid, qkv, att, lse, vec, w_qkv, w_proj, held, clips
        )
        tok_back.append([from_rank(g, k) for k, g in zip(shifts, held[3:])])
        held = held[:3]
    dqkv, one_sums, grad_tokens = held
    old = (fc2_chain, fc1_chain)
    here = after(info, *[chain.step(one_sums) for chain in old])
    early = qkv_grad(0, here, n1, dqkv, wide)
    x_second = (("wide", 0), ("wide", 1), ("narrow", 0), ("wide", 2))
    chains = [ScatterSum(*early, wide, narrow, x_second)]
    here = after(info, *[chain.step(early[0]) for chain in old])
    *halves, out, grad_tokens = qkv_grad(
        1, here, n1, dqkv, wide, (one_sums, two_sums, small, out, out_back, grad_tokens, tok_back)
    )
    x_first = (("wide", 0), ("narrow", 0), ("wide", 1), ("wide", 2))
    chains.append(ScatterSum(*halves, wide, narrow, x_first))
    sent = [chains[0].step(halves[0]), chains[1].step(halves[0])]
    grad_fc2 = fc2_chain.finish(sent)
    fc1_proj = fc1_chain.finish(sent)
    grad_fc1, grad_proj = fc1_proj[:, :ff], fc1_proj[:, ff:]
    while any(chain.sums is None for chain in chains):
        sent = [chain.step(sent) for chain in chains]
    last = jnp.concatenate([chain.finish() for chain in chains], axis=1)
    grad_qkv = last[:, : 3 * d]
    vectors = last[:, 3 * d :]
    return (
        out.reshape(tokens.shape),
        grad_tokens.reshape(tokens.shape),
        vectors[:, 0],
        vectors[:, 1:3],
        vectors[:, 3:9],
        grad_qkv,
        grad_proj,
        grad_fc1,
        vectors[:, 9 : 9 + ff // d].reshape(-1),
        grad_fc2,
    )


def solution(mesh):
    split = P("wide", None, "narrow", None)
    every = P(("wide", "narrow"))
    rows = P(("wide", "narrow"), None)
    return jax.shard_map(
        functools.partial(body, mesh.shape["wide"], mesh.shape["narrow"]),
        mesh=mesh,
        in_specs=(split, P("wide", None, "narrow"), P("wide")) + (P(),) * 8 + (split,),
        out_specs=(split, split, every, rows, rows, rows, rows, rows, every, rows),
        check_vma=False,
    )
```
